512 devices in a mesh: dp: 8 (over z), context: 16 (over y, core), tensor: 4 (over x).
Axes of the slice: x: 4, y: 8, z: 8, core: 2. Of those that a mesh axis runs over, the one named last changes fastest.
Arguments:
- layer_input: bfloat16 [8, 8192, 4096], P('dp', 'context', 'tensor'), may hold values from -6 to 6
- queries: bfloat16 [8, 16, 8192, 128], P('dp', 'tensor', 'context'), may hold values from -6 to 6
- key_states: bfloat16 [8, 4, 8192, 128], P('dp', 'tensor', 'context'), may hold values from -6 to 6
- value_states: bfloat16 [8, 4, 8192, 128], P('dp', 'tensor', 'context'), may hold values from -6 to 6
- out_grad: bfloat16 [8, 16, 8192, 128], P('dp', 'tensor', 'context'), may hold values from -0.0234375 to 0.0234375
- log_sums: bfloat16 [8, 16, 8192], P('dp', 'tensor', 'context'), may hold values from 2 to 5
- grad_dots: bfloat16 [8, 16, 8192], P('dp', 'tensor', 'context'), may hold values from -0.1875 to 0.1875
- doc_stretches: int32 [8, 10], P('dp'), may hold values from 1 to 8, as said below
- stretch_order: int32 [8, 256], P('dp'), may hold values from 0 to 255, as said below
- sign_vector: int32 [32, 128], P('context'), may hold values from -1 to 1, as said below
- exponents: int32 [8, 32], P('dp', 'context'), may hold values from 0 to 3
Outputs:
- rotated_grad: float32 [32, 128, 1024], P('context', 'dp', 'tensor')
The draws below stay inside these ranges and needn't reach their ends.
Inputs may be any that keep to these rules, and one draw needn't show every extreme that they name: `doc_stretches`: each row gives the lengths in units of 128 tokens of 10 documents; they sum to 64. The second document is one of the longest, exactly 8 units, and begins 512 - 128 tokens after a multiple of 512 tokens. `stretch_order`: each row is a permutation of the 256 sequence blocks. Sequence blocks d * 16 to d * 16 + 15 belong to index d of context; the 16 stored blocks of one index of context hold at most 1 block belonging to any one index. `sign_vector`: every entry is 1 or -1.
All inputs are finite; a program needn't handle non-finite values.
Results may differ from the reference program's by a relative error of at most 0.0075.
Values may be sent and summed in bfloat16 or wider, within the bound.
No kernel may reach another device: no remote copies, remote signals or barrier semaphores. Data moves between devices by JAX's collectives and lax.ppermute only.
A program may use at most 64 MiB of HBM per device.

```python
import jax
import jax.numpy as jnp
from jax import lax

D = 4096
HD = 128
KVH = 4
GROUP = 4
BLK = 32
PAD = 128
HB = 128
NDOCS = 10
TOK_DEV = 512
SEQS = 8
LEN = 8192
STRETCHES = 256
SBLK = 16
CAP = 1
SPREAD = 16
DOCUNITS = 64
LONGU = 8
MAXTOK = 1024
QH = 16
NBLK = 32
COLS = 1024
N_DP = 8


def draw_sign_vector(key, part):
    picked = jax.random.randint(key, (NBLK, HB), 0, 2)
    return (2 * picked - 1).astype(jnp.int32)


def doc_row(key):
    pick_key, fill_key = jax.random.split(key, 2)
    longest = LONGU
    ratio = TOK_DEV // PAD
    top_pick = (longest + 1) // ratio
    first_len = jnp.maximum(ratio * jax.random.randint(pick_key, (), 1, top_pick + 1) - 1, 1).astype(jnp.int32)
    others = NDOCS - 2
    extra = DOCUNITS - longest - first_len - others

    def add_one(index_val, counts):
        scores = jax.random.randint(jax.random.fold_in(fill_key, index_val), (others,), 0, 1 << 20) * others
        scores = scores + jnp.arange(others, dtype=jnp.int32)
        scores = jnp.where(counts < longest, scores, -1)
        chosen = lax.top_k(scores, 1)[1][0]
        return counts + (jnp.arange(others, dtype=jnp.int32) == chosen).astype(jnp.int32)
    counts = lax.fori_loop(0, extra, add_one, jnp.ones((others,), jnp.int32))
    head = jnp.stack([first_len, jnp.int32(longest)])
    return jnp.concatenate([head, counts]).astype(jnp.int32)


def draw_doc_stretches(key, part):
    keys_all = jax.random.split(key, SEQS)
    return jax.vmap(doc_row)(keys_all).astype(jnp.int32)


def shuffle_slots(sub_key):
    return jax.random.permutation(sub_key, SBLK)


def order_row(key):
    devices = STRETCHES // SBLK
    offset_key, send_key, slot_key = jax.random.split(key, 3)
    offsets = jax.random.permutation(offset_key, devices)[:SPREAD]
    send_perm = jax.vmap(shuffle_slots)(jax.random.split(send_key, devices))
    slot_perm = jax.vmap(shuffle_slots)(jax.random.split(slot_key, devices))
    source = jnp.arange(devices, dtype=jnp.int32)[:, None]
    lane = send_perm % SPREAD
    copy_index = send_perm // SPREAD
    target = (source + offsets[lane]) % devices
    landing = slot_perm[target, lane * CAP + copy_index]
    return (target * SBLK + landing).reshape(STRETCHES).astype(jnp.int32)


def draw_stretch_order(key, part):
    keys_all = jax.random.split(key, SEQS)
    return jax.vmap(order_row)(keys_all).astype(jnp.int32)


def plant(array, own_key, least, top_value):
    index_at = [jax.random.randint(jax.random.fold_in(own_key, axis), (), 0, length) for axis, length in enumerate(array.shape)]
    widest = array.shape.index(max(array.shape))
    neighbour = index_at[:widest] + [(index_at[widest] + 1) % array.shape[widest]] + index_at[widest + 1:]
    return array.at[tuple(index_at)].set(least).at[tuple(neighbour)].set(top_value)


def steps_of(key, extent, cuts, low, high):
    loudness, own = 1.0, jax.random.fold_in(key, 6)
    for dim, shards_of in cuts:
        draws = jnp.exp(jax.random.uniform(jax.random.fold_in(own, dim), (shards_of,), jnp.float32, low / len(cuts), high / len(cuts)))
        loudness = loudness * jnp.repeat(draws, extent[dim] // shards_of).reshape([-1 if axis == dim else 1 for axis in range(len(extent))])
    return loudness


def bell_draw(key, extent, scale, most, cuts=(), kind=jnp.bfloat16):
    result = jax.random.normal(key, extent, jnp.float32) * scale
    if len(cuts) > 0:
        result = steps_of(key, extent, cuts, -0.22, 0.18) * result
    return jnp.clip(result, min=-most, max=most).astype(kind)


def setup_inputs(seed: int = 0) -> dict:
    key_list = jax.random.split(jax.random.key(seed), 12)
    layer_input = bell_draw(key_list[0], (SEQS, LEN, D), 1.0, 6.0, ((0, 8), (1, 16), (2, 4)))
    queries = bell_draw(key_list[1], (SEQS, QH, LEN, HD), 1.0, 6.0, ((0, 8), (1, 4), (2, 16)))
    key_states = bell_draw(key_list[2], (SEQS, KVH, LEN, HD), 1.0, 6.0, ((0, 8), (1, 4), (2, 16)))
    value_states = bell_draw(key_list[3], (SEQS, KVH, LEN, HD), 1.0, 6.0, ((0, 8), (1, 4), (2, 16)))
    out_grad = bell_draw(key_list[4], (SEQS, QH, LEN, HD), (LEN * N_DP) ** -0.5, 0.0234375, ((0, 8), (1, 4), (2, 16)))
    log_sums = jnp.clip(2.0 + 3.0 * jax.random.uniform(key_list[5], (SEQS, QH, LEN), jnp.float32) ** steps_of(key_list[5], (SEQS, QH, LEN), ((0, 8), (1, 4), (2, 16)), -0.2, 0.2), 2.0, 5.0).astype(jnp.bfloat16)
    grad_dots = bell_draw(key_list[6], (SEQS, QH, LEN), (LEN * N_DP // 64) ** -0.5, 0.1875, ((0, 8), (1, 4), (2, 16)))
    doc_stretches = draw_doc_stretches(jax.random.fold_in(key_list[11], 71), 0)
    stretch_order = draw_stretch_order(jax.random.fold_in(key_list[11], 71), 0)
    sign_vector = draw_sign_vector(jax.random.fold_in(key_list[11], 71), 0)
    exponents = plant(jax.random.randint(key_list[10], (SEQS, NBLK), 0, 4), jax.random.fold_in(key_list[10], 1), 0, 3).astype(jnp.int32)
    return dict(layer_input=layer_input, queries=queries, key_states=key_states, value_states=value_states, out_grad=out_grad, log_sums=log_sums, grad_dots=grad_dots, doc_stretches=doc_stretches, stretch_order=stretch_order, sign_vector=sign_vector, exponents=exponents)


def hadamard_table(table_size):
    index_row = jnp.arange(table_size, dtype=jnp.int32)
    common = jnp.bitwise_and(index_row[:, None], index_row[None, :])
    parity = jnp.zeros((table_size, table_size), jnp.int32)
    for bit_pos in range(table_size.bit_length() - 1):
        parity = parity + jnp.bitwise_and(jnp.right_shift(common, bit_pos), 1)
    signed = 1 - 2 * jnp.bitwise_and(parity, 1)
    return signed.astype(jnp.float32) * (float(table_size) ** -0.5)


def sort_blocks(values, inverse, axis_pos):
    shape_list = list(values.shape)
    split_shape = shape_list[:axis_pos] + [STRETCHES, BLK] + shape_list[axis_pos + 1:]
    blocked = values.reshape(split_shape)
    picked = jnp.take(blocked, inverse, axis=axis_pos)
    return picked.reshape(shape_list)


def member_columns(query_seq, key_seq, value_seq, grad_seq, lse_seq, dots_seq, lengths_seq, order_seq):
    inverse = jnp.argsort(order_seq).astype(jnp.int32)
    query_sorted = sort_blocks(query_seq, inverse, 1).astype(jnp.float32)
    key_sorted = sort_blocks(key_seq, inverse, 1).astype(jnp.float32)
    value_sorted = sort_blocks(value_seq, inverse, 1).astype(jnp.float32)
    grad_sorted = sort_blocks(grad_seq, inverse, 1).astype(jnp.float32)
    lse_sorted = sort_blocks(lse_seq, inverse, 1).astype(jnp.float32)
    dots_sorted = sort_blocks(dots_seq, inverse, 1).astype(jnp.float32)
    ends = jnp.cumsum(lengths_seq).astype(jnp.int32)
    positions = jnp.arange(LEN, dtype=jnp.int32)
    token_doc = jnp.sum(((positions // PAD)[:, None] >= ends[None, :]).astype(jnp.int32), axis=1)
    window = MAXTOK // BLK
    width = MAXTOK
    scale = HD ** -0.5

    query_heads = query_sorted.reshape(KVH, GROUP, LEN, HD)
    grad_heads = grad_sorted.reshape(KVH, GROUP, LEN, HD)
    lse_heads = lse_sorted.reshape(KVH, GROUP, LEN)
    dots_heads = dots_sorted.reshape(KVH, GROUP, LEN)

    def one_head(operands):
        query_group, grad_group, lse_group, dots_group, key_head, value_head = operands

        def visit(carry, block_index):
            key_total, value_total = carry
            first_token = block_index * BLK
            window_start = jnp.clip(block_index - (window - 1), 0, STRETCHES - window) * BLK
            query_block = lax.dynamic_slice_in_dim(query_group, first_token, BLK, 1)
            grad_block = lax.dynamic_slice_in_dim(grad_group, first_token, BLK, 1)
            lse_block = lax.dynamic_slice_in_dim(lse_group, first_token, BLK, 1)
            dots_block = lax.dynamic_slice_in_dim(dots_group, first_token, BLK, 1)
            key_window = lax.dynamic_slice_in_dim(key_head, window_start, width, 0)
            value_window = lax.dynamic_slice_in_dim(value_head, window_start, width, 0)
            query_pos = lax.dynamic_slice_in_dim(positions, first_token, BLK, 0)
            query_doc = lax.dynamic_slice_in_dim(token_doc, first_token, BLK, 0)
            key_pos = lax.dynamic_slice_in_dim(positions, window_start, width, 0)
            key_doc = lax.dynamic_slice_in_dim(token_doc, window_start, width, 0)
            live = (query_doc[:, None] == key_doc[None, :]) & (key_pos[None, :] <= query_pos[:, None])
            scores = jnp.einsum('hqd,kd->hqk', query_block, key_window) * scale
            probs = jnp.where(live[None], jnp.exp(scores - lse_block[:, :, None]), 0.0)
            probs_low = lax.optimization_barrier(probs.astype(jnp.bfloat16)).astype(jnp.float32)
            value_part = jnp.einsum('hqk,hqd->kd', probs_low, grad_block)
            dprobs = jnp.einsum('hqd,kd->hqk', grad_block, value_window)
            dscores = probs * (dprobs - dots_block[:, :, None])
            dscores = lax.optimization_barrier(dscores.astype(jnp.bfloat16)).astype(jnp.float32)
            key_part = jnp.einsum('hqk,hqd->kd', dscores, query_block) * scale
            key_old = lax.dynamic_slice_in_dim(key_total, window_start, width, 0)
            value_old = lax.dynamic_slice_in_dim(value_total, window_start, width, 0)
            key_total = lax.dynamic_update_slice_in_dim(key_total, key_old + key_part, window_start, 0)
            value_total = lax.dynamic_update_slice_in_dim(value_total, value_old + value_part, window_start, 0)
            return (key_total, value_total), 0

        empty = jnp.zeros((LEN, HD), jnp.float32)
        totals, unused = lax.scan(visit, (empty, empty), jnp.arange(STRETCHES, dtype=jnp.int32))
        return jnp.stack([totals[0], totals[1]], axis=0).astype(jnp.bfloat16)

    stacked = lax.map(one_head, (query_heads, grad_heads, lse_heads, dots_heads, key_sorted, value_sorted))
    columns = jnp.transpose(stacked, (2, 0, 1, 3)).reshape(LEN, COLS)
    return columns, inverse


def reference(layer_input, queries, key_states, value_states, out_grad, log_sums, grad_dots, doc_stretches, stretch_order, sign_vector, exponents):
    had = hadamard_table(HB)
    signs_float = sign_vector.astype(jnp.float32)
    summed = jnp.zeros((NBLK, HB, COLS), jnp.float32)
    for seq_index in range(SEQS):
        columns, inverse = member_columns(queries[seq_index], key_states[seq_index], value_states[seq_index], out_grad[seq_index], log_sums[seq_index], grad_dots[seq_index], doc_stretches[seq_index], stretch_order[seq_index])
        input_sorted = sort_blocks(layer_input[seq_index], inverse, 0)
        member_grad = jnp.dot(input_sorted.T, columns, preferred_element_type=jnp.float32)
        shaped = member_grad.reshape(NBLK, HB, COLS) * signs_float[:, :, None]
        rotated = jnp.einsum('ij,bjc->bic', had, shaped, precision=lax.Precision.HIGHEST)
        factor = 1.0 / jnp.left_shift(jnp.int32(1), exponents[seq_index]).astype(jnp.float32)
        quantized = (rotated * factor[:, None, None]).astype(jnp.bfloat16)
        summed = summed + quantized.astype(jnp.float32)
    return summed
```

```python
import jax
import jax.numpy as jnp
from jax import lax
from jax.experimental import pallas as pl
from jax.experimental.pallas import tpu as pltpu
from jax.sharding import Mesh
from jax.sharding import PartitionSpec as P

HD = 128
GROUP = 4
BLK = 32
PAD = 128
HB = 128
CORES = 2
SPAN = 3
LOG2E = 1.4426950408889634

QROWS = GROUP * BLK
KV_AT = 2 * QROWS
AUX_AT = KV_AT + SPAN * 2 * BLK
AUX_ROWS = 16
ROWS = AUX_AT + AUX_ROWS
UNIT_BLKS = PAD // BLK


def hadamard_signs(table_size):
    index_row = jnp.arange(table_size, dtype=jnp.int32)
    common = jnp.bitwise_and(index_row[:, None], index_row[None, :])
    parity = jnp.zeros((table_size, table_size), jnp.int32)
    for bit_pos in range(table_size.bit_length() - 1):
        parity = parity + jnp.bitwise_and(jnp.right_shift(common, bit_pos), 1)
    return (1 - 2 * jnp.bitwise_and(parity, 1)).astype(jnp.bfloat16)


def pack_kernel(order_ref, where_ref, query_ref, grad_ref, key_ref, value_ref, aux_ref, out_ref):
    slots = key_ref.shape[0] // BLK
    groups = out_ref.shape[0]
    first = where_ref[0] * slots
    for span in range(1, SPAN):
        for dest in range(span):
            at = KV_AT + span * 2 * BLK
            out_ref[dest, at : at + 2 * BLK, :] = jnp.zeros((2 * BLK, HD), out_ref.dtype)
    for slot in range(slots):
        dest = order_ref[first + slot] // slots
        rows = slice(slot * BLK, (slot + 1) * BLK)
        for head in range(GROUP):
            out_ref[dest, head * BLK : (head + 1) * BLK, :] = query_ref[head, rows, :]
            at = QROWS + head * BLK
            out_ref[dest, at : at + BLK, :] = grad_ref[head, rows, :]
        out_ref[dest, AUX_AT:ROWS, :] = aux_ref[slot]
        key_blk = key_ref[rows, :]
        value_blk = value_ref[rows, :]
        for span in range(SPAN):

            @pl.when(dest + span < groups)
            def _():
                at = KV_AT + span * 2 * BLK
                out_ref[dest + span, at : at + BLK, :] = key_blk
                out_ref[dest + span, at + BLK : at + 2 * BLK, :] = value_blk


def attend_kernel(
    slot_ref, start_ref, recv_ref, out_ref,
    query_scr, grad_scr, stat_scr, key_scr, value_scr, dkey_scr, dvalue_scr,
):
    groups = recv_ref.shape[0]
    chunk = key_scr.shape[0] // SPAN
    units = chunk // PAD
    width = UNIT_BLKS * QROWS
    dkey_scr[...] = jnp.zeros_like(dkey_scr)
    dvalue_scr[...] = jnp.zeros_like(dvalue_scr)
    for src in range(groups):
        slot = slot_ref[0, src]
        at = pl.multiple_of(slot * QROWS, QROWS)
        query_scr[pl.ds(at, QROWS), :] = recv_ref[src, 0:QROWS, :]
        grad_scr[pl.ds(at, QROWS), :] = recv_ref[src, QROWS : 2 * QROWS, :]
        stat_scr[slot] = recv_ref[src, AUX_AT:ROWS, :].astype(jnp.float32)
        for span in range(SPAN):
            row = (SPAN - 1 - span) * chunk + slot_ref[span, src] * BLK
            row = pl.multiple_of(row, BLK)
            at = KV_AT + span * 2 * BLK
            key_scr[pl.ds(row, BLK), :] = recv_ref[src, at : at + BLK, :]
            value_scr[pl.ds(row, BLK), :] = recv_ref[src, at + BLK : at + 2 * BLK, :]

    scale = HD ** (-0.5)
    key_at = lax.broadcasted_iota(jnp.int32, (PAD, width), 0)
    column = lax.broadcasted_iota(jnp.int32, (PAD, width), 1)
    query_at = (column // QROWS) * BLK + column % BLK
    causal = key_at <= query_at

    for unit in range(units):
        cols = slice(unit * width, (unit + 1) * width)
        blocks = range(unit * UNIT_BLKS, (unit + 1) * UNIT_BLKS)
        lse = jnp.concatenate([stat_scr[b, 0:1, :] for b in blocks], axis=1) * LOG2E
        dots = jnp.concatenate([stat_scr[b, 1:2, :] for b in blocks], axis=1)

        def visit(tile, diagonal):
            row = pl.multiple_of(tile * PAD, PAD)
            query_blk = query_scr[cols, :]
            grad_blk = grad_scr[cols, :]
            key_blk = key_scr[pl.ds(row, PAD), :]
            value_blk = value_scr[pl.ds(row, PAD), :]
            contract_last = (((1,), (1,)), ((), ()))
            scores = lax.dot_general(
                key_blk, query_blk, contract_last, preferred_element_type=jnp.float32
            )
            probs = jnp.exp2(scores * (scale * LOG2E) - lse)
            if diagonal:
                probs = jnp.where(causal, probs, 0.0)
            dprobs = lax.dot_general(
                value_blk, grad_blk, contract_last, preferred_element_type=jnp.float32
            )
            dscores = (probs * (dprobs - dots)).astype(jnp.bfloat16)
            dvalue_scr[pl.ds(row, PAD), :] += jnp.dot(
                probs.astype(jnp.bfloat16), grad_blk, preferred_element_type=jnp.float32
            )
            dkey_scr[pl.ds(row, PAD), :] += jnp.dot(
                dscores, query_blk, preferred_element_type=jnp.float32
            )

        last = (SPAN - 1) * units + unit

        @pl.loop(start_ref[unit], last)
        def _(tile):
            visit(tile, False)

        visit(jnp.int32(last), True)

    for src in range(groups):
        for span in range(SPAN):
            row = (SPAN - 1 - span) * chunk + slot_ref[span, src] * BLK
            row = pl.multiple_of(row, BLK)
            dkey = dkey_scr[pl.ds(row, BLK), :] * scale
            out_ref[src, span, 0:BLK, :] = dkey.astype(out_ref.dtype)
            out_ref[src, span, BLK : 2 * BLK, :] = dvalue_scr[pl.ds(row, BLK), :].astype(
                out_ref.dtype
            )


def collect_kernel(target_ref, recv_ref, out_ref):
    groups = recv_ref.shape[0]
    for slot in range(out_ref.shape[0] // BLK):
        owner = target_ref[slot]
        total = recv_ref[owner, 0].astype(jnp.float32)
        for span in range(1, SPAN):
            extra = recv_ref[jnp.minimum(owner + span, groups - 1), span].astype(jnp.float32)
            total = total + jnp.where(owner + span < groups, extra, 0.0)
        rows = slice(slot * BLK, (slot + 1) * BLK)
        total = total.astype(out_ref.dtype)
        out_ref[rows, 0:HD] = total[0:BLK]
        out_ref[rows, HD : 2 * HD] = total[BLK : 2 * BLK]


def turn_kernel(core_ref, input_ref, own_ref, other_ref):
    span = 2 * HB
    core = core_ref[0]
    for part in range(own_ref.shape[0] // span):
        rows = slice(part * span, (part + 1) * span)
        at = pl.multiple_of((CORES * part + core) * span, span)
        own_ref[rows, :] = input_ref[:, pl.ds(at, span)].T
        at = pl.multiple_of((CORES * part + 1 - core) * span, span)
        other_ref[rows, :] = input_ref[:, pl.ds(at, span)].T


def product_kernel(
    core_ref, own_ref, other_ref, own_kv_ref, other_kv_ref, had_ref, aux_ref, out_ref
):
    grad = jnp.dot(own_ref[...], own_kv_ref[...], preferred_element_type=jnp.float32)
    grad = grad + jnp.dot(other_ref[...], other_kv_ref[...], preferred_element_type=jnp.float32)
    aux = aux_ref[0].astype(jnp.float32)
    replicas = out_ref.shape[0]
    had = had_ref[...].astype(jnp.float32)
    for blk in range(grad.shape[0] // HB):
        rows = grad[blk * HB : (blk + 1) * HB]
        table = (had * aux[2 + blk : 3 + blk, :]).astype(jnp.bfloat16)
        high = rows.astype(jnp.bfloat16)
        low = (rows - high.astype(jnp.float32)).astype(jnp.bfloat16)
        rotated = jnp.dot(table, high, preferred_element_type=jnp.float32)
        rotated = rotated + jnp.dot(table, low, preferred_element_type=jnp.float32)
        factor = aux[4 + blk : 5 + blk, :] * (HB ** (-0.5))
        rotated = rotated * jnp.concatenate([factor] * (rows.shape[1] // HB), axis=1)
        out_ref[:, 0, blk] = rotated.astype(out_ref.dtype).reshape(
            replicas, HB // replicas, rows.shape[1]
        )


def prefetched(kernel, scalars, out_shape, scratch=(), grid=(), in_specs=None, out_specs=None):
    vmem = pl.BlockSpec(memory_space=pltpu.VMEM)
    many = isinstance(out_shape, tuple)

    def call(*operands):
        specs = in_specs or [vmem] * (len(operands) - scalars)
        outs = out_specs or (tuple(vmem for _ in out_shape) if many else vmem)
        return pl.pallas_call(
            kernel,
            out_shape=out_shape,
            grid_spec=pltpu.PrefetchScalarGridSpec(
                num_scalar_prefetch=scalars,
                grid=grid,
                in_specs=specs,
                out_specs=outs,
                scratch_shapes=list(scratch),
            ),
            compiler_params=pltpu.CompilerParams(vmem_limit_bytes=48 << 20),
        )(*operands)

    return call


def per_device(
    layer_input,
    queries,
    key_states,
    value_states,
    out_grad,
    log_sums,
    grad_dots,
    doc_stretches,
    stretch_order,
    sign_vector,
    exponents,
):
    context = ("y", "core")
    low = jnp.bfloat16
    tokens = queries.shape[2]
    slots = tokens // BLK
    groups = lax.axis_size(context)
    lines = lax.axis_size("y")
    replicas = lax.axis_size("dp")
    widths = lax.axis_size("tensor")
    order_row = stretch_order[0]
    where = lax.axis_index(context)
    core = lax.axis_index("core").reshape(1)

    def by_block(array):
        return jnp.transpose(array[0].reshape(GROUP, slots, BLK), (1, 0, 2)).reshape(slots, 1, HD)

    signs = jnp.broadcast_to(sign_vector.astype(low)[None], (slots, 2, HB))
    factor = 1.0 / jnp.left_shift(jnp.int32(1), exponents[0]).astype(jnp.float32)
    factors = jnp.broadcast_to(factor.astype(low)[None, :, None], (slots, 2, HB))
    aux = jnp.concatenate(
        [
            by_block(log_sums),
            by_block(grad_dots),
            signs,
            factors,
            jnp.zeros((slots, AUX_ROWS - 6, HD), low),
        ],
        axis=1,
    )
    packed = prefetched(pack_kernel, 2, jax.ShapeDtypeStruct((groups, ROWS, HD), low))(
        order_row,
        where.reshape(1),
        queries[0],
        out_grad[0],
        key_states[0, 0],
        value_states[0, 0],
        aux,
    )
    recv = lax.all_to_all(packed, context, split_axis=0, concat_axis=0, tiled=True)

    half = layer_input.shape[2] // CORES
    turned = jax.ShapeDtypeStruct((half, tokens), low)
    own_input, other_input = prefetched(turn_kernel, 1, (turned, turned))(core, layer_input[0])
    other_input = lax.ppermute(other_input, "core", [(0, 1), (1, 0)])
    own_input = lax.all_gather(own_input, "tensor", axis=0, tiled=True)
    other_input = lax.all_gather(other_input, "tensor", axis=0, tiled=True)

    order_grid = order_row.reshape(groups, slots)
    chunk_ids = (where - jnp.arange(SPAN, dtype=jnp.int32))[:, None, None]
    slot_map = jnp.sum(
        jnp.where(order_grid[None] // slots == chunk_ids, order_grid[None] % slots, 0), axis=2
    )
    ends = jnp.cumsum(doc_stretches[0])
    chunk_units = tokens // PAD
    unit_ids = where * chunk_units + jnp.arange(chunk_units, dtype=jnp.int32)
    doc_start = jnp.max(jnp.where(ends[None, :] <= unit_ids[:, None], ends[None, :], 0), axis=1)
    starts = doc_start - (where - (SPAN - 1)) * chunk_units

    window = SPAN * tokens
    partial_grads = prefetched(
        attend_kernel,
        2,
        jax.ShapeDtypeStruct((groups, SPAN, 2 * BLK, HD), low),
        scratch=(
            pltpu.VMEM((slots * QROWS, HD), low),
            pltpu.VMEM((slots * QROWS, HD), low),
            pltpu.VMEM((slots, AUX_ROWS, HD), jnp.float32),
            pltpu.VMEM((window, HD), low),
            pltpu.VMEM((window, HD), low),
            pltpu.VMEM((window, HD), jnp.float32),
            pltpu.VMEM((window, HD), jnp.float32),
        ),
    )(slot_map, starts, recv)
    returned = lax.all_to_all(partial_grads, context, split_axis=0, concat_axis=0, tiled=True)
    targets = lax.dynamic_slice_in_dim(order_row, where * slots, slots, 0) // slots
    own_kv = prefetched(collect_kernel, 1, jax.ShapeDtypeStruct((tokens, 2 * HD), low))(
        targets, returned
    )
    other_kv = lax.ppermute(own_kv, "core", [(0, 1), (1, 0)])

    rows = 2 * HB
    spread = prefetched(
        product_kernel,
        1,
        jax.ShapeDtypeStruct((replicas, lines, 2, HB // replicas, 2 * HD), low),
        grid=(lines,),
        in_specs=[
            pl.BlockSpec((rows, tokens), lambda i, core: (i, 0)),
            pl.BlockSpec((rows, tokens), lambda i, core: (i, 0)),
            pl.BlockSpec((tokens, 2 * HD), lambda i, core: (0, 0)),
            pl.BlockSpec((tokens, 2 * HD), lambda i, core: (0, 0)),
            pl.BlockSpec((HB, HB), lambda i, core: (0, 0)),
            pl.BlockSpec(
                (1, AUX_ROWS, HD), lambda i, core: (CORES * i + core[0], AUX_AT // AUX_ROWS, 0)
            ),
        ],
        out_specs=pl.BlockSpec(
            (replicas, 1, 2, HB // replicas, 2 * HD), lambda i, core: (0, i, 0, 0, 0)
        ),
    )(core, own_input, other_input, own_kv, other_kv, hadamard_signs(HB), recv)
    spread = spread.reshape(replicas * lines, 2, HB // replicas, 2 * HD)
    shares = lax.all_to_all(spread, ("dp", "y"), split_axis=0, concat_axis=0, tiled=True)
    return jnp.sum(shares.astype(jnp.float32), axis=0)


def solution(mesh):
    replicas, groups, widths = mesh.devices.shape
    split = Mesh(
        mesh.devices.reshape(replicas, groups // CORES, CORES, widths),
        ("dp", "y", "core", "tensor"),
    )
    context = ("y", "core")
    return jax.shard_map(
        per_device,
        mesh=split,
        in_specs=(
            P("dp", context, "tensor"),
            P("dp", "tensor", context, None),
            P("dp", "tensor", context, None),
            P("dp", "tensor", context, None),
            P("dp", "tensor", context, None),
            P("dp", "tensor", context),
            P("dp", "tensor", context),
            P("dp", None),
            P("dp", None),
            P(context, None),
            P("dp", context),
        ),
        out_specs=P(context, "dp", "tensor"),
        check_vma=False,
    )
```

```python
import jax
import jax.numpy as jnp
from jax import lax
from jax.experimental import pallas as pl
from jax.experimental.pallas import tpu as pltpu
from jax.sharding import Mesh
from jax.sharding import PartitionSpec as P

HD = 128
GROUP = 4
BLK = 32
PAD = 128
HB = 128
CORES = 2
SPAN = 3
LOG2E = 1.4426950408889634

QROWS = GROUP * BLK
KV_AT = 2 * QROWS
AUX_AT = KV_AT + SPAN * 2 * BLK
AUX_ROWS = 16
ROWS = AUX_AT + AUX_ROWS
UNIT_BLKS = PAD // BLK


def hadamard_signs(table_size):
    index_row = jnp.arange(table_size, dtype=jnp.int32)
    common = jnp.bitwise_and(index_row[:, None], index_row[None, :])
    parity = jnp.zeros((table_size, table_size), jnp.int32)
    for bit_pos in range(table_size.bit_length() - 1):
        parity = parity + jnp.bitwise_and(jnp.right_shift(common, bit_pos), 1)
    return (1 - 2 * jnp.bitwise_and(parity, 1)).astype(jnp.bfloat16)


def pack_kernel(
    order_ref, where_ref, exponent_ref,
    query_ref, grad_ref, key_ref, value_ref, lse_ref, dots_ref, sign_ref, out_ref,
):
    slots = key_ref.shape[0] // BLK
    groups = out_ref.shape[0]
    first = where_ref[0] * slots
    for span in range(1, SPAN):
        for dest in range(span):
            at = KV_AT + span * 2 * BLK
            out_ref[dest, at : at + 2 * BLK, :] = jnp.zeros((2 * BLK, HD), out_ref.dtype)
    signs = sign_ref[...].astype(jnp.float32)
    fixed = [signs]
    for blk in range(sign_ref.shape[0]):
        power = jnp.full((1, HD), jnp.left_shift(jnp.int32(1), exponent_ref[blk]), jnp.int32)
        fixed.append(1.0 / power.astype(jnp.float32))
    fixed.append(jnp.zeros((AUX_ROWS - 6, HD), jnp.float32))
    head_of = lax.broadcasted_iota(jnp.int32, (1, HD), 1) // BLK
    stats = (lse_ref[...].astype(jnp.float32), dots_ref[...].astype(jnp.float32))

    def by_head(array, slot):
        part = slot * BLK // HD * HD
        inner = slot % (HD // BLK)
        row = jnp.zeros((1, HD), jnp.float32)
        for head in range(GROUP):
            line = array[head : head + 1, part : part + HD]
            turn = (head - inner) * BLK % HD
            line = pltpu.roll(line, turn, 1) if turn else line
            row = jnp.where(head_of == head, line, row)
        return row

    for slot in range(slots):
        dest = order_ref[first + slot] // slots
        rows = slice(slot * BLK, (slot + 1) * BLK)
        for head in range(GROUP):
            out_ref[dest, head * BLK : (head + 1) * BLK, :] = query_ref[head, rows, :]
            at = QROWS + head * BLK
            out_ref[dest, at : at + BLK, :] = grad_ref[head, rows, :]
        aux = jnp.concatenate([by_head(array, slot) for array in stats] + fixed, axis=0)
        out_ref[dest, AUX_AT:ROWS, :] = aux.astype(out_ref.dtype)
        key_blk = key_ref[rows, :]
        value_blk = value_ref[rows, :]
        for span in range(SPAN):

            @pl.when(dest + span < groups)
            def _():
                at = KV_AT + span * 2 * BLK
                out_ref[dest + span, at : at + BLK, :] = key_blk
                out_ref[dest + span, at + BLK : at + 2 * BLK, :] = value_blk


def attend_kernel(
    slot_ref, start_ref, recv_ref, out_ref,
    query_scr, grad_scr, query_turned, grad_turned, stat_scr,
    key_scr, value_scr, dkey_scr, dvalue_scr,
):
    groups = recv_ref.shape[0]
    chunk = key_scr.shape[0] // SPAN
    units = chunk // PAD
    width = UNIT_BLKS * QROWS
    pair = 2 * PAD
    dkey_scr[...] = jnp.zeros_like(dkey_scr)
    dvalue_scr[...] = jnp.zeros_like(dvalue_scr)
    for src in range(groups):
        slot = slot_ref[0, src]
        at = pl.multiple_of(slot * QROWS, QROWS)
        query_blk = recv_ref[src, 0:QROWS, :]
        grad_blk = recv_ref[src, QROWS : 2 * QROWS, :]
        query_scr[pl.ds(at, QROWS), :] = query_blk
        grad_scr[pl.ds(at, QROWS), :] = grad_blk
        query_turned[:, pl.ds(at, QROWS)] = query_blk.T
        grad_turned[:, pl.ds(at, QROWS)] = grad_blk.T
        stat_scr[slot] = recv_ref[src, AUX_AT:ROWS, :].astype(jnp.float32)
        for span in range(SPAN):
            row = (SPAN - 1 - span) * chunk + slot_ref[span, src] * BLK
            row = pl.multiple_of(row, BLK)
            at = KV_AT + span * 2 * BLK
            key_scr[pl.ds(row, BLK), :] = recv_ref[src, at : at + BLK, :]
            value_scr[pl.ds(row, BLK), :] = recv_ref[src, at + BLK : at + 2 * BLK, :]

    scale = HD ** (-0.5)
    key_at = lax.broadcasted_iota(jnp.int32, (pair, width), 0)
    column = lax.broadcasted_iota(jnp.int32, (pair, width), 1)
    query_at = (column // QROWS) * BLK + column % BLK
    causal = key_at - PAD <= query_at

    for unit in range(units):
        cols = slice(unit * width, (unit + 1) * width)
        blocks = range(unit * UNIT_BLKS, (unit + 1) * UNIT_BLKS)
        lse = jnp.concatenate([stat_scr[b, 0:1, :] for b in blocks], axis=1) * LOG2E
        dots = jnp.concatenate([stat_scr[b, 1:2, :] for b in blocks], axis=1)

        def visit(row, live):
            rows = pl.ds(row, pair)
            scores = jnp.dot(
                key_scr[rows, :], query_turned[:, cols], preferred_element_type=jnp.float32
            )
            dprobs = jnp.dot(
                value_scr[rows, :], grad_turned[:, cols], preferred_element_type=jnp.float32
            )
            probs = jnp.where(live, jnp.exp2(scores * (scale * LOG2E) - lse), 0.0)
            dscores = (probs * (dprobs - dots)).astype(jnp.bfloat16)
            dvalue_scr[rows, :] += jnp.dot(
                probs.astype(jnp.bfloat16), grad_scr[cols, :], preferred_element_type=jnp.float32
            )
            dkey_scr[rows, :] += jnp.dot(
                dscores, query_scr[cols, :], preferred_element_type=jnp.float32
            )

        first = start_ref[unit]
        last = (SPAN - 1) * units + unit
        visit((last - 1) * PAD, causal & (key_at >= (first - (last - 1)) * PAD))

        @pl.loop(1, (last - first + 2) // 2)
        def _(step):
            base = last - 1 - 2 * step
            visit(pl.multiple_of(base * PAD, PAD), key_at >= (first - base) * PAD)

    for src in range(groups):
        for span in range(SPAN):
            row = (SPAN - 1 - span) * chunk + slot_ref[span, src] * BLK
            row = pl.multiple_of(row, BLK)
            dkey = dkey_scr[pl.ds(row, BLK), :] * scale
            out_ref[src, span, 0:BLK, :] = dkey.astype(out_ref.dtype)
            out_ref[src, span, BLK : 2 * BLK, :] = dvalue_scr[pl.ds(row, BLK), :].astype(
                out_ref.dtype
            )


def collect_kernel(target_ref, recv_ref, out_ref):
    groups = recv_ref.shape[0]
    for slot in range(out_ref.shape[0] // BLK):
        owner = target_ref[slot]
        total = recv_ref[owner, 0].astype(jnp.float32)
        for span in range(1, SPAN):
            extra = recv_ref[jnp.minimum(owner + span, groups - 1), span].astype(jnp.float32)
            total = total + jnp.where(owner + span < groups, extra, 0.0)
        rows = slice(slot * BLK, (slot + 1) * BLK)
        total = total.astype(out_ref.dtype)
        out_ref[rows, 0:HD] = total[0:BLK]
        out_ref[rows, HD : 2 * HD] = total[BLK : 2 * BLK]


def turn_kernel(core_ref, input_ref, own_ref, other_ref):
    span = 2 * HB
    core = core_ref[0]
    for part in range(own_ref.shape[0] // span):
        rows = slice(part * span, (part + 1) * span)
        at = pl.multiple_of((CORES * part + core) * span, span)
        own_ref[rows, :] = input_ref[:, pl.ds(at, span)].T
        at = pl.multiple_of((CORES * part + 1 - core) * span, span)
        other_ref[rows, :] = input_ref[:, pl.ds(at, span)].T


def product_kernel(where_ref, *refs):
    own_refs = refs[: len(refs) // 2 - 2]
    other_refs = refs[len(own_refs) : 2 * len(own_refs)]
    own_kv_ref, other_kv_ref, had_ref, aux_ref, out_ref = refs[2 * len(own_refs) :]
    core, width = where_ref[0], where_ref[1]
    replicas = out_ref.shape[0]
    span = 2 * HB
    parts = own_refs[0].shape[0] // span
    had = had_ref[...].astype(jnp.float32)
    for step, (own_ref, other_ref) in enumerate(zip(own_refs, other_refs)):
        source = (width + len(own_refs) - step) % len(own_refs)
        grad = jnp.dot(own_ref[...], own_kv_ref[...], preferred_element_type=jnp.float32)
        grad += jnp.dot(other_ref[...], other_kv_ref[...], preferred_element_type=jnp.float32)
        for part in range(parts):
            line = source * parts + part
            aux = aux_ref[CORES * line + core].astype(jnp.float32)
            for blk in range(2):
                at = part * span + blk * HB
                rows = grad[at : at + HB]
                table = (had * aux[2 + blk : 3 + blk, :]).astype(jnp.bfloat16)
                high = rows.astype(jnp.bfloat16)
                low = (rows - high.astype(jnp.float32)).astype(jnp.bfloat16)
                rotated = jnp.dot(table, high, preferred_element_type=jnp.float32)
                rotated += jnp.dot(table, low, preferred_element_type=jnp.float32)
                factor = aux[4 + blk : 5 + blk, :] * (HB ** (-0.5))
                rotated *= jnp.concatenate([factor] * (rows.shape[1] // HB), axis=1)
                out_ref[:, line, blk] = rotated.astype(out_ref.dtype).reshape(
                    replicas, HB // replicas, rows.shape[1]
                )


def prefetched(kernel, scalars, out_shape, scratch=()):
    vmem = pl.BlockSpec(memory_space=pltpu.VMEM)

    def call(*operands):
        return pl.pallas_call(
            kernel,
            out_shape=out_shape,
            grid_spec=pltpu.PrefetchScalarGridSpec(
                num_scalar_prefetch=scalars,
                in_specs=[vmem] * (len(operands) - scalars),
                out_specs=jax.tree.map(lambda _: vmem, out_shape),
                scratch_shapes=list(scratch),
            ),
            compiler_params=pltpu.CompilerParams(vmem_limit_bytes=48 << 20),
        )(*operands)

    return call


def gather_ring(own, other):
    count = lax.axis_size("tensor")
    up = [(i, (i + 1) % count) for i in range(count)]
    down = [(i, (i - 1) % count) for i in range(count)]
    own_list = [own, lax.ppermute(own, "tensor", up)]
    own_last = lax.ppermute(own, "tensor", down)
    other_list = [other, lax.ppermute(other, "tensor", up)]
    other_last = lax.ppermute(other, "tensor", down)
    own_list += [lax.ppermute(own_list[1], "tensor", up), own_last]
    other_list += [lax.ppermute(other_last, "tensor", down), other_last]
    return own_list, other_list


def per_device(
    layer_input,
    queries,
    key_states,
    value_states,
    out_grad,
    log_sums,
    grad_dots,
    doc_stretches,
    stretch_order,
    sign_vector,
    exponents,
):
    context = ("y", "core")
    low = jnp.bfloat16
    tokens = queries.shape[2]
    slots = tokens // BLK
    groups = lax.axis_size(context)
    lines = lax.axis_size("y")
    replicas = lax.axis_size("dp")
    order_row = stretch_order[0]
    where = lax.axis_index(context)
    core = lax.axis_index("core")

    packed = prefetched(pack_kernel, 3, jax.ShapeDtypeStruct((groups, ROWS, HD), low))(
        order_row,
        where.reshape(1),
        exponents[0],
        queries[0],
        out_grad[0],
        key_states[0, 0],
        value_states[0, 0],
        log_sums[0],
        grad_dots[0],
        sign_vector,
    )
    packed, layer_input = lax.optimization_barrier((packed, layer_input))
    recv = lax.all_to_all(packed, context, split_axis=0, concat_axis=0, tiled=True)

    half = layer_input.shape[2] // CORES
    turned = jax.ShapeDtypeStruct((half, tokens), low)
    own_input, other_input = prefetched(turn_kernel, 1, (turned, turned))(
        core.reshape(1), layer_input[0]
    )
    swap = [(0, 1), (1, 0)]
    other_input = lax.ppermute(other_input, "core", swap)
    own_list, other_list = gather_ring(own_input, other_input)

    order_grid = order_row.reshape(groups, slots)
    chunk_ids = (where - jnp.arange(SPAN, dtype=jnp.int32))[:, None, None]
    slot_map = jnp.sum(
        jnp.where(order_grid[None] // slots == chunk_ids, order_grid[None] % slots, 0), axis=2
    )
    ends = jnp.cumsum(doc_stretches[0])
    chunk_units = tokens // PAD
    unit_ids = where * chunk_units + jnp.arange(chunk_units, dtype=jnp.int32)
    doc_start = jnp.max(jnp.where(ends[None, :] <= unit_ids[:, None], ends[None, :], 0), axis=1)
    starts = doc_start - (where - (SPAN - 1)) * chunk_units

    window = SPAN * tokens
    partial_grads = prefetched(
        attend_kernel,
        2,
        jax.ShapeDtypeStruct((groups, SPAN, 2 * BLK, HD), low),
        scratch=(
            pltpu.VMEM((slots * QROWS, HD), low),
            pltpu.VMEM((slots * QROWS, HD), low),
            pltpu.VMEM((HD, slots * QROWS), low),
            pltpu.VMEM((HD, slots * QROWS), low),
            pltpu.VMEM((slots, AUX_ROWS, HD), jnp.float32),
            pltpu.VMEM((window, HD), low),
            pltpu.VMEM((window, HD), low),
            pltpu.VMEM((window, HD), jnp.float32),
            pltpu.VMEM((window, HD), jnp.float32),
        ),
    )(slot_map, starts, recv)
    returned = lax.all_to_all(partial_grads, context, split_axis=0, concat_axis=0, tiled=True)
    targets = lax.dynamic_slice_in_dim(order_row, where * slots, slots, 0) // slots
    own_kv = prefetched(collect_kernel, 1, jax.ShapeDtypeStruct((tokens, 2 * HD), low))(
        targets, returned
    )
    other_kv = lax.ppermute(own_kv, "core", swap)

    spread = prefetched(
        product_kernel,
        1,
        jax.ShapeDtypeStruct((replicas, lines, 2, HB // replicas, 2 * HD), low),
    )(
        jnp.stack([core, lax.axis_index("tensor")]),
        *own_list,
        *other_list,
        own_kv,
        other_kv,
        hadamard_signs(HB),
        recv[:, AUX_AT:ROWS],
    )
    spread = spread.reshape(replicas * lines, 2, HB // replicas, 2 * HD)
    shares = lax.all_to_all(spread, ("dp", "y"), split_axis=0, concat_axis=0, tiled=True)
    return jnp.sum(shares.astype(jnp.float32), axis=0)


def solution(mesh):
    replicas, groups, widths = mesh.devices.shape
    split = Mesh(
        mesh.devices.reshape(replicas, groups // CORES, CORES, widths),
        ("dp", "y", "core", "tensor"),
    )
    context = ("y", "core")
    return jax.shard_map(
        per_device,
        mesh=split,
        in_specs=(
            P("dp", context, "tensor"),
            P("dp", "tensor", context, None),
            P("dp", "tensor", context, None),
            P("dp", "tensor", context, None),
            P("dp", "tensor", context, None),
            P("dp", "tensor", context),
            P("dp", "tensor", context),
            P("dp", None),
            P("dp", None),
            P(context, None),
            P("dp", context),
        ),
        out_specs=P(context, "dp", "tensor"),
        check_vma=False,
    )
```

```python
import jax
import jax.numpy as jnp
from jax import lax
from jax.experimental import pallas as pl
from jax.experimental.pallas import tpu as pltpu
from jax.sharding import Mesh
from jax.sharding import PartitionSpec as P

HD = 128
GROUP = 4
BLK = 32
PAD = 128
HB = 128
CORES = 2
SPAN = 3
LOG2E = 1.4426950408889634

QROWS = GROUP * BLK
KV_AT = 2 * QROWS
AUX_AT = KV_AT + SPAN * 2 * BLK
AUX_ROWS = 16
ROWS = AUX_AT + AUX_ROWS
UNIT_BLKS = PAD // BLK


def hadamard_signs(table_size):
    index_row = jnp.arange(table_size, dtype=jnp.int32)
    common = jnp.bitwise_and(index_row[:, None], index_row[None, :])
    parity = jnp.zeros((table_size, table_size), jnp.int32)
    for bit_pos in range(table_size.bit_length() - 1):
        parity = parity + jnp.bitwise_and(jnp.right_shift(common, bit_pos), 1)
    return (1 - 2 * jnp.bitwise_and(parity, 1)).astype(jnp.bfloat16)


def pack_kernel(where_ref, *refs):
    (query_ref, grad_ref, key_ref, value_ref, lse_ref, dots_ref, sign_ref), refs = refs[:7], refs[7:]
    order_ref, exponent_ref, out_ref = refs[:3]
    query_scr, grad_scr, key_scr, value_scr, lse_scr, dots_scr, sign_scr = refs[3:10]
    order_scr, exponent_scr, held_scr, aux_scr, packed_scr, in_sem, out_sem = refs[10:]
    sources = (order_ref, exponent_ref, lse_ref, dots_ref, sign_ref)
    sources += (key_ref, value_ref, query_ref, grad_ref)
    places = (order_scr, exponent_scr, lse_scr, dots_scr, sign_scr)
    places += (key_scr, value_scr, query_scr, grad_scr)
    loads = [
        pltpu.make_async_copy(source, place, in_sem.at[i])
        for i, (source, place) in enumerate(zip(sources, places))
    ]
    for load in loads:
        load.start()
    groups = out_ref.shape[0]
    slots = key_ref.shape[2] // BLK
    for load in loads[:5]:
        load.wait()
    first = where_ref[0] * slots
    for slot in range(slots):
        held_scr[order_scr[0, first + slot] // slots] = slot

    fixed = [sign_scr[...].astype(jnp.float32)]
    for blk in range(sign_ref.shape[0]):
        power = jnp.full((1, HD), jnp.left_shift(jnp.int32(1), exponent_scr[0, blk]), jnp.int32)
        fixed.append(1.0 / power.astype(jnp.float32))
    fixed.append(jnp.zeros((AUX_ROWS - 6, HD), jnp.float32))
    head_of = lax.broadcasted_iota(jnp.int32, (1, HD), 1) // BLK
    stats = (lse_scr[0].astype(jnp.float32), dots_scr[0].astype(jnp.float32))

    def by_head(array, slot):
        part = slot * BLK // HD * HD
        inner = slot % (HD // BLK)
        row = jnp.zeros((1, HD), jnp.float32)
        for head in range(GROUP):
            line = array[head : head + 1, part : part + HD]
            turn = (head - inner) * BLK % HD
            line = pltpu.roll(line, turn, 1) if turn else line
            row = jnp.where(head_of == head, line, row)
        return row

    for slot in range(slots):
        aux = jnp.concatenate([by_head(array, slot) for array in stats] + fixed, axis=0)
        aux_scr[slot] = aux.astype(aux_scr.dtype)
    for load in loads[5:]:
        load.wait()

    stores = []
    for dest in range(groups):
        slot = held_scr[dest]
        rows = pl.ds(pl.multiple_of(slot * BLK, BLK), BLK)
        for head in range(GROUP):
            packed_scr[dest, head * BLK : (head + 1) * BLK, :] = query_scr[0, head, rows, :]
            at = QROWS + head * BLK
            packed_scr[dest, at : at + BLK, :] = grad_scr[0, head, rows, :]
        for span in range(SPAN):
            at = KV_AT + span * 2 * BLK
            if dest >= span:
                rows = pl.ds(pl.multiple_of(held_scr[dest - span] * BLK, BLK), BLK)
                packed_scr[dest, at : at + BLK, :] = key_scr[0, 0, rows, :]
                packed_scr[dest, at + BLK : at + 2 * BLK, :] = value_scr[0, 0, rows, :]
            else:
                packed_scr[dest, at : at + 2 * BLK, :] = jnp.zeros((2 * BLK, HD), out_ref.dtype)
        packed_scr[dest, AUX_AT:ROWS, :] = aux_scr[slot]
        stores.append(pltpu.make_async_copy(packed_scr.at[dest], out_ref.at[dest], out_sem.at[dest]))
        stores[-1].start()
    for store in stores:
        store.wait()


def attend_kernel(
    slot_ref, start_ref, recv_ref, out_ref,
    query_scr, grad_scr, query_turned, grad_turned, stat_scr,
    key_scr, value_scr, dkey_scr, dvalue_scr,
):
    groups = recv_ref.shape[0]
    chunk = key_scr.shape[0] // SPAN
    units = chunk // PAD
    width = UNIT_BLKS * QROWS
    pair = 2 * PAD
    dkey_scr[...] = jnp.zeros_like(dkey_scr)
    dvalue_scr[...] = jnp.zeros_like(dvalue_scr)
    for src in range(groups):
        slot = slot_ref[0, src]
        at = pl.multiple_of(slot * QROWS, QROWS)
        query_blk = recv_ref[src, 0:QROWS, :]
        grad_blk = recv_ref[src, QROWS : 2 * QROWS, :]
        query_scr[pl.ds(at, QROWS), :] = query_blk
        grad_scr[pl.ds(at, QROWS), :] = grad_blk
        query_turned[:, pl.ds(at, QROWS)] = query_blk.T
        grad_turned[:, pl.ds(at, QROWS)] = grad_blk.T
        stat_scr[slot] = recv_ref[src, AUX_AT:ROWS, :].astype(jnp.float32)
        for span in range(SPAN):
            row = (SPAN - 1 - span) * chunk + slot_ref[span, src] * BLK
            row = pl.multiple_of(row, BLK)
            at = KV_AT + span * 2 * BLK
            key_scr[pl.ds(row, BLK), :] = recv_ref[src, at : at + BLK, :]
            value_scr[pl.ds(row, BLK), :] = recv_ref[src, at + BLK : at + 2 * BLK, :]

    scale = HD ** (-0.5)
    key_at = lax.broadcasted_iota(jnp.int32, (pair, width), 0)
    column = lax.broadcasted_iota(jnp.int32, (pair, width), 1)
    query_at = (column // QROWS) * BLK + column % BLK
    causal = key_at - PAD <= query_at

    for unit in range(units):
        cols = slice(unit * width, (unit + 1) * width)
        blocks = range(unit * UNIT_BLKS, (unit + 1) * UNIT_BLKS)
        lse = jnp.concatenate([stat_scr[b, 0:1, :] for b in blocks], axis=1) * LOG2E
        dots = jnp.concatenate([stat_scr[b, 1:2, :] for b in blocks], axis=1)

        def visit(row, live):
            rows = pl.ds(row, pair)
            scores = jnp.dot(
                key_scr[rows, :], query_turned[:, cols], preferred_element_type=jnp.float32
            )
            dprobs = jnp.dot(
                value_scr[rows, :], grad_turned[:, cols], preferred_element_type=jnp.float32
            )
            probs = jnp.where(live, jnp.exp2(scores * (scale * LOG2E) - lse), 0.0)
            dscores = (probs * (dprobs - dots)).astype(jnp.bfloat16)
            dvalue_scr[rows, :] += jnp.dot(
                probs.astype(jnp.bfloat16), grad_scr[cols, :], preferred_element_type=jnp.float32
            )
            dkey_scr[rows, :] += jnp.dot(
                dscores, query_scr[cols, :], preferred_element_type=jnp.float32
            )

        first = start_ref[unit]
        last = (SPAN - 1) * units + unit
        visit((last - 1) * PAD, causal & (key_at >= (first - (last - 1)) * PAD))

        @pl.loop(1, (last - first + 2) // 2)
        def _(step):
            base = last - 1 - 2 * step
            visit(pl.multiple_of(base * PAD, PAD), key_at >= (first - base) * PAD)

    for src in range(groups):
        for span in range(SPAN):
            row = (SPAN - 1 - span) * chunk + slot_ref[span, src] * BLK
            row = pl.multiple_of(row, BLK)
            dkey = dkey_scr[pl.ds(row, BLK), :] * scale
            out_ref[src, span, 0:BLK, :] = dkey.astype(out_ref.dtype)
            out_ref[src, span, BLK : 2 * BLK, :] = dvalue_scr[pl.ds(row, BLK), :].astype(
                out_ref.dtype
            )


def collect_kernel(target_ref, recv_ref, out_ref):
    groups = recv_ref.shape[0]
    for slot in range(out_ref.shape[0] // BLK):
        owner = target_ref[slot]
        total = recv_ref[owner, 0].astype(jnp.float32)
        for span in range(1, SPAN):
            extra = recv_ref[jnp.minimum(owner + span, groups - 1), span].astype(jnp.float32)
            total = total + jnp.where(owner + span < groups, extra, 0.0)
        rows = slice(slot * BLK, (slot + 1) * BLK)
        total = total.astype(out_ref.dtype)
        out_ref[rows, 0:HD] = total[0:BLK]
        out_ref[rows, HD : 2 * HD] = total[BLK : 2 * BLK]


def turn_kernel(core_ref, input_ref, own_ref, other_ref):
    span = 2 * HB
    core = core_ref[0]
    for part in range(own_ref.shape[0] // span):
        rows = slice(part * span, (part + 1) * span)
        at = pl.multiple_of((CORES * part + core) * span, span)
        own_ref[rows, :] = input_ref[:, pl.ds(at, span)].T
        at = pl.multiple_of((CORES * part + 1 - core) * span, span)
        other_ref[rows, :] = input_ref[:, pl.ds(at, span)].T


def load_all(sources, places, sems):
    loads = [
        pltpu.make_async_copy(source, places.at[i], sems.at[i]) for i, source in enumerate(sources)
    ]
    for load in loads:
        load.start()
    return loads


def first_product_kernel(*refs):
    kv_ref, out_ref, input_scr, sems = refs[-4:]
    for step, load in enumerate(load_all(refs[:-4], input_scr, sems)):
        load.wait()
        out_ref[step] = jnp.dot(input_scr[step], kv_ref[...], preferred_element_type=jnp.float32)


def product_kernel(where_ref, *refs):
    other_refs = refs[:-7]
    first_ref, kv_ref, had_ref, aux_ref, out_ref, input_scr, sems = refs[-7:]
    loads = load_all(other_refs, input_scr, sems)
    core, width = where_ref[0], where_ref[1]
    replicas = out_ref.shape[0]
    span = 2 * HB
    parts = input_scr.shape[1] // span
    had = jnp.concatenate([had_ref[...].astype(jnp.float32)] * 2, axis=1)
    for step, load in enumerate(loads):
        source = (width + len(loads) - step) % len(loads)
        load.wait()
        grad = jnp.dot(input_scr[step], kv_ref[...], preferred_element_type=jnp.float32)
        grad = grad + first_ref[step]
        for part in range(parts):
            line = source * parts + part
            aux = aux_ref[CORES * line + core].astype(jnp.float32)
            for blk in range(2):
                at = part * span + blk * HB
                rows = grad[at : at + HB]
                sign = aux[2 + blk : 3 + blk, :]
                table = (had * jnp.concatenate([sign, sign], axis=1)).astype(jnp.bfloat16)
                high = rows.astype(jnp.bfloat16)
                low = (rows - high.astype(jnp.float32)).astype(jnp.bfloat16)
                both = jnp.concatenate([high, low], axis=0)
                rotated = jnp.dot(table, both, preferred_element_type=jnp.float32)
                factor = aux[4 + blk : 5 + blk, :] * (HB ** (-0.5))
                rotated *= jnp.concatenate([factor] * (rows.shape[1] // HB), axis=1)
                out_ref[:, line, blk] = rotated.astype(out_ref.dtype).reshape(
                    replicas, HB // replicas, rows.shape[1]
                )


def prefetched(kernel, scalars, out_shape, scratch=(), in_place=0, out_space=pltpu.VMEM):
    vmem = pl.BlockSpec(memory_space=pltpu.VMEM)
    hbm = pl.BlockSpec(memory_space=pltpu.HBM)
    out_spec = pl.BlockSpec(memory_space=out_space)

    def call(*operands):
        held = scalars + in_place
        kept = [
            pltpu.with_memory_space_constraint(array, pltpu.HBM)
            for array in operands[scalars:held]
        ]
        return pl.pallas_call(
            kernel,
            out_shape=out_shape,
            grid_spec=pltpu.PrefetchScalarGridSpec(
                num_scalar_prefetch=scalars,
                in_specs=[hbm] * in_place + [vmem] * (len(operands) - held),
                out_specs=jax.tree.map(lambda _: out_spec, out_shape),
                scratch_shapes=list(scratch),
            ),
            compiler_params=pltpu.CompilerParams(vmem_limit_bytes=16 << 20),
        )(*operands[:scalars], *kept, *operands[held:])

    return call


def gather_ring(own, other):
    count = lax.axis_size("tensor")
    up = [(i, (i + 1) % count) for i in range(count)]
    down = [(i, (i - 1) % count) for i in range(count)]
    own_list = [own, lax.ppermute(own, "tensor", up)]
    own_last = lax.ppermute(own, "tensor", down)
    other_list = [other, lax.ppermute(other, "tensor", up)]
    other_last = lax.ppermute(other, "tensor", down)
    own_list += [lax.ppermute(own_list[1], "tensor", up), own_last]
    other_list += [lax.ppermute(other_last, "tensor", down), other_last]
    return own_list, other_list


def per_device(
    layer_input,
    queries,
    key_states,
    value_states,
    out_grad,
    log_sums,
    grad_dots,
    doc_stretches,
    stretch_order,
    sign_vector,
    exponents,
):
    context = ("y", "core")
    low = jnp.bfloat16
    tokens = queries.shape[2]
    slots = tokens // BLK
    groups = lax.axis_size(context)
    lines = lax.axis_size("y")
    replicas = lax.axis_size("dp")
    order_row = stretch_order[0]
    where = lax.axis_index(context)
    core = lax.axis_index("core")

    raw = (queries, out_grad, key_states, value_states, log_sums, grad_dots, sign_vector)
    packed = prefetched(
        pack_kernel,
        1,
        pltpu.HBM((groups, ROWS, HD), low),
        scratch=(
            *(pltpu.VMEM(array.shape, array.dtype) for array in raw),
            pltpu.SMEM(stretch_order.shape, jnp.int32),
            pltpu.SMEM(exponents.shape, jnp.int32),
            pltpu.SMEM((groups,), jnp.int32),
            pltpu.VMEM((slots, AUX_ROWS, HD), low),
            pltpu.VMEM((groups, ROWS, HD), low),
            pltpu.SemaphoreType.DMA((9,)),
            pltpu.SemaphoreType.DMA((groups,)),
        ),
        in_place=len(raw) + 2,
        out_space=pltpu.HBM,
    )(where.reshape(1), *raw, stretch_order, exponents)
    packed, layer_input = lax.optimization_barrier((packed, layer_input))
    recv = lax.all_to_all(packed, context, split_axis=0, concat_axis=0, tiled=True)

    half = layer_input.shape[2] // CORES
    turned = jax.ShapeDtypeStruct((half, tokens), low)
    own_input, other_input = prefetched(turn_kernel, 1, (turned, turned))(
        core.reshape(1), layer_input[0]
    )
    swap = [(0, 1), (1, 0)]
    other_input = lax.ppermute(other_input, "core", swap)
    own_list, other_list = gather_ring(own_input, other_input)
    recv, own_list, other_list = lax.optimization_barrier((recv, own_list, other_list))

    order_grid = order_row.reshape(groups, slots)
    chunk_ids = (where - jnp.arange(SPAN, dtype=jnp.int32))[:, None, None]
    slot_map = jnp.sum(
        jnp.where(order_grid[None] // slots == chunk_ids, order_grid[None] % slots, 0), axis=2
    )
    ends = jnp.cumsum(doc_stretches[0])
    chunk_units = tokens // PAD
    unit_ids = where * chunk_units + jnp.arange(chunk_units, dtype=jnp.int32)
    doc_start = jnp.max(jnp.where(ends[None, :] <= unit_ids[:, None], ends[None, :], 0), axis=1)
    starts = doc_start - (where - (SPAN - 1)) * chunk_units

    window = SPAN * tokens
    partial_grads = prefetched(
        attend_kernel,
        2,
        jax.ShapeDtypeStruct((groups, SPAN, 2 * BLK, HD), low),
        scratch=(
            pltpu.VMEM((slots * QROWS, HD), low),
            pltpu.VMEM((slots * QROWS, HD), low),
            pltpu.VMEM((HD, slots * QROWS), low),
            pltpu.VMEM((HD, slots * QROWS), low),
            pltpu.VMEM((slots, AUX_ROWS, HD), jnp.float32),
            pltpu.VMEM((window, HD), low),
            pltpu.VMEM((window, HD), low),
            pltpu.VMEM((window, HD), jnp.float32),
            pltpu.VMEM((window, HD), jnp.float32),
        ),
    )(slot_map, starts, recv)
    returned = lax.all_to_all(partial_grads, context, split_axis=0, concat_axis=0, tiled=True)
    targets = lax.dynamic_slice_in_dim(order_row, where * slots, slots, 0) // slots
    own_kv = prefetched(collect_kernel, 1, jax.ShapeDtypeStruct((tokens, 2 * HD), low))(
        targets, returned
    )
    other_kv = lax.ppermute(own_kv, "core", swap)

    input_scratch = (
        pltpu.VMEM((len(own_list), half, tokens), low),
        pltpu.SemaphoreType.DMA((len(own_list),)),
    )
    first_product = prefetched(
        first_product_kernel,
        0,
        jax.ShapeDtypeStruct((len(own_list), half, 2 * HD), jnp.float32),
        scratch=input_scratch,
        in_place=len(own_list),
    )(*own_list, own_kv)
    spread = prefetched(
        product_kernel,
        1,
        jax.ShapeDtypeStruct((replicas, lines, 2, HB // replicas, 2 * HD), low),
        scratch=input_scratch,
        in_place=len(other_list),
    )(
        jnp.stack([core, lax.axis_index("tensor")]),
        *other_list,
        first_product,
        other_kv,
        hadamard_signs(HB),
        recv[:, AUX_AT:ROWS],
    )
    spread = spread.reshape(replicas * lines, 2, HB // replicas, 2 * HD)
    shares = lax.all_to_all(spread, ("dp", "y"), split_axis=0, concat_axis=0, tiled=True)
    return jnp.sum(shares.astype(jnp.float32), axis=0)


def solution(mesh):
    replicas, groups, widths = mesh.devices.shape
    split = Mesh(
        mesh.devices.reshape(replicas, groups // CORES, CORES, widths),
        ("dp", "y", "core", "tensor"),
    )
    context = ("y", "core")
    return jax.shard_map(
        per_device,
        mesh=split,
        in_specs=(
            P("dp", context, "tensor"),
            P("dp", "tensor", context, None),
            P("dp", "tensor", context, None),
            P("dp", "tensor", context, None),
            P("dp", "tensor", context, None),
            P("dp", "tensor", context),
            P("dp", "tensor", context),
            P("dp", None),
            P("dp", None),
            P(context, None),
            P("dp", context),
        ),
        out_specs=P(context, "dp", "tensor"),
        check_vma=False,
    )
```

```python
import jax
import jax.numpy as jnp
from jax import lax
from jax.experimental import pallas as pl
from jax.experimental.pallas import tpu as pltpu
from jax.sharding import Mesh
from jax.sharding import PartitionSpec as P

HD = 128
GROUP = 4
BLK = 32
PAD = 128
HB = 128
CORES = 2
SPAN = 3
LOG2E = 1.4426950408889634

QROWS = GROUP * BLK
KV_AT = 2 * QROWS
AUX_AT = KV_AT + 2 * BLK
AUX_ROWS = 16
ROWS = AUX_AT + AUX_ROWS
UNIT_BLKS = PAD // BLK


def hadamard_signs(table_size):
    index_row = jnp.arange(table_size, dtype=jnp.int32)
    common = jnp.bitwise_and(index_row[:, None], index_row[None, :])
    parity = jnp.zeros((table_size, table_size), jnp.int32)
    for bit_pos in range(table_size.bit_length() - 1):
        parity = parity + jnp.bitwise_and(jnp.right_shift(common, bit_pos), 1)
    return (1 - 2 * jnp.bitwise_and(parity, 1)).astype(jnp.bfloat16)


def pack_kernel(where_ref, *refs):
    (query_ref, grad_ref, key_ref, value_ref, lse_ref, dots_ref, sign_ref), refs = refs[:7], refs[7:]
    order_ref, exponent_ref, out_ref = refs[:3]
    query_scr, grad_scr, key_scr, value_scr, lse_scr, dots_scr, sign_scr = refs[3:10]
    order_scr, exponent_scr, held_scr, aux_scr, packed_scr, in_sem, out_sem = refs[10:]
    sources = (order_ref, exponent_ref, lse_ref, dots_ref, sign_ref)
    sources += (key_ref, value_ref, query_ref, grad_ref)
    places = (order_scr, exponent_scr, lse_scr, dots_scr, sign_scr)
    places += (key_scr, value_scr, query_scr, grad_scr)
    loads = [
        pltpu.make_async_copy(source, place, in_sem.at[i])
        for i, (source, place) in enumerate(zip(sources, places))
    ]
    for load in loads:
        load.start()
    groups = out_ref.shape[0]
    slots = key_ref.shape[2] // BLK
    for load in loads[:5]:
        load.wait()
    first = where_ref[0] * slots
    for slot in range(slots):
        held_scr[order_scr[0, first + slot] // slots] = slot

    fixed = [sign_scr[...].astype(jnp.float32)]
    for blk in range(sign_ref.shape[0]):
        power = jnp.full((1, HD), jnp.left_shift(jnp.int32(1), exponent_scr[0, blk]), jnp.int32)
        fixed.append(1.0 / power.astype(jnp.float32))
    fixed.append(jnp.zeros((AUX_ROWS - 6, HD), jnp.float32))
    head_of = lax.broadcasted_iota(jnp.int32, (1, HD), 1) // BLK
    stats = (lse_scr[0].astype(jnp.float32), dots_scr[0].astype(jnp.float32))

    def by_head(array, slot):
        part = slot * BLK // HD * HD
        inner = slot % (HD // BLK)
        row = jnp.zeros((1, HD), jnp.float32)
        for head in range(GROUP):
            line = array[head : head + 1, part : part + HD]
            turn = (head - inner) * BLK % HD
            line = pltpu.roll(line, turn, 1) if turn else line
            row = jnp.where(head_of == head, line, row)
        return row

    for slot in range(slots):
        aux = jnp.concatenate([by_head(array, slot) for array in stats] + fixed, axis=0)
        aux_scr[slot] = aux.astype(aux_scr.dtype)
    for load in loads[5:]:
        load.wait()

    stores = []
    for dest in range(groups):
        slot = held_scr[dest]
        rows = pl.ds(pl.multiple_of(slot * BLK, BLK), BLK)
        for head in range(GROUP):
            packed_scr[dest, head * BLK : (head + 1) * BLK, :] = query_scr[0, head, rows, :]
            at = QROWS + head * BLK
            packed_scr[dest, at : at + BLK, :] = grad_scr[0, head, rows, :]
        packed_scr[dest, KV_AT : KV_AT + BLK, :] = key_scr[0, 0, rows, :]
        packed_scr[dest, KV_AT + BLK : AUX_AT, :] = value_scr[0, 0, rows, :]
        packed_scr[dest, AUX_AT:ROWS, :] = aux_scr[slot]
        stores.append(pltpu.make_async_copy(packed_scr.at[dest], out_ref.at[dest], out_sem.at[dest]))
        stores[-1].start()
    for store in stores:
        store.wait()


def pair_grads(key_blk, value_blk, query_refs, cols, lse, dots, live):
    query_ref, grad_ref, query_turned, grad_turned = query_refs
    scores = jnp.dot(key_blk, query_turned[:, cols], preferred_element_type=jnp.float32)
    dprobs = jnp.dot(value_blk, grad_turned[:, cols], preferred_element_type=jnp.float32)
    probs = jnp.where(live, jnp.exp2(scores * (HD ** (-0.5) * LOG2E) - lse), 0.0)
    dscores = (probs * (dprobs - dots)).astype(jnp.bfloat16)
    value_part = jnp.dot(
        probs.astype(jnp.bfloat16), grad_ref[cols, :], preferred_element_type=jnp.float32
    )
    key_part = jnp.dot(dscores, query_ref[cols, :], preferred_element_type=jnp.float32)
    return key_part, value_part


def unit_stats(stat_ref, unit):
    blocks = range(unit * UNIT_BLKS, (unit + 1) * UNIT_BLKS)
    lse = jnp.concatenate([stat_ref[b, 0:1, :] for b in blocks], axis=1) * LOG2E
    dots = jnp.concatenate([stat_ref[b, 1:2, :] for b in blocks], axis=1)
    return lse, dots


def own_attend_kernel(
    slot_ref, start_ref, recv_ref,
    query_ref, grad_ref, query_turned, grad_turned, stat_ref, out_ref,
    key_scr, value_scr, dkey_scr, dvalue_scr,
):
    groups = recv_ref.shape[0]
    units = key_scr.shape[0] // PAD
    width = UNIT_BLKS * QROWS
    for src in range(groups):
        slot = slot_ref[0, src]
        at = pl.multiple_of(slot * QROWS, QROWS)
        query_blk = recv_ref[src, 0:QROWS, :]
        grad_blk = recv_ref[src, QROWS : 2 * QROWS, :]
        query_ref[pl.ds(at, QROWS), :] = query_blk
        grad_ref[pl.ds(at, QROWS), :] = grad_blk
        query_turned[:, pl.ds(at, QROWS)] = query_blk.T
        grad_turned[:, pl.ds(at, QROWS)] = grad_blk.T
        stat_ref[slot] = recv_ref[src, AUX_AT:ROWS, :].astype(jnp.float32)
        row = pl.multiple_of(slot * BLK, BLK)
        key_scr[pl.ds(row, BLK), :] = recv_ref[src, KV_AT : KV_AT + BLK, :]
        value_scr[pl.ds(row, BLK), :] = recv_ref[src, KV_AT + BLK : AUX_AT, :]

    queries = (query_ref, grad_ref, query_turned, grad_turned)
    dkey_scr[...] = jnp.zeros_like(dkey_scr)
    dvalue_scr[...] = jnp.zeros_like(dvalue_scr)
    for unit in range(units):
        rows = slice(0, (unit + 1) * PAD)
        cols = slice(unit * width, (unit + 1) * width)
        lse, dots = unit_stats(stat_ref, unit)
        key_at = lax.broadcasted_iota(jnp.int32, (rows.stop, width), 0)
        column = lax.broadcasted_iota(jnp.int32, (rows.stop, width), 1)
        query_at = unit * PAD + (column // QROWS) * BLK + column % BLK
        first = (start_ref[unit] - (SPAN - 1) * units) * PAD
        live = (key_at <= query_at) & (key_at >= first)
        key_part, value_part = pair_grads(
            key_scr[rows, :], value_scr[rows, :], queries, cols, lse, dots, live
        )
        dkey_scr[rows, :] += key_part
        dvalue_scr[rows, :] += value_part

    for src in range(groups):
        rows = pl.ds(pl.multiple_of(slot_ref[0, src] * BLK, BLK), BLK)
        dkey = dkey_scr[rows, :] * HD ** (-0.5)
        out_ref[src, 0:BLK, :] = dkey.astype(out_ref.dtype)
        out_ref[src, BLK : 2 * BLK, :] = dvalue_scr[rows, :].astype(out_ref.dtype)


def earlier_attend_kernel(slot_ref, start_ref, *refs):
    earlier_refs, refs = refs[: SPAN - 1], refs[SPAN - 1 :]
    query_ref, grad_ref, query_turned, grad_turned, stat_ref, own_ref, out_ref = refs[:7]
    key_scr, value_scr, dkey_scr, dvalue_scr = refs[7:]
    groups = out_ref.shape[0]
    chunk = key_scr.shape[0] // (SPAN - 1)
    units = chunk // PAD
    width = UNIT_BLKS * QROWS
    pair = 2 * PAD
    edge = (SPAN - 1) * units

    def rows_of(span, src):
        row = (SPAN - 1 - span) * chunk + slot_ref[span, src] * BLK
        return pl.ds(pl.multiple_of(row, BLK), BLK)

    for src in range(groups):
        for span in range(1, SPAN):
            rows = rows_of(span, src)
            key_scr[rows, :] = earlier_refs[span - 1][src, 0:BLK, :]
            value_scr[rows, :] = earlier_refs[span - 1][src, BLK : 2 * BLK, :]
    dkey_scr[...] = jnp.zeros_like(dkey_scr)
    dvalue_scr[...] = jnp.zeros_like(dvalue_scr)
    queries = (query_ref, grad_ref, query_turned, grad_turned)
    key_at = lax.broadcasted_iota(jnp.int32, (pair, width), 0)
    for unit in range(units):
        cols = slice(unit * width, (unit + 1) * width)
        lse, dots = unit_stats(stat_ref, unit)
        first = jnp.minimum(start_ref[unit], edge)

        @pl.loop(0, (edge - first + 1) // 2)
        def _(step):
            base = edge - 2 - 2 * step
            rows = pl.ds(pl.multiple_of(base * PAD, pair), pair)
            key_part, value_part = pair_grads(
                key_scr[rows, :],
                value_scr[rows, :],
                queries,
                cols,
                lse,
                dots,
                key_at >= (first - base) * PAD,
            )
            dkey_scr[rows, :] += key_part
            dvalue_scr[rows, :] += value_part

    for src in range(groups):
        out_ref[src, 0] = own_ref[src]
        for span in range(1, SPAN):
            rows = rows_of(span, src)
            dkey = dkey_scr[rows, :] * HD ** (-0.5)
            out_ref[src, span, 0:BLK, :] = dkey.astype(out_ref.dtype)
            out_ref[src, span, BLK : 2 * BLK, :] = dvalue_scr[rows, :].astype(out_ref.dtype)


def collect_kernel(target_ref, recv_ref, out_ref):
    groups = recv_ref.shape[0]
    for slot in range(out_ref.shape[0] // BLK):
        owner = target_ref[slot]
        total = recv_ref[owner, 0].astype(jnp.float32)
        for span in range(1, SPAN):
            extra = recv_ref[jnp.minimum(owner + span, groups - 1), span].astype(jnp.float32)
            total = total + jnp.where(owner + span < groups, extra, 0.0)
        rows = slice(slot * BLK, (slot + 1) * BLK)
        total = total.astype(out_ref.dtype)
        out_ref[rows, 0:HD] = total[0:BLK]
        out_ref[rows, HD : 2 * HD] = total[BLK : 2 * BLK]


def turn_kernel(core_ref, input_ref, own_ref, other_ref):
    span = 2 * HB
    core = core_ref[0]
    for part in range(own_ref.shape[0] // span):
        rows = slice(part * span, (part + 1) * span)
        at = pl.multiple_of((CORES * part + core) * span, span)
        own_ref[rows, :] = input_ref[:, pl.ds(at, span)].T
        at = pl.multiple_of((CORES * part + 1 - core) * span, span)
        other_ref[rows, :] = input_ref[:, pl.ds(at, span)].T


def load_all(sources, places, sems):
    loads = [
        pltpu.make_async_copy(source, places.at[i], sems.at[i]) for i, source in enumerate(sources)
    ]
    for load in loads:
        load.start()
    return loads


def first_product_kernel(*refs):
    kv_ref, out_ref, input_scr, sems = refs[-4:]
    for step, load in enumerate(load_all(refs[:-4], input_scr, sems)):
        load.wait()
        out_ref[step] = jnp.dot(input_scr[step], kv_ref[...], preferred_element_type=jnp.float32)


def product_kernel(where_ref, *refs):
    other_refs = refs[:-7]
    first_ref, kv_ref, had_ref, aux_ref, out_ref, input_scr, sems = refs[-7:]
    loads = load_all(other_refs, input_scr, sems)
    core, width = where_ref[0], where_ref[1]
    replicas = out_ref.shape[0]
    span = 2 * HB
    parts = input_scr.shape[1] // span
    had = jnp.concatenate([had_ref[...].astype(jnp.float32)] * 2, axis=1)
    for step, load in enumerate(loads):
        source = (width + len(loads) - step) % len(loads)
        load.wait()
        grad = jnp.dot(input_scr[step], kv_ref[...], preferred_element_type=jnp.float32)
        grad = grad + first_ref[step]
        for part in range(parts):
            line = source * parts + part
            aux = aux_ref[CORES * line + core].astype(jnp.float32)
            for blk in range(2):
                at = part * span + blk * HB
                rows = grad[at : at + HB]
                sign = aux[2 + blk : 3 + blk, :]
                table = (had * jnp.concatenate([sign, sign], axis=1)).astype(jnp.bfloat16)
                high = rows.astype(jnp.bfloat16)
                low = (rows - high.astype(jnp.float32)).astype(jnp.bfloat16)
                both = jnp.concatenate([high, low], axis=0)
                rotated = jnp.dot(table, both, preferred_element_type=jnp.float32)
                factor = aux[4 + blk : 5 + blk, :] * (HB ** (-0.5))
                rotated *= jnp.concatenate([factor] * (rows.shape[1] // HB), axis=1)
                out_ref[:, line, blk] = rotated.astype(out_ref.dtype).reshape(
                    replicas, HB // replicas, rows.shape[1]
                )


def prefetched(kernel, scalars, out_shape, scratch=(), in_place=0, out_space=pltpu.VMEM):
    vmem = pl.BlockSpec(memory_space=pltpu.VMEM)
    hbm = pl.BlockSpec(memory_space=pltpu.HBM)
    out_spec = pl.BlockSpec(memory_space=out_space)

    def call(*operands):
        held = scalars + in_place
        kept = [
            pltpu.with_memory_space_constraint(array, pltpu.HBM)
            for array in operands[scalars:held]
        ]
        return pl.pallas_call(
            kernel,
            out_shape=out_shape,
            grid_spec=pltpu.PrefetchScalarGridSpec(
                num_scalar_prefetch=scalars,
                in_specs=[hbm] * in_place + [vmem] * (len(operands) - held),
                out_specs=jax.tree.map(lambda _: out_spec, out_shape),
                scratch_shapes=list(scratch),
            ),
            compiler_params=pltpu.CompilerParams(vmem_limit_bytes=16 << 20),
        )(*operands[:scalars], *kept, *operands[held:])

    return call


def around(count, step):
    return [(i, (i + step) % count) for i in range(count)]


def onward(count, step):
    return [(i, i + step) for i in range(count - step)]


def per_device(
    layer_input,
    queries,
    key_states,
    value_states,
    out_grad,
    log_sums,
    grad_dots,
    doc_stretches,
    stretch_order,
    sign_vector,
    exponents,
):
    context = ("y", "core")
    low = jnp.bfloat16
    tokens = queries.shape[2]
    slots = tokens // BLK
    groups = lax.axis_size(context)
    lines = lax.axis_size("y")
    replicas = lax.axis_size("dp")
    order_row = stretch_order[0]
    where = lax.axis_index(context)
    core = lax.axis_index("core")

    raw = (queries, out_grad, key_states, value_states, log_sums, grad_dots, sign_vector)
    packed = prefetched(
        pack_kernel,
        1,
        pltpu.HBM((groups, ROWS, HD), low),
        scratch=(
            *(pltpu.VMEM(array.shape, array.dtype) for array in raw),
            pltpu.SMEM(stretch_order.shape, jnp.int32),
            pltpu.SMEM(exponents.shape, jnp.int32),
            pltpu.SMEM((groups,), jnp.int32),
            pltpu.VMEM((slots, AUX_ROWS, HD), low),
            pltpu.VMEM((groups, ROWS, HD), low),
            pltpu.SemaphoreType.DMA((9,)),
            pltpu.SemaphoreType.DMA((groups,)),
        ),
        in_place=len(raw) + 2,
        out_space=pltpu.HBM,
    )(where.reshape(1), *raw, stretch_order, exponents)
    packed, layer_input = lax.optimization_barrier((packed, layer_input))
    recv = lax.all_to_all(packed, context, split_axis=0, concat_axis=0, tiled=True)

    half = layer_input.shape[2] // CORES
    turned = jax.ShapeDtypeStruct((half, tokens), low)
    own_input, other_input = prefetched(turn_kernel, 1, (turned, turned))(
        core.reshape(1), layer_input[0]
    )
    swap = [(0, 1), (1, 0)]
    other_input = lax.ppermute(other_input, "core", swap)
    widths = lax.axis_size("tensor")
    up, down = around(widths, 1), around(widths, -1)
    near = [
        lax.ppermute(array, "tensor", way)
        for array in (own_input, other_input)
        for way in (up, down)
    ]
    recv, near = lax.optimization_barrier((recv, near))
    held = recv[:, KV_AT:AUX_AT]
    earlier = [lax.ppermute(held, context, onward(groups, span)) for span in range(1, SPAN)]

    order_grid = order_row.reshape(groups, slots)
    chunk_ids = (where - jnp.arange(SPAN, dtype=jnp.int32))[:, None, None]
    slot_map = jnp.sum(
        jnp.where(order_grid[None] // slots == chunk_ids, order_grid[None] % slots, 0), axis=2
    )
    ends = jnp.cumsum(doc_stretches[0])
    chunk_units = tokens // PAD
    unit_ids = where * chunk_units + jnp.arange(chunk_units, dtype=jnp.int32)
    doc_start = jnp.max(jnp.where(ends[None, :] <= unit_ids[:, None], ends[None, :], 0), axis=1)
    starts = doc_start - (where - (SPAN - 1)) * chunk_units

    sorted_rows = jax.ShapeDtypeStruct((slots * QROWS, HD), low)
    turned_rows = jax.ShapeDtypeStruct((HD, slots * QROWS), low)
    own_work = prefetched(
        own_attend_kernel,
        2,
        (
            sorted_rows,
            sorted_rows,
            turned_rows,
            turned_rows,
            jax.ShapeDtypeStruct((slots, AUX_ROWS, HD), jnp.float32),
            jax.ShapeDtypeStruct((groups, 2 * BLK, HD), low),
        ),
        scratch=tuple(
            pltpu.VMEM((tokens, HD), dtype) for dtype in (low, low, jnp.float32, jnp.float32)
        ),
    )(slot_map, starts, recv)
    partial_grads = prefetched(
        earlier_attend_kernel,
        2,
        jax.ShapeDtypeStruct((groups, SPAN, 2 * BLK, HD), low),
        scratch=tuple(
            pltpu.VMEM(((SPAN - 1) * tokens, HD), dtype)
            for dtype in (low, low, jnp.float32, jnp.float32)
        ),
    )(slot_map, starts, *earlier, *own_work)
    partial_grads, near = lax.optimization_barrier((partial_grads, near))
    own_up, own_down, other_up, other_down = near
    own_list = [own_input, own_up, lax.ppermute(own_up, "tensor", up), own_down]
    other_list = [other_input, other_up, lax.ppermute(other_down, "tensor", down), other_down]
    returned = lax.all_to_all(partial_grads, context, split_axis=0, concat_axis=0, tiled=True)
    targets = lax.dynamic_slice_in_dim(order_row, where * slots, slots, 0) // slots
    own_kv = prefetched(collect_kernel, 1, jax.ShapeDtypeStruct((tokens, 2 * HD), low))(
        targets, returned
    )
    other_kv = lax.ppermute(own_kv, "core", swap)

    input_scratch = (
        pltpu.VMEM((len(own_list), half, tokens), low),
        pltpu.SemaphoreType.DMA((len(own_list),)),
    )
    first_product = prefetched(
        first_product_kernel,
        0,
        jax.ShapeDtypeStruct((len(own_list), half, 2 * HD), jnp.float32),
        scratch=input_scratch,
        in_place=len(own_list),
    )(*own_list, own_kv)
    spread = prefetched(
        product_kernel,
        1,
        jax.ShapeDtypeStruct((replicas, lines, 2, HB // replicas, 2 * HD), low),
        scratch=input_scratch,
        in_place=len(other_list),
    )(
        jnp.stack([core, lax.axis_index("tensor")]),
        *other_list,
        first_product,
        other_kv,
        hadamard_signs(HB),
        recv[:, AUX_AT:ROWS],
    )
    spread = spread.reshape(replicas * lines, 2, HB // replicas, 2 * HD)
    shares = lax.all_to_all(spread, ("dp", "y"), split_axis=0, concat_axis=0, tiled=True)
    return jnp.sum(shares.astype(jnp.float32), axis=0)


def solution(mesh):
    replicas, groups, widths = mesh.devices.shape
    split = Mesh(
        mesh.devices.reshape(replicas, groups // CORES, CORES, widths),
        ("dp", "y", "core", "tensor"),
    )
    context = ("y", "core")
    return jax.shard_map(
        per_device,
        mesh=split,
        in_specs=(
            P("dp", context, "tensor"),
            P("dp", "tensor", context, None),
            P("dp", "tensor", context, None),
            P("dp", "tensor", context, None),
            P("dp", "tensor", context, None),
            P("dp", "tensor", context),
            P("dp", "tensor", context),
            P("dp", None),
            P("dp", None),
            P(context, None),
            P("dp", context),
        ),
        out_specs=P(context, "dp", "tensor"),
        check_vma=False,
    )
```

```python
import jax
import jax.numpy as jnp
from jax import lax
from jax.experimental import pallas as pl
from jax.experimental.pallas import tpu as pltpu
from jax.sharding import Mesh
from jax.sharding import PartitionSpec as P

HD = 128
GROUP = 4
BLK = 32
PAD = 128
HB = 128
CORES = 2
SPAN = 3
LOG2E = 1.4426950408889634

QROWS = GROUP * BLK
KV_AT = 2 * QROWS
AUX_AT = KV_AT + SPAN * 2 * BLK
AUX_ROWS = 8
ROWS = AUX_AT + AUX_ROWS
UNIT_BLKS = PAD // BLK
HOPS = (0, 1, 3, 2)


def hadamard_signs(table_size):
    index_row = jnp.arange(table_size, dtype=jnp.int32)
    common = jnp.bitwise_and(index_row[:, None], index_row[None, :])
    parity = jnp.zeros((table_size, table_size), jnp.int32)
    for bit_pos in range(table_size.bit_length() - 1):
        parity = parity + jnp.bitwise_and(jnp.right_shift(common, bit_pos), 1)
    return (1 - 2 * jnp.bitwise_and(parity, 1)).astype(jnp.bfloat16)


def pack_kernel(where_ref, *refs):
    (query_ref, grad_ref, key_ref, value_ref, lse_ref, dots_ref, sign_ref), refs = refs[:7], refs[7:]
    order_ref, exponent_ref, out_ref = refs[:3]
    query_scr, grad_scr, key_scr, value_scr, lse_scr, dots_scr, sign_scr = refs[3:10]
    order_scr, exponent_scr, held_scr, aux_scr, packed_scr, in_sem, out_sem = refs[10:]
    sources = (order_ref, exponent_ref, lse_ref, dots_ref, sign_ref)
    sources += (key_ref, value_ref, query_ref, grad_ref)
    places = (order_scr, exponent_scr, lse_scr, dots_scr, sign_scr)
    places += (key_scr, value_scr, query_scr, grad_scr)
    loads = [
        pltpu.make_async_copy(source, place, in_sem.at[i])
        for i, (source, place) in enumerate(zip(sources, places))
    ]
    for load in loads:
        load.start()
    groups = out_ref.shape[0]
    slots = key_ref.shape[2] // BLK
    for load in loads[:5]:
        load.wait()
    first = where_ref[0] * slots
    for slot in range(slots):
        held_scr[order_scr[0, first + slot] // slots] = slot

    fixed = [sign_scr[...].astype(jnp.float32)]
    for blk in range(sign_ref.shape[0]):
        power = jnp.full((1, HD), jnp.left_shift(jnp.int32(1), exponent_scr[0, blk]), jnp.int32)
        fixed.append(1.0 / power.astype(jnp.float32))
    fixed.append(jnp.zeros((AUX_ROWS - 6, HD), jnp.float32))
    head_of = lax.broadcasted_iota(jnp.int32, (1, HD), 1) // BLK
    stats = (lse_scr[0].astype(jnp.float32), dots_scr[0].astype(jnp.float32))

    def by_head(array, slot):
        part = slot * BLK // HD * HD
        inner = slot % (HD // BLK)
        row = jnp.zeros((1, HD), jnp.float32)
        for head in range(GROUP):
            line = array[head : head + 1, part : part + HD]
            turn = (head - inner) * BLK % HD
            line = pltpu.roll(line, turn, 1) if turn else line
            row = jnp.where(head_of == head, line, row)
        return row

    for slot in range(slots):
        aux = jnp.concatenate([by_head(array, slot) for array in stats] + fixed, axis=0)
        aux_scr[slot] = aux.astype(aux_scr.dtype)
    for load in loads[5:]:
        load.wait()

    stores = []
    for dest in range(groups):
        slot = held_scr[dest]
        rows = pl.ds(pl.multiple_of(slot * BLK, BLK), BLK)
        for head in range(GROUP):
            packed_scr[dest, head * BLK : (head + 1) * BLK, :] = query_scr[0, head, rows, :]
            at = QROWS + head * BLK
            packed_scr[dest, at : at + BLK, :] = grad_scr[0, head, rows, :]
        for span in range(SPAN):
            at = KV_AT + span * 2 * BLK
            if dest >= span:
                rows = pl.ds(pl.multiple_of(held_scr[dest - span] * BLK, BLK), BLK)
                packed_scr[dest, at : at + BLK, :] = key_scr[0, 0, rows, :]
                packed_scr[dest, at + BLK : at + 2 * BLK, :] = value_scr[0, 0, rows, :]
            else:
                packed_scr[dest, at : at + 2 * BLK, :] = jnp.zeros((2 * BLK, HD), out_ref.dtype)
        packed_scr[dest, AUX_AT:ROWS, :] = aux_scr[slot]
        stores.append(pltpu.make_async_copy(packed_scr.at[dest], out_ref.at[dest], out_sem.at[dest]))
        stores[-1].start()
    for store in stores:
        store.wait()


def attend_kernel(
    slot_ref, start_ref, recv_ref, out_ref,
    query_scr, grad_scr, query_turned, grad_turned, stat_scr,
    key_scr, value_scr, dkey_scr, dvalue_scr,
):
    groups = recv_ref.shape[0]
    chunk = key_scr.shape[0] // SPAN
    units = chunk // PAD
    width = UNIT_BLKS * QROWS
    pair = 2 * PAD
    dkey_scr[...] = jnp.zeros_like(dkey_scr)
    dvalue_scr[...] = jnp.zeros_like(dvalue_scr)
    for src in range(groups):
        slot = slot_ref[0, src]
        at = pl.multiple_of(slot * QROWS, QROWS)
        query_blk = recv_ref[src, 0:QROWS, :]
        grad_blk = recv_ref[src, QROWS : 2 * QROWS, :]
        query_scr[pl.ds(at, QROWS), :] = query_blk
        grad_scr[pl.ds(at, QROWS), :] = grad_blk
        query_turned[:, pl.ds(at, QROWS)] = query_blk.T
        grad_turned[:, pl.ds(at, QROWS)] = grad_blk.T
        stat_scr[slot] = recv_ref[src, AUX_AT:ROWS, :].astype(jnp.float32)
        for span in range(SPAN):
            row = (SPAN - 1 - span) * chunk + slot_ref[span, src] * BLK
            row = pl.multiple_of(row, BLK)
            at = KV_AT + span * 2 * BLK
            key_scr[pl.ds(row, BLK), :] = recv_ref[src, at : at + BLK, :]
            value_scr[pl.ds(row, BLK), :] = recv_ref[src, at + BLK : at + 2 * BLK, :]

    scale = HD ** (-0.5)
    key_at = lax.broadcasted_iota(jnp.int32, (pair, width), 0)
    column = lax.broadcasted_iota(jnp.int32, (pair, width), 1)
    query_at = (column // QROWS) * BLK + column % BLK
    causal = key_at - PAD <= query_at

    for unit in range(units):
        cols = slice(unit * width, (unit + 1) * width)
        blocks = range(unit * UNIT_BLKS, (unit + 1) * UNIT_BLKS)
        lse = jnp.concatenate([stat_scr[b, 0:1, :] for b in blocks], axis=1) * LOG2E
        dots = jnp.concatenate([stat_scr[b, 1:2, :] for b in blocks], axis=1)

        def visit(row, live):
            rows = pl.ds(row, pair)
            scores = jnp.dot(
                key_scr[rows, :], query_turned[:, cols], preferred_element_type=jnp.float32
            )
            dprobs = jnp.dot(
                value_scr[rows, :], grad_turned[:, cols], preferred_element_type=jnp.float32
            )
            probs = jnp.where(live, jnp.exp2(scores * (scale * LOG2E) - lse), 0.0)
            dscores = (probs * (dprobs - dots)).astype(jnp.bfloat16)
            dvalue_scr[rows, :] += jnp.dot(
                probs.astype(jnp.bfloat16), grad_scr[cols, :], preferred_element_type=jnp.float32
            )
            dkey_scr[rows, :] += jnp.dot(
                dscores, query_scr[cols, :], preferred_element_type=jnp.float32
            )

        first = start_ref[unit]
        last = (SPAN - 1) * units + unit
        visit((last - 1) * PAD, causal & (key_at >= (first - (last - 1)) * PAD))

        @pl.loop(1, (last - first + 2) // 2)
        def _(step):
            base = last - 1 - 2 * step
            visit(pl.multiple_of(base * PAD, PAD), key_at >= (first - base) * PAD)

    for src in range(groups):
        for span in range(SPAN):
            row = (SPAN - 1 - span) * chunk + slot_ref[span, src] * BLK
            row = pl.multiple_of(row, BLK)
            dkey = dkey_scr[pl.ds(row, BLK), :] * scale
            out_ref[src, span, 0:BLK, :] = dkey.astype(out_ref.dtype)
            out_ref[src, span, BLK : 2 * BLK, :] = dvalue_scr[pl.ds(row, BLK), :].astype(
                out_ref.dtype
            )


def collect_kernel(target_ref, recv_ref, out_ref):
    groups = recv_ref.shape[0]
    for slot in range(out_ref.shape[0] // BLK):
        owner = target_ref[slot]
        total = recv_ref[owner, 0].astype(jnp.float32)
        for span in range(1, SPAN):
            extra = recv_ref[jnp.minimum(owner + span, groups - 1), span].astype(jnp.float32)
            total = total + jnp.where(owner + span < groups, extra, 0.0)
        rows = slice(slot * BLK, (slot + 1) * BLK)
        total = total.astype(out_ref.dtype)
        out_ref[rows, 0:HD] = total[0:BLK]
        out_ref[rows, HD : 2 * HD] = total[BLK : 2 * BLK]


def turn_kernel(core_ref, input_ref, own_ref, other_ref):
    span = 2 * HB
    core = core_ref[0]
    for part in range(own_ref.shape[0] // span):
        rows = slice(part * span, (part + 1) * span)
        at = pl.multiple_of((CORES * part + core) * span, span)
        own_ref[rows, :] = input_ref[:, pl.ds(at, span)].T
        at = pl.multiple_of((CORES * part + 1 - core) * span, span)
        other_ref[rows, :] = input_ref[:, pl.ds(at, span)].T


def load_all(sources, places, sems):
    loads = [
        pltpu.make_async_copy(source, places.at[i], sems.at[i]) for i, source in enumerate(sources)
    ]
    for load in loads:
        load.start()
    return loads


def first_product_kernel(*refs):
    far_ref, kv_ref, out_ref, input_scr, sems = refs[-5:]
    loads = load_all(refs[:-5], input_scr, sems)
    last = len(loads)
    out_ref[last] = jnp.dot(far_ref[...], kv_ref[...], preferred_element_type=jnp.float32)
    for step, load in enumerate(loads):
        load.wait()
        out_ref[step] = jnp.dot(input_scr[step], kv_ref[...], preferred_element_type=jnp.float32)


def product_kernel(where_ref, *refs):
    far_ref, first_ref, kv_ref, had_ref, aux_ref, out_ref, input_scr, sems = refs[-8:]
    loads = load_all(refs[:-8], input_scr, sems)
    core, width = where_ref[0], where_ref[1]
    replicas = out_ref.shape[0]
    span = 2 * HB
    parts = far_ref.shape[0] // span
    had = jnp.concatenate([had_ref[...].astype(jnp.float32)] * 2, axis=1)
    widths = len(HOPS)
    for step in (widths - 1, *range(widths - 1)):
        source = (width + widths - HOPS[step]) % widths
        if step < len(loads):
            loads[step].wait()
            inputs = input_scr[step]
        else:
            inputs = far_ref[...]
        grad = jnp.dot(inputs, kv_ref[...], preferred_element_type=jnp.float32)
        grad = grad + first_ref[step]
        for part in range(parts):
            line = source * parts + part
            aux = aux_ref[CORES * line + core].astype(jnp.float32)
            for blk in range(2):
                at = part * span + blk * HB
                rows = grad[at : at + HB]
                sign = aux[2 + blk : 3 + blk, :]
                table = (had * jnp.concatenate([sign, sign], axis=1)).astype(jnp.bfloat16)
                high = rows.astype(jnp.bfloat16)
                low = (rows - high.astype(jnp.float32)).astype(jnp.bfloat16)
                both = jnp.concatenate([high, low], axis=0)
                rotated = jnp.dot(table, both, preferred_element_type=jnp.float32)
                factor = aux[4 + blk : 5 + blk, :] * (HB ** (-0.5))
                rotated *= jnp.concatenate([factor] * (rows.shape[1] // HB), axis=1)
                out_ref[:, line, blk] = rotated.astype(out_ref.dtype).reshape(
                    replicas, HB // replicas, rows.shape[1]
                )


def prefetched(kernel, scalars, out_shape, scratch=(), in_place=0, out_space=pltpu.VMEM):
    vmem = pl.BlockSpec(memory_space=pltpu.VMEM)
    hbm = pl.BlockSpec(memory_space=pltpu.HBM)
    out_spec = pl.BlockSpec(memory_space=out_space)

    def call(*operands):
        held = scalars + in_place
        kept = [
            pltpu.with_memory_space_constraint(array, pltpu.HBM)
            for array in operands[scalars:held]
        ]
        return pl.pallas_call(
            kernel,
            out_shape=out_shape,
            grid_spec=pltpu.PrefetchScalarGridSpec(
                num_scalar_prefetch=scalars,
                in_specs=[hbm] * in_place + [vmem] * (len(operands) - held),
                out_specs=jax.tree.map(lambda _: out_spec, out_shape),
                scratch_shapes=list(scratch),
            ),
            compiler_params=pltpu.CompilerParams(vmem_limit_bytes=16 << 20),
        )(*operands[:scalars], *kept, *operands[held:])

    return call


def around(count, step):
    return [(i, (i + step) % count) for i in range(count)]


def per_device(
    layer_input,
    queries,
    key_states,
    value_states,
    out_grad,
    log_sums,
    grad_dots,
    doc_stretches,
    stretch_order,
    sign_vector,
    exponents,
):
    context = ("y", "core")
    low = jnp.bfloat16
    tokens = queries.shape[2]
    slots = tokens // BLK
    groups = lax.axis_size(context)
    lines = lax.axis_size("y")
    replicas = lax.axis_size("dp")
    order_row = stretch_order[0]
    where = lax.axis_index(context)
    core = lax.axis_index("core")

    raw = (queries, out_grad, key_states, value_states, log_sums, grad_dots, sign_vector)
    packed = prefetched(
        pack_kernel,
        1,
        pltpu.HBM((groups, ROWS, HD), low),
        scratch=(
            *(pltpu.VMEM(array.shape, array.dtype) for array in raw),
            pltpu.SMEM(stretch_order.shape, jnp.int32),
            pltpu.SMEM(exponents.shape, jnp.int32),
            pltpu.SMEM((groups,), jnp.int32),
            pltpu.VMEM((slots, AUX_ROWS, HD), low),
            pltpu.VMEM((groups, ROWS, HD), low),
            pltpu.SemaphoreType.DMA((9,)),
            pltpu.SemaphoreType.DMA((groups,)),
        ),
        in_place=len(raw) + 2,
        out_space=pltpu.HBM,
    )(where.reshape(1), *raw, stretch_order, exponents)
    packed, layer_input = lax.optimization_barrier((packed, layer_input))
    recv = lax.all_to_all(packed, context, split_axis=0, concat_axis=0, tiled=True)

    half = layer_input.shape[2] // CORES
    turned = jax.ShapeDtypeStruct((half, tokens), low)
    own_input, other_input = prefetched(turn_kernel, 1, (turned, turned))(
        core.reshape(1), layer_input[0]
    )
    swap = [(0, 1), (1, 0)]
    other_input = lax.ppermute(other_input, "core", swap)
    widths = lax.axis_size("tensor")
    up, down = around(widths, 1), around(widths, -1)
    near = [
        lax.ppermute(array, "tensor", way)
        for array in (own_input, other_input)
        for way in (up, down)
    ]
    recv, near = lax.optimization_barrier((recv, near))

    order_grid = order_row.reshape(groups, slots)
    chunk_ids = (where - jnp.arange(SPAN, dtype=jnp.int32))[:, None, None]
    slot_map = jnp.sum(
        jnp.where(order_grid[None] // slots == chunk_ids, order_grid[None] % slots, 0), axis=2
    )
    ends = jnp.cumsum(doc_stretches[0])
    chunk_units = tokens // PAD
    unit_ids = where * chunk_units + jnp.arange(chunk_units, dtype=jnp.int32)
    doc_start = jnp.max(jnp.where(ends[None, :] <= unit_ids[:, None], ends[None, :], 0), axis=1)
    starts = doc_start - (where - (SPAN - 1)) * chunk_units

    window = SPAN * tokens
    partial_grads = prefetched(
        attend_kernel,
        2,
        jax.ShapeDtypeStruct((groups, SPAN, 2 * BLK, HD), low),
        scratch=(
            pltpu.VMEM((slots * QROWS, HD), low),
            pltpu.VMEM((slots * QROWS, HD), low),
            pltpu.VMEM((HD, slots * QROWS), low),
            pltpu.VMEM((HD, slots * QROWS), low),
            pltpu.VMEM((slots, AUX_ROWS, HD), jnp.float32),
            pltpu.VMEM((window, HD), low),
            pltpu.VMEM((window, HD), low),
            pltpu.VMEM((window, HD), jnp.float32),
            pltpu.VMEM((window, HD), jnp.float32),
        ),
    )(slot_map, starts, recv)
    partial_grads, near = lax.optimization_barrier((partial_grads, near))
    own_up, own_down, other_up, other_down = near
    own_list = [own_input, own_up, own_down, lax.ppermute(own_up, "tensor", up)]
    other_list = [other_input, other_up, other_down, lax.ppermute(other_down, "tensor", down)]
    returned = lax.all_to_all(partial_grads, context, split_axis=0, concat_axis=0, tiled=True)
    targets = lax.dynamic_slice_in_dim(order_row, where * slots, slots, 0) // slots
    own_kv = prefetched(collect_kernel, 1, jax.ShapeDtypeStruct((tokens, 2 * HD), low))(
        targets, returned
    )
    other_kv = lax.ppermute(own_kv, "core", swap)

    input_scratch = (
        pltpu.VMEM((widths - 1, half, tokens), low),
        pltpu.SemaphoreType.DMA((widths - 1,)),
    )
    first_product = prefetched(
        first_product_kernel,
        0,
        jax.ShapeDtypeStruct((len(own_list), half, 2 * HD), jnp.float32),
        scratch=input_scratch,
        in_place=widths - 1,
    )(*own_list, own_kv)
    spread = prefetched(
        product_kernel,
        1,
        jax.ShapeDtypeStruct((replicas, lines, 2, HB // replicas, 2 * HD), low),
        scratch=input_scratch,
        in_place=widths - 1,
    )(
        jnp.stack([core, lax.axis_index("tensor")]),
        *other_list,
        first_product,
        other_kv,
        hadamard_signs(HB),
        recv[:, AUX_AT:ROWS],
    )
    spread = spread.reshape(replicas * lines, 2, HB // replicas, 2 * HD)
    shares = lax.all_to_all(spread, ("dp", "y"), split_axis=0, concat_axis=0, tiled=True)
    return jnp.sum(shares.astype(jnp.float32), axis=0)


def solution(mesh):
    replicas, groups, widths = mesh.devices.shape
    split = Mesh(
        mesh.devices.reshape(replicas, groups // CORES, CORES, widths),
        ("dp", "y", "core", "tensor"),
    )
    context = ("y", "core")
    return jax.shard_map(
        per_device,
        mesh=split,
        in_specs=(
            P("dp", context, "tensor"),
            P("dp", "tensor", context, None),
            P("dp", "tensor", context, None),
            P("dp", "tensor", context, None),
            P("dp", "tensor", context, None),
            P("dp", "tensor", context),
            P("dp", "tensor", context),
            P("dp", None),
            P("dp", None),
            P(context, None),
            P("dp", context),
        ),
        out_specs=P(context, "dp", "tensor"),
        check_vma=False,
    )
```

```python
import functools

import jax
import jax.numpy as jnp
from jax import lax
from jax.experimental import pallas as pl
from jax.experimental.pallas import tpu as pltpu
from jax.sharding import Mesh
from jax.sharding import PartitionSpec as P

HD = 128
GROUP = 4
BLK = 32
PAD = 128
HB = 128
CORES = 2
SPAN = 3
SENT = (0, 2)
LOG2E = 1.4426950408889634

QROWS = GROUP * BLK
KV_AT = 2 * QROWS
AUX_AT = KV_AT + len(SENT) * 2 * BLK
AUX_ROWS = 8
ROWS = AUX_AT + AUX_ROWS
UNIT_BLKS = PAD // BLK
HOPS = (0, 1, 3, 2)


def hadamard_signs(table_size):
    index_row = jnp.arange(table_size, dtype=jnp.int32)
    common = jnp.bitwise_and(index_row[:, None], index_row[None, :])
    parity = jnp.zeros((table_size, table_size), jnp.int32)
    for bit_pos in range(table_size.bit_length() - 1):
        parity = parity + jnp.bitwise_and(jnp.right_shift(common, bit_pos), 1)
    return (1 - 2 * jnp.bitwise_and(parity, 1)).astype(jnp.bfloat16)


def pack_kernel(where_ref, *refs):
    (query_ref, grad_ref, key_ref, value_ref, lse_ref, dots_ref, sign_ref), refs = refs[:7], refs[7:]
    order_ref, exponent_ref, out_ref = refs[:3]
    query_scr, grad_scr, key_scr, value_scr, lse_scr, dots_scr, sign_scr = refs[3:10]
    order_scr, exponent_scr, held_scr, aux_scr, packed_scr, in_sem, out_sem = refs[10:]
    sources = (order_ref, exponent_ref, lse_ref, dots_ref, sign_ref)
    sources += (key_ref, value_ref, query_ref, grad_ref)
    places = (order_scr, exponent_scr, lse_scr, dots_scr, sign_scr)
    places += (key_scr, value_scr, query_scr, grad_scr)
    loads = [
        pltpu.make_async_copy(source, place, in_sem.at[i])
        for i, (source, place) in enumerate(zip(sources, places))
    ]
    for load in loads:
        load.start()
    groups = out_ref.shape[0]
    slots = key_ref.shape[2] // BLK
    for load in loads[:5]:
        load.wait()
    first = where_ref[0] * slots
    for slot in range(slots):
        held_scr[order_scr[0, first + slot] // slots] = slot

    fixed = [sign_scr[...].astype(jnp.float32)]
    for blk in range(sign_ref.shape[0]):
        power = jnp.full((1, HD), jnp.left_shift(jnp.int32(1), exponent_scr[0, blk]), jnp.int32)
        fixed.append(1.0 / power.astype(jnp.float32))
    fixed.append(jnp.zeros((AUX_ROWS - 6, HD), jnp.float32))
    head_of = lax.broadcasted_iota(jnp.int32, (1, HD), 1) // BLK
    stats = (lse_scr[0].astype(jnp.float32), dots_scr[0].astype(jnp.float32))

    def by_head(array, slot):
        part = slot * BLK // HD * HD
        inner = slot % (HD // BLK)
        row = jnp.zeros((1, HD), jnp.float32)
        for head in range(GROUP):
            line = array[head : head + 1, part : part + HD]
            turn = (head - inner) * BLK % HD
            line = pltpu.roll(line, turn, 1) if turn else line
            row = jnp.where(head_of == head, line, row)
        return row

    for slot in range(slots):
        aux = jnp.concatenate([by_head(array, slot) for array in stats] + fixed, axis=0)
        aux_scr[slot] = aux.astype(aux_scr.dtype)
    for load in loads[5:]:
        load.wait()

    stores = []
    for dest in range(groups):
        slot = held_scr[dest]
        rows = pl.ds(pl.multiple_of(slot * BLK, BLK), BLK)
        for head in range(GROUP):
            packed_scr[dest, head * BLK : (head + 1) * BLK, :] = query_scr[0, head, rows, :]
            at = QROWS + head * BLK
            packed_scr[dest, at : at + BLK, :] = grad_scr[0, head, rows, :]
        for place, span in enumerate(SENT):
            at = KV_AT + place * 2 * BLK
            if dest >= span:
                rows = pl.ds(pl.multiple_of(held_scr[dest - span] * BLK, BLK), BLK)
                packed_scr[dest, at : at + BLK, :] = key_scr[0, 0, rows, :]
                packed_scr[dest, at + BLK : at + 2 * BLK, :] = value_scr[0, 0, rows, :]
            else:
                packed_scr[dest, at : at + 2 * BLK, :] = jnp.zeros((2 * BLK, HD), out_ref.dtype)
        packed_scr[dest, AUX_AT:ROWS, :] = aux_scr[slot]
        stores.append(pltpu.make_async_copy(packed_scr.at[dest], out_ref.at[dest], out_sem.at[dest]))
        stores[-1].start()
    for store in stores:
        store.wait()


def block_grads(key_blk, value_blk, query_refs, cols, lse, dots, live):
    query_ref, grad_ref, query_turned, grad_turned = query_refs
    scores = jnp.dot(key_blk, query_turned[:, cols], preferred_element_type=jnp.float32)
    dprobs = jnp.dot(value_blk, grad_turned[:, cols], preferred_element_type=jnp.float32)
    probs = jnp.where(live, jnp.exp2(scores * (HD ** (-0.5) * LOG2E) - lse), 0.0)
    dscores = (probs * (dprobs - dots)).astype(jnp.bfloat16)
    value_part = jnp.dot(
        probs.astype(jnp.bfloat16), grad_ref[cols, :], preferred_element_type=jnp.float32
    )
    key_part = jnp.dot(dscores, query_ref[cols, :], preferred_element_type=jnp.float32)
    return key_part, value_part


def unit_stats(stat_ref, unit):
    blocks = range(unit * UNIT_BLKS, (unit + 1) * UNIT_BLKS)
    lse = jnp.concatenate([stat_ref[b, 0:1, :] for b in blocks], axis=1) * LOG2E
    dots = jnp.concatenate([stat_ref[b, 1:2, :] for b in blocks], axis=1)
    return lse, dots


def rows_of(slot_ref, span, src):
    return pl.ds(pl.multiple_of(slot_ref[span, src] * BLK, BLK), BLK)


def store_slab(slot_ref, span, dkey_scr, dvalue_scr, out_ref):
    for src in range(out_ref.shape[0]):
        rows = rows_of(slot_ref, span, src)
        dkey = dkey_scr[rows, :] * HD ** (-0.5)
        out_ref[src, 0:BLK, :] = dkey.astype(out_ref.dtype)
        out_ref[src, BLK : 2 * BLK, :] = dvalue_scr[rows, :].astype(out_ref.dtype)


def own_attend_kernel(
    slot_ref, start_ref, recv_ref,
    query_ref, grad_ref, query_turned, grad_turned, stat_ref, out_ref,
    key_scr, value_scr, dkey_scr, dvalue_scr,
):
    units = key_scr.shape[0] // PAD
    width = UNIT_BLKS * QROWS
    for src in range(recv_ref.shape[0]):
        slot = slot_ref[0, src]
        at = pl.multiple_of(slot * QROWS, QROWS)
        query_blk = recv_ref[src, 0:QROWS, :]
        grad_blk = recv_ref[src, QROWS : 2 * QROWS, :]
        query_ref[pl.ds(at, QROWS), :] = query_blk
        grad_ref[pl.ds(at, QROWS), :] = grad_blk
        query_turned[:, pl.ds(at, QROWS)] = query_blk.T
        grad_turned[:, pl.ds(at, QROWS)] = grad_blk.T
        stat_ref[slot] = recv_ref[src, AUX_AT:ROWS, :].astype(jnp.float32)
        rows = rows_of(slot_ref, 0, src)
        key_scr[rows, :] = recv_ref[src, KV_AT : KV_AT + BLK, :]
        value_scr[rows, :] = recv_ref[src, KV_AT + BLK : KV_AT + 2 * BLK, :]

    queries = (query_ref, grad_ref, query_turned, grad_turned)
    dkey_scr[...] = jnp.zeros_like(dkey_scr)
    dvalue_scr[...] = jnp.zeros_like(dvalue_scr)
    for unit in range(units):
        rows = slice(0, (unit + 1) * PAD)
        cols = slice(unit * width, (unit + 1) * width)
        lse, dots = unit_stats(stat_ref, unit)
        key_at = lax.broadcasted_iota(jnp.int32, (rows.stop, width), 0)
        column = lax.broadcasted_iota(jnp.int32, (rows.stop, width), 1)
        query_at = unit * PAD + (column // QROWS) * BLK + column % BLK
        first = (start_ref[unit] - (SPAN - 1) * units) * PAD
        live = (key_at <= query_at) & (key_at >= first)
        key_part, value_part = block_grads(
            key_scr[rows, :], value_scr[rows, :], queries, cols, lse, dots, live
        )
        dkey_scr[rows, :] += key_part
        dvalue_scr[rows, :] += value_part
    store_slab(slot_ref, 0, dkey_scr, dvalue_scr, out_ref)


def earlier_attend_kernel(span, slot_ref, start_ref, kv_ref, *refs):
    queries, refs = refs[:4], refs[4:]
    stat_ref, out_ref, key_scr, value_scr, dkey_scr, dvalue_scr = refs
    units = key_scr.shape[0] // PAD
    width = UNIT_BLKS * QROWS
    pair = 2 * PAD
    for src in range(kv_ref.shape[0]):
        rows = rows_of(slot_ref, span, src)
        key_scr[rows, :] = kv_ref[src, 0:BLK, :]
        value_scr[rows, :] = kv_ref[src, BLK : 2 * BLK, :]
    dkey_scr[...] = jnp.zeros_like(dkey_scr)
    dvalue_scr[...] = jnp.zeros_like(dvalue_scr)
    key_at = lax.broadcasted_iota(jnp.int32, (pair, width), 0)
    for unit in range(units):
        cols = slice(unit * width, (unit + 1) * width)
        lse, dots = unit_stats(stat_ref, unit)
        first = jnp.clip(start_ref[unit] - (SPAN - 1 - span) * units, 0, units)

        @pl.loop(0, (units - first + 1) // 2)
        def _(step):
            base = units - 2 - 2 * step
            rows = pl.ds(pl.multiple_of(base * PAD, pair), pair)
            key_part, value_part = block_grads(
                key_scr[rows, :],
                value_scr[rows, :],
                queries,
                cols,
                lse,
                dots,
                key_at >= (first - base) * PAD,
            )
            dkey_scr[rows, :] += key_part
            dvalue_scr[rows, :] += value_part

    store_slab(slot_ref, span, dkey_scr, dvalue_scr, out_ref)


def merge_kernel(core_ref, own_ref, far_ref, shared_ref, out_ref):
    core = core_ref[0]
    for src in range(out_ref.shape[0]):
        shared = shared_ref[src].astype(jnp.float32)
        own = own_ref[src] + jnp.where(core == 0, shared, 0.0)
        far = far_ref[src] + jnp.where(core == 0, 0.0, shared)
        out_ref[src, 0] = own.astype(out_ref.dtype)
        out_ref[src, 1] = far.astype(out_ref.dtype)


def collect_kernel(target_ref, recv_ref, out_ref):
    groups = recv_ref.shape[0]
    for slot in range(out_ref.shape[0] // BLK):
        owner = target_ref[slot]
        total = recv_ref[owner, 0].astype(jnp.float32)
        later = owner + SENT[1]
        extra = recv_ref[jnp.minimum(later, groups - 1), 1].astype(jnp.float32)
        total = total + jnp.where(later < groups, extra, 0.0)
        rows = slice(slot * BLK, (slot + 1) * BLK)
        total = total.astype(out_ref.dtype)
        out_ref[rows, 0:HD] = total[0:BLK]
        out_ref[rows, HD : 2 * HD] = total[BLK : 2 * BLK]


def turn_kernel(core_ref, input_ref, own_ref, other_ref):
    span = 2 * HB
    core = core_ref[0]
    for part in range(own_ref.shape[0] // span):
        rows = slice(part * span, (part + 1) * span)
        at = pl.multiple_of((CORES * part + core) * span, span)
        own_ref[rows, :] = input_ref[:, pl.ds(at, span)].T
        at = pl.multiple_of((CORES * part + 1 - core) * span, span)
        other_ref[rows, :] = input_ref[:, pl.ds(at, span)].T


def load_all(sources, places, sems):
    loads = [
        pltpu.make_async_copy(source, places.at[i], sems.at[i]) for i, source in enumerate(sources)
    ]
    for load in loads:
        load.start()
    return loads


def first_product_kernel(*refs):
    far_ref, kv_ref, out_ref, input_scr, sems = refs[-5:]
    loads = load_all(refs[:-5], input_scr, sems)
    last = len(loads)
    out_ref[last] = jnp.dot(far_ref[...], kv_ref[...], preferred_element_type=jnp.float32)
    for step, load in enumerate(loads):
        load.wait()
        out_ref[step] = jnp.dot(input_scr[step], kv_ref[...], preferred_element_type=jnp.float32)


def product_kernel(where_ref, *refs):
    far_ref, first_ref, kv_ref, had_ref, aux_ref, out_ref, input_scr, sems = refs[-8:]
    loads = load_all(refs[:-8], input_scr, sems)
    core, width = where_ref[0], where_ref[1]
    replicas = out_ref.shape[0]
    span = 2 * HB
    parts = far_ref.shape[0] // span
    had = jnp.concatenate([had_ref[...].astype(jnp.float32)] * 2, axis=1)
    widths = len(HOPS)
    for step in (widths - 1, *range(widths - 1)):
        source = (width + widths - HOPS[step]) % widths
        if step < len(loads):
            loads[step].wait()
            inputs = input_scr[step]
        else:
            inputs = far_ref[...]
        grad = jnp.dot(inputs, kv_ref[...], preferred_element_type=jnp.float32)
        grad = grad + first_ref[step]
        for part in range(parts):
            line = source * parts + part
            aux = aux_ref[CORES * line + core].astype(jnp.float32)
            for blk in range(2):
                at = part * span + blk * HB
                rows = grad[at : at + HB]
                sign = aux[2 + blk : 3 + blk, :]
                table = (had * jnp.concatenate([sign, sign], axis=1)).astype(jnp.bfloat16)
                high = rows.astype(jnp.bfloat16)
                low = (rows - high.astype(jnp.float32)).astype(jnp.bfloat16)
                both = jnp.concatenate([high, low], axis=0)
                rotated = jnp.dot(table, both, preferred_element_type=jnp.float32)
                factor = aux[4 + blk : 5 + blk, :] * (HB ** (-0.5))
                rotated *= jnp.concatenate([factor] * (rows.shape[1] // HB), axis=1)
                out_ref[:, line, blk] = rotated.astype(out_ref.dtype).reshape(
                    replicas, HB // replicas, rows.shape[1]
                )


def prefetched(kernel, scalars, out_shape, scratch=(), in_place=0, out_space=pltpu.VMEM):
    vmem = pl.BlockSpec(memory_space=pltpu.VMEM)
    hbm = pl.BlockSpec(memory_space=pltpu.HBM)
    out_spec = pl.BlockSpec(memory_space=out_space)

    def call(*operands):
        held = scalars + in_place
        kept = [
            pltpu.with_memory_space_constraint(array, pltpu.HBM)
            for array in operands[scalars:held]
        ]
        return pl.pallas_call(
            kernel,
            out_shape=out_shape,
            grid_spec=pltpu.PrefetchScalarGridSpec(
                num_scalar_prefetch=scalars,
                in_specs=[hbm] * in_place + [vmem] * (len(operands) - held),
                out_specs=jax.tree.map(lambda _: out_spec, out_shape),
                scratch_shapes=list(scratch),
            ),
            compiler_params=pltpu.CompilerParams(vmem_limit_bytes=16 << 20),
        )(*operands[:scalars], *kept, *operands[held:])

    return call


def around(count, step):
    return [(i, (i + step) % count) for i in range(count)]


def per_device(
    layer_input,
    queries,
    key_states,
    value_states,
    out_grad,
    log_sums,
    grad_dots,
    doc_stretches,
    stretch_order,
    sign_vector,
    exponents,
):
    context = ("y", "core")
    low = jnp.bfloat16
    tokens = queries.shape[2]
    slots = tokens // BLK
    groups = lax.axis_size(context)
    lines = lax.axis_size("y")
    replicas = lax.axis_size("dp")
    order_row = stretch_order[0]
    where = lax.axis_index(context)
    core = lax.axis_index("core")

    raw = (queries, out_grad, key_states, value_states, log_sums, grad_dots, sign_vector)
    packed = prefetched(
        pack_kernel,
        1,
        pltpu.HBM((groups, ROWS, HD), low),
        scratch=(
            *(pltpu.VMEM(array.shape, array.dtype) for array in raw),
            pltpu.SMEM(stretch_order.shape, jnp.int32),
            pltpu.SMEM(exponents.shape, jnp.int32),
            pltpu.SMEM((groups,), jnp.int32),
            pltpu.VMEM((slots, AUX_ROWS, HD), low),
            pltpu.VMEM((groups, ROWS, HD), low),
            pltpu.SemaphoreType.DMA((9,)),
            pltpu.SemaphoreType.DMA((groups,)),
        ),
        in_place=len(raw) + 2,
        out_space=pltpu.HBM,
    )(where.reshape(1), *raw, stretch_order, exponents)
    packed, layer_input = lax.optimization_barrier((packed, layer_input))
    recv = lax.all_to_all(packed, context, split_axis=0, concat_axis=0, tiled=True)

    half = layer_input.shape[2] // CORES
    turned = jax.ShapeDtypeStruct((half, tokens), low)
    own_input, other_input = prefetched(turn_kernel, 1, (turned, turned))(
        core.reshape(1), layer_input[0]
    )
    swap = [(0, 1), (1, 0)]
    other_input = lax.ppermute(other_input, "core", swap)
    widths = lax.axis_size("tensor")
    up, down = around(widths, 1), around(widths, -1)
    near = [
        lax.ppermute(array, "tensor", way)
        for array in (own_input, other_input)
        for way in (up, down)
    ]
    recv, near = lax.optimization_barrier((recv, near))

    order_grid = order_row.reshape(groups, slots)
    chunk_ids = (where - jnp.arange(SPAN, dtype=jnp.int32))[:, None, None]
    slot_map = jnp.sum(
        jnp.where(order_grid[None] // slots == chunk_ids, order_grid[None] % slots, 0), axis=2
    )
    ends = jnp.cumsum(doc_stretches[0])
    chunk_units = tokens // PAD
    unit_ids = where * chunk_units + jnp.arange(chunk_units, dtype=jnp.int32)
    doc_start = jnp.max(jnp.where(ends[None, :] <= unit_ids[:, None], ends[None, :], 0), axis=1)
    starts = doc_start - (where - (SPAN - 1)) * chunk_units

    at = KV_AT + lax.axis_index("core") * 2 * BLK
    shared_kv = lax.ppermute(lax.dynamic_slice_in_dim(recv, at, 2 * BLK, 1), "core", swap)
    sorted_rows = jax.ShapeDtypeStruct((slots * QROWS, HD), low)
    turned_rows = jax.ShapeDtypeStruct((HD, slots * QROWS), low)
    slab = (groups, 2 * BLK, HD)
    chunk_scratch = tuple(
        pltpu.VMEM((tokens, HD), dtype) for dtype in (low, low, jnp.float32, jnp.float32)
    )
    *shared_work, own_slab = prefetched(
        own_attend_kernel,
        2,
        (
            sorted_rows,
            sorted_rows,
            turned_rows,
            turned_rows,
            jax.ShapeDtypeStruct((slots, AUX_ROWS, HD), jnp.float32),
            jax.ShapeDtypeStruct(slab, jnp.float32),
        ),
        scratch=chunk_scratch,
    )(slot_map, starts, recv)
    before_slab = prefetched(
        functools.partial(earlier_attend_kernel, 1),
        2,
        jax.ShapeDtypeStruct(slab, low),
        scratch=chunk_scratch,
    )(slot_map, starts, shared_kv, *shared_work)
    shared_slab = lax.ppermute(before_slab, "core", swap)
    far_slab = prefetched(
        functools.partial(earlier_attend_kernel, 2),
        2,
        jax.ShapeDtypeStruct(slab, jnp.float32),
        scratch=chunk_scratch,
    )(slot_map, starts, recv[:, KV_AT + 2 * BLK : AUX_AT], *shared_work)
    partial_grads = prefetched(
        merge_kernel, 1, jax.ShapeDtypeStruct((groups, len(SENT), 2 * BLK, HD), low)
    )(core.reshape(1), own_slab, far_slab, shared_slab)
    partial_grads, near = lax.optimization_barrier((partial_grads, near))
    own_up, own_down, other_up, other_down = near
    own_list = [own_input, own_up, own_down, lax.ppermute(own_up, "tensor", up)]
    other_list = [other_input, other_up, other_down, lax.ppermute(other_down, "tensor", down)]
    returned = lax.all_to_all(partial_grads, context, split_axis=0, concat_axis=0, tiled=True)
    targets = lax.dynamic_slice_in_dim(order_row, where * slots, slots, 0) // slots
    own_kv = prefetched(collect_kernel, 1, jax.ShapeDtypeStruct((tokens, 2 * HD), low))(
        targets, returned
    )
    other_kv = lax.ppermute(own_kv, "core", swap)

    input_scratch = (
        pltpu.VMEM((widths - 1, half, tokens), low),
        pltpu.SemaphoreType.DMA((widths - 1,)),
    )
    first_product = prefetched(
        first_product_kernel,
        0,
        jax.ShapeDtypeStruct((len(own_list), half, 2 * HD), jnp.float32),
        scratch=input_scratch,
        in_place=widths - 1,
    )(*own_list, own_kv)
    spread = prefetched(
        product_kernel,
        1,
        jax.ShapeDtypeStruct((replicas, lines, 2, HB // replicas, 2 * HD), low),
        scratch=input_scratch,
        in_place=widths - 1,
    )(
        jnp.stack([core, lax.axis_index("tensor")]),
        *other_list,
        first_product,
        other_kv,
        hadamard_signs(HB),
        recv[:, AUX_AT:ROWS],
    )
    spread = spread.reshape(replicas * lines, 2, HB // replicas, 2 * HD)
    shares = lax.all_to_all(spread, ("dp", "y"), split_axis=0, concat_axis=0, tiled=True)
    return jnp.sum(shares.astype(jnp.float32), axis=0)


def solution(mesh):
    replicas, groups, widths = mesh.devices.shape
    split = Mesh(
        mesh.devices.reshape(replicas, groups // CORES, CORES, widths),
        ("dp", "y", "core", "tensor"),
    )
    context = ("y", "core")
    return jax.shard_map(
        per_device,
        mesh=split,
        in_specs=(
            P("dp", context, "tensor"),
            P("dp", "tensor", context, None),
            P("dp", "tensor", context, None),
            P("dp", "tensor", context, None),
            P("dp", "tensor", context, None),
            P("dp", "tensor", context),
            P("dp", "tensor", context),
            P("dp", None),
            P("dp", None),
            P(context, None),
            P("dp", context),
        ),
        out_specs=P(context, "dp", "tensor"),
        check_vma=False,
    )
```

```python
import functools

import jax
import jax.numpy as jnp
from jax import lax
from jax.experimental import pallas as pl
from jax.experimental.pallas import tpu as pltpu
from jax.sharding import Mesh
from jax.sharding import PartitionSpec as P

HD = 128
GROUP = 4
BLK = 32
PAD = 128
HB = 128
CORES = 2
SPAN = 3
SENT = (0, 2)
LOG2E = 1.4426950408889634

QROWS = GROUP * BLK
KV_AT = 2 * QROWS
AUX_AT = KV_AT + len(SENT) * 2 * BLK
AUX_ROWS = 8
ROWS = AUX_AT + AUX_ROWS
UNIT_BLKS = PAD // BLK
HOPS = (0, 1, 3, 2)


def hadamard_signs(table_size):
    index_row = jnp.arange(table_size, dtype=jnp.int32)
    common = jnp.bitwise_and(index_row[:, None], index_row[None, :])
    parity = jnp.zeros((table_size, table_size), jnp.int32)
    for bit_pos in range(table_size.bit_length() - 1):
        parity = parity + jnp.bitwise_and(jnp.right_shift(common, bit_pos), 1)
    return (1 - 2 * jnp.bitwise_and(parity, 1)).astype(jnp.bfloat16)


def pack_kernel(where_ref, *refs):
    (query_ref, grad_ref, key_ref, value_ref, lse_ref, dots_ref, sign_ref), refs = refs[:7], refs[7:]
    order_ref, exponent_ref, out_ref = refs[:3]
    query_scr, grad_scr, key_scr, value_scr, lse_scr, dots_scr, sign_scr = refs[3:10]
    order_scr, exponent_scr, held_scr, aux_scr, packed_scr, in_sem, out_sem = refs[10:]
    sources = (order_ref, exponent_ref, lse_ref, dots_ref, sign_ref)
    sources += (key_ref, value_ref, query_ref, grad_ref)
    places = (order_scr, exponent_scr, lse_scr, dots_scr, sign_scr)
    places += (key_scr, value_scr, query_scr, grad_scr)
    loads = [
        pltpu.make_async_copy(source, place, in_sem.at[i])
        for i, (source, place) in enumerate(zip(sources, places))
    ]
    for load in loads:
        load.start()
    groups = out_ref.shape[0]
    slots = key_ref.shape[2] // BLK
    for load in loads[:5]:
        load.wait()
    first = where_ref[0] * slots
    for slot in range(slots):
        held_scr[order_scr[0, first + slot] // slots] = slot

    fixed = [sign_scr[...].astype(jnp.float32)]
    for blk in range(sign_ref.shape[0]):
        power = jnp.full((1, HD), jnp.left_shift(jnp.int32(1), exponent_scr[0, blk]), jnp.int32)
        fixed.append(1.0 / power.astype(jnp.float32))
    fixed.append(jnp.zeros((AUX_ROWS - 6, HD), jnp.float32))
    head_of = lax.broadcasted_iota(jnp.int32, (1, HD), 1) // BLK
    stats = (lse_scr[0].astype(jnp.float32), dots_scr[0].astype(jnp.float32))

    def by_head(array, slot):
        part = slot * BLK // HD * HD
        inner = slot % (HD // BLK)
        row = jnp.zeros((1, HD), jnp.float32)
        for head in range(GROUP):
            line = array[head : head + 1, part : part + HD]
            turn = (head - inner) * BLK % HD
            line = pltpu.roll(line, turn, 1) if turn else line
            row = jnp.where(head_of == head, line, row)
        return row

    for slot in range(slots):
        aux = jnp.concatenate([by_head(array, slot) for array in stats] + fixed, axis=0)
        aux_scr[slot] = aux.astype(aux_scr.dtype)
    for load in loads[5:]:
        load.wait()

    stores = []
    for dest in range(groups):
        slot = held_scr[dest]
        rows = pl.ds(pl.multiple_of(slot * BLK, BLK), BLK)
        for head in range(GROUP):
            packed_scr[dest, head * BLK : (head + 1) * BLK, :] = query_scr[0, head, rows, :]
            at = QROWS + head * BLK
            packed_scr[dest, at : at + BLK, :] = grad_scr[0, head, rows, :]
        for place, span in enumerate(SENT):
            at = KV_AT + place * 2 * BLK
            if dest >= span:
                rows = pl.ds(pl.multiple_of(held_scr[dest - span] * BLK, BLK), BLK)
                packed_scr[dest, at : at + BLK, :] = key_scr[0, 0, rows, :]
                packed_scr[dest, at + BLK : at + 2 * BLK, :] = value_scr[0, 0, rows, :]
            else:
                packed_scr[dest, at : at + 2 * BLK, :] = jnp.zeros((2 * BLK, HD), out_ref.dtype)
        packed_scr[dest, AUX_AT:ROWS, :] = aux_scr[slot]
        stores.append(pltpu.make_async_copy(packed_scr.at[dest], out_ref.at[dest], out_sem.at[dest]))
        stores[-1].start()
    for store in stores:
        store.wait()


def block_grads(key_blk, value_blk, query_refs, cols, lse, dots, live):
    query_ref, grad_ref, query_turned, grad_turned = query_refs
    scores = jnp.dot(key_blk, query_turned[:, cols], preferred_element_type=jnp.float32)
    dprobs = jnp.dot(value_blk, grad_turned[:, cols], preferred_element_type=jnp.float32)
    probs = jnp.where(live, jnp.exp2(scores * (HD ** (-0.5) * LOG2E) - lse), 0.0)
    dscores = (probs * (dprobs - dots)).astype(jnp.bfloat16)
    value_part = jnp.dot(
        probs.astype(jnp.bfloat16), grad_ref[cols, :], preferred_element_type=jnp.float32
    )
    key_part = jnp.dot(dscores, query_ref[cols, :], preferred_element_type=jnp.float32)
    return key_part, value_part


def unit_stats(stat_ref, unit):
    blocks = range(unit * UNIT_BLKS, (unit + 1) * UNIT_BLKS)
    lse = jnp.concatenate([stat_ref[b, 0:1, :] for b in blocks], axis=1) * LOG2E
    dots = jnp.concatenate([stat_ref[b, 1:2, :] for b in blocks], axis=1)
    return lse, dots


def rows_of(slot_ref, span, src):
    return pl.ds(pl.multiple_of(slot_ref[span, src] * BLK, BLK), BLK)


def store_slab(slot_ref, span, dkey_scr, dvalue_scr, out_ref):
    for src in range(out_ref.shape[0]):
        rows = rows_of(slot_ref, span, src)
        dkey = dkey_scr[rows, :] * HD ** (-0.5)
        out_ref[src, 0:BLK, :] = dkey.astype(out_ref.dtype)
        out_ref[src, BLK : 2 * BLK, :] = dvalue_scr[rows, :].astype(out_ref.dtype)


def own_attend_kernel(
    slot_ref, start_ref, recv_ref,
    query_ref, grad_ref, query_turned, grad_turned, stat_ref, out_ref,
    key_scr, value_scr, dkey_scr, dvalue_scr,
):
    units = key_scr.shape[0] // PAD
    width = UNIT_BLKS * QROWS
    for src in range(recv_ref.shape[0]):
        slot = slot_ref[0, src]
        at = pl.multiple_of(slot * QROWS, QROWS)
        query_blk = recv_ref[src, 0:QROWS, :]
        grad_blk = recv_ref[src, QROWS : 2 * QROWS, :]
        query_ref[pl.ds(at, QROWS), :] = query_blk
        grad_ref[pl.ds(at, QROWS), :] = grad_blk
        query_turned[:, pl.ds(at, QROWS)] = query_blk.T
        grad_turned[:, pl.ds(at, QROWS)] = grad_blk.T
        stat_ref[slot] = recv_ref[src, AUX_AT:ROWS, :].astype(jnp.float32)
        rows = rows_of(slot_ref, 0, src)
        key_scr[rows, :] = recv_ref[src, KV_AT : KV_AT + BLK, :]
        value_scr[rows, :] = recv_ref[src, KV_AT + BLK : KV_AT + 2 * BLK, :]

    queries = (query_ref, grad_ref, query_turned, grad_turned)
    dkey_scr[...] = jnp.zeros_like(dkey_scr)
    dvalue_scr[...] = jnp.zeros_like(dvalue_scr)
    for unit in range(units):
        rows = slice(0, (unit + 1) * PAD)
        cols = slice(unit * width, (unit + 1) * width)
        lse, dots = unit_stats(stat_ref, unit)
        key_at = lax.broadcasted_iota(jnp.int32, (rows.stop, width), 0)
        column = lax.broadcasted_iota(jnp.int32, (rows.stop, width), 1)
        query_at = unit * PAD + (column // QROWS) * BLK + column % BLK
        first = (start_ref[unit] - (SPAN - 1) * units) * PAD
        live = (key_at <= query_at) & (key_at >= first)
        key_part, value_part = block_grads(
            key_scr[rows, :], value_scr[rows, :], queries, cols, lse, dots, live
        )
        dkey_scr[rows, :] += key_part
        dvalue_scr[rows, :] += value_part
    store_slab(slot_ref, 0, dkey_scr, dvalue_scr, out_ref)


def earlier_attend_kernel(span, slot_ref, start_ref, kv_ref, *refs):
    queries, refs = refs[:4], refs[4:]
    stat_ref, out_ref, key_scr, value_scr, dkey_scr, dvalue_scr = refs
    units = key_scr.shape[0] // PAD
    width = UNIT_BLKS * QROWS
    pair = 2 * PAD
    for src in range(kv_ref.shape[0]):
        rows = rows_of(slot_ref, span, src)
        key_scr[rows, :] = kv_ref[src, 0:BLK, :]
        value_scr[rows, :] = kv_ref[src, BLK : 2 * BLK, :]
    dkey_scr[...] = jnp.zeros_like(dkey_scr)
    dvalue_scr[...] = jnp.zeros_like(dvalue_scr)
    key_at = lax.broadcasted_iota(jnp.int32, (pair, width), 0)
    for unit in range(units):
        cols = slice(unit * width, (unit + 1) * width)
        lse, dots = unit_stats(stat_ref, unit)
        first = jnp.clip(start_ref[unit] - (SPAN - 1 - span) * units, 0, units)

        @pl.loop(0, (units - first + 1) // 2)
        def _(step):
            base = units - 2 - 2 * step
            rows = pl.ds(pl.multiple_of(base * PAD, pair), pair)
            key_part, value_part = block_grads(
                key_scr[rows, :],
                value_scr[rows, :],
                queries,
                cols,
                lse,
                dots,
                key_at >= (first - base) * PAD,
            )
            dkey_scr[rows, :] += key_part
            dvalue_scr[rows, :] += value_part

    store_slab(slot_ref, span, dkey_scr, dvalue_scr, out_ref)


def merge_kernel(core_ref, own_ref, far_ref, shared_ref, out_ref):
    core = core_ref[0]
    for src in range(out_ref.shape[0]):
        shared = shared_ref[src].astype(jnp.float32)
        own = own_ref[src] + jnp.where(core == 0, shared, 0.0)
        far = far_ref[src] + jnp.where(core == 0, 0.0, shared)
        out_ref[src, 0] = own.astype(out_ref.dtype)
        out_ref[src, 1] = far.astype(out_ref.dtype)


def collect_kernel(target_ref, recv_ref, aux_ref, out_ref):
    groups = recv_ref.shape[0]
    tokens = out_ref.shape[0] - groups
    for blk in range(2):
        factors = [aux_ref[i].astype(jnp.float32)[4 + blk : 5 + blk, :] for i in range(groups)]
        factors = jnp.concatenate(factors, axis=0).astype(out_ref.dtype)
        out_ref[tokens:, blk * HD : (blk + 1) * HD] = factors
    for slot in range(tokens // BLK):
        owner = target_ref[slot]
        total = recv_ref[owner, 0].astype(jnp.float32)
        later = owner + SENT[1]
        extra = recv_ref[jnp.minimum(later, groups - 1), 1].astype(jnp.float32)
        total = total + jnp.where(later < groups, extra, 0.0)
        rows = slice(slot * BLK, (slot + 1) * BLK)
        total = total.astype(out_ref.dtype)
        out_ref[rows, 0:HD] = total[0:BLK]
        out_ref[rows, HD : 2 * HD] = total[BLK : 2 * BLK]


def turn_kernel(where_ref, input_ref, keep_ref, core_ref, line_ref):
    core, half = where_ref[0], where_ref[1]
    rows = keep_ref.shape[0] // 2
    places = (
        (keep_ref, 0, core, half),
        (core_ref, 0, 1 - core, half),
        (line_ref, 0, core, 1 - half),
        (line_ref, 2 * rows, 1 - core, 1 - half),
    )
    for ref, start, parity, blk in places:
        for part in range(2):
            at = pl.multiple_of((CORES * part + parity) * 2 * HB + blk * HB, HB)
            begin = start + part * rows
            ref[begin : begin + rows, :] = input_ref[:, pl.ds(at, HB)].T


def load_all(sources, places, sems):
    loads = [
        pltpu.make_async_copy(source, places.at[i], sems.at[i]) for i, source in enumerate(sources)
    ]
    for load in loads:
        load.start()
    return loads


def paired_products(refs, far_ref, kv_refs, input_scr, sems):
    loads = load_all(refs, input_scr, sems)
    for step in (len(loads), *range(len(loads))):
        if step < len(loads):
            loads[step].wait()
            inputs = input_scr[step]
        else:
            inputs = far_ref[...]
        half, tokens = inputs.shape[0] // 2, inputs.shape[1]
        grad = jnp.dot(inputs[:half], kv_refs[0][:tokens], preferred_element_type=jnp.float32)
        grad += jnp.dot(inputs[half:], kv_refs[1][:tokens], preferred_element_type=jnp.float32)
        yield step, grad


def first_product_kernel(*refs):
    far_ref, own_ref, other_ref, out_ref, input_scr, sems = refs[-6:]
    kv_refs = (own_ref, other_ref)
    for step, grad in paired_products(refs[:-6], far_ref, kv_refs, input_scr, sems):
        out_ref[step] = grad


def product_kernel(where_ref, *refs):
    far_ref, own_ref, other_ref, first_ref, had_ref, aux_ref = refs[-9:-3]
    out_ref, input_scr, sems = refs[-3:]
    core, half, width = where_ref[0], where_ref[1], where_ref[2]
    replicas = out_ref.shape[0]
    had = jnp.concatenate([had_ref[...].astype(jnp.float32)] * 2, axis=1)
    widths = len(HOPS)
    kv_refs = (own_ref, other_ref)
    tokens = input_scr.shape[2]
    paired_factors = own_ref[tokens:, :].astype(jnp.float32)
    paired_factors = jnp.where(half == 0, paired_factors[:, :HD], paired_factors[:, HD:])
    context_of = lax.broadcasted_iota(jnp.int32, paired_factors.shape, 0)

    def chosen(aux, at):
        return jnp.where(half == 0, aux[at : at + 1, :], aux[at + 1 : at + 2, :])

    for step, grad in paired_products(refs[:-9], far_ref, kv_refs, input_scr, sems):
        source = (width + widths - HOPS[step]) % widths
        for part in range(2):
            line = source * 2 + part
            aux = aux_ref[CORES * line + core].astype(jnp.float32)
            mine = context_of == CORES * line + core
            paired = jnp.sum(jnp.where(mine, paired_factors, 0.0), axis=0, keepdims=True)
            at = slice(part * HB, (part + 1) * HB)
            factor, paired = [
                jnp.concatenate([row * HB ** (-0.5)] * 2, axis=1)
                for row in (chosen(aux, 4), paired)
            ]
            rows = first_ref[step, at] * factor + grad[at] * paired
            sign = chosen(aux, 2)
            table = (had * jnp.concatenate([sign, sign], axis=1)).astype(jnp.bfloat16)
            high = rows.astype(jnp.bfloat16)
            low = (rows - high.astype(jnp.float32)).astype(jnp.bfloat16)
            both = jnp.concatenate([high, low], axis=0)
            rotated = jnp.dot(table, both, preferred_element_type=jnp.float32)
            out_ref[:, line] = rotated.astype(out_ref.dtype).reshape(
                replicas, HB // replicas, rows.shape[1]
            )


def prefetched(kernel, scalars, out_shape, scratch=(), in_place=0, out_space=pltpu.VMEM):
    vmem = pl.BlockSpec(memory_space=pltpu.VMEM)
    hbm = pl.BlockSpec(memory_space=pltpu.HBM)
    out_spec = pl.BlockSpec(memory_space=out_space)

    def call(*operands):
        held = scalars + in_place
        kept = [
            pltpu.with_memory_space_constraint(array, pltpu.HBM)
            for array in operands[scalars:held]
        ]
        return pl.pallas_call(
            kernel,
            out_shape=out_shape,
            grid_spec=pltpu.PrefetchScalarGridSpec(
                num_scalar_prefetch=scalars,
                in_specs=[hbm] * in_place + [vmem] * (len(operands) - held),
                out_specs=jax.tree.map(lambda _: out_spec, out_shape),
                scratch_shapes=list(scratch),
            ),
            compiler_params=pltpu.CompilerParams(vmem_limit_bytes=16 << 20),
        )(*operands[:scalars], *kept, *operands[held:])

    return call


def around(count, step):
    return [(i, (i + step) % count) for i in range(count)]


def per_device(
    layer_input,
    queries,
    key_states,
    value_states,
    out_grad,
    log_sums,
    grad_dots,
    doc_stretches,
    stretch_order,
    sign_vector,
    exponents,
):
    context = ("y", "core")
    low = jnp.bfloat16
    tokens = queries.shape[2]
    slots = tokens // BLK
    groups = lax.axis_size(context)
    lines = lax.axis_size("y")
    sequences = ("zh", "zl")
    replicas = lax.axis_size(sequences)
    order_row = stretch_order[0]
    where = lax.axis_index(context)
    core, half = lax.axis_index("core"), lax.axis_index("zl")

    raw = (queries, out_grad, key_states, value_states, log_sums, grad_dots, sign_vector)
    packed = prefetched(
        pack_kernel,
        1,
        pltpu.HBM((groups, ROWS, HD), low),
        scratch=(
            *(pltpu.VMEM(array.shape, array.dtype) for array in raw),
            pltpu.SMEM(stretch_order.shape, jnp.int32),
            pltpu.SMEM(exponents.shape, jnp.int32),
            pltpu.SMEM((groups,), jnp.int32),
            pltpu.VMEM((slots, AUX_ROWS, HD), low),
            pltpu.VMEM((groups, ROWS, HD), low),
            pltpu.SemaphoreType.DMA((9,)),
            pltpu.SemaphoreType.DMA((groups,)),
        ),
        in_place=len(raw) + 2,
        out_space=pltpu.HBM,
    )(where.reshape(1), *raw, stretch_order, exponents)
    packed, layer_input = lax.optimization_barrier((packed, layer_input))
    recv = lax.all_to_all(packed, context, split_axis=0, concat_axis=0, tiled=True)

    swap = [(0, 1), (1, 0)]
    piece = layer_input.shape[2] // (2 * CORES)
    keep, to_core, to_line = prefetched(
        turn_kernel,
        1,
        tuple(jax.ShapeDtypeStruct((rows, tokens), low) for rows in (piece, piece, 2 * piece)),
    )(jnp.stack([core, half]), layer_input[0])
    from_line = lax.ppermute(to_line, "zl", swap)
    own_input = jnp.concatenate([keep, lax.ppermute(to_core, "core", swap)], axis=0)
    diagonal = lax.ppermute(from_line[piece:], "core", swap)
    other_input = jnp.concatenate([from_line[:piece], diagonal], axis=0)
    widths = lax.axis_size("tensor")
    up, down = around(widths, 1), around(widths, -1)
    near = [
        lax.ppermute(array, "tensor", way)
        for array in (own_input, other_input)
        for way in (up, down)
    ]
    recv, near = lax.optimization_barrier((recv, near))

    order_grid = order_row.reshape(groups, slots)
    chunk_ids = (where - jnp.arange(SPAN, dtype=jnp.int32))[:, None, None]
    slot_map = jnp.sum(
        jnp.where(order_grid[None] // slots == chunk_ids, order_grid[None] % slots, 0), axis=2
    )
    ends = jnp.cumsum(doc_stretches[0])
    chunk_units = tokens // PAD
    unit_ids = where * chunk_units + jnp.arange(chunk_units, dtype=jnp.int32)
    doc_start = jnp.max(jnp.where(ends[None, :] <= unit_ids[:, None], ends[None, :], 0), axis=1)
    starts = doc_start - (where - (SPAN - 1)) * chunk_units

    at = KV_AT + lax.axis_index("core") * 2 * BLK
    shared_kv = lax.ppermute(lax.dynamic_slice_in_dim(recv, at, 2 * BLK, 1), "core", swap)
    sorted_rows = jax.ShapeDtypeStruct((slots * QROWS, HD), low)
    turned_rows = jax.ShapeDtypeStruct((HD, slots * QROWS), low)
    slab = (groups, 2 * BLK, HD)
    chunk_scratch = tuple(
        pltpu.VMEM((tokens, HD), dtype) for dtype in (low, low, jnp.float32, jnp.float32)
    )
    *shared_work, own_slab = prefetched(
        own_attend_kernel,
        2,
        (
            sorted_rows,
            sorted_rows,
            turned_rows,
            turned_rows,
            jax.ShapeDtypeStruct((slots, AUX_ROWS, HD), jnp.float32),
            jax.ShapeDtypeStruct(slab, jnp.float32),
        ),
        scratch=chunk_scratch,
    )(slot_map, starts, recv)
    before_slab = prefetched(
        functools.partial(earlier_attend_kernel, 1),
        2,
        jax.ShapeDtypeStruct(slab, low),
        scratch=chunk_scratch,
    )(slot_map, starts, shared_kv, *shared_work)
    shared_slab = lax.ppermute(before_slab, "core", swap)
    far_slab = prefetched(
        functools.partial(earlier_attend_kernel, 2),
        2,
        jax.ShapeDtypeStruct(slab, jnp.float32),
        scratch=chunk_scratch,
    )(slot_map, starts, recv[:, KV_AT + 2 * BLK : AUX_AT], *shared_work)
    partial_grads = prefetched(
        merge_kernel, 1, jax.ShapeDtypeStruct((groups, len(SENT), 2 * BLK, HD), low)
    )(core.reshape(1), own_slab, far_slab, shared_slab)
    partial_grads, near = lax.optimization_barrier((partial_grads, near))
    own_up, own_down, other_up, other_down = near
    own_far = lax.ppermute(own_up, "tensor", up)
    other_far = lax.ppermute(other_down, "tensor", down)
    returned = lax.all_to_all(partial_grads, context, split_axis=0, concat_axis=0, tiled=True)
    returned, own_far, other_far = lax.optimization_barrier((returned, own_far, other_far))
    own_list = [own_input, own_up, own_down, own_far]
    other_list = [other_input, other_up, other_down, other_far]
    targets = lax.dynamic_slice_in_dim(order_row, where * slots, slots, 0) // slots
    aux = recv[:, AUX_AT:ROWS]
    own_kv = prefetched(collect_kernel, 1, jax.ShapeDtypeStruct((tokens + groups, 2 * HD), low))(
        targets, returned, aux
    )
    line_kv = lax.ppermute(own_kv, "zl", swap)
    core_kv = lax.ppermute(own_kv, "core", swap)

    input_scratch = (
        pltpu.VMEM((widths - 1, 2 * piece, tokens), low),
        pltpu.SemaphoreType.DMA((widths - 1,)),
    )
    first_product = prefetched(
        first_product_kernel,
        0,
        jax.ShapeDtypeStruct((widths, piece, 2 * HD), jnp.float32),
        scratch=input_scratch,
        in_place=widths - 1,
    )(*own_list, own_kv, core_kv)
    diagonal_kv = lax.ppermute(line_kv, "core", swap)
    spread = prefetched(
        product_kernel,
        1,
        jax.ShapeDtypeStruct((replicas, lines, HB // replicas, 2 * HD), low),
        scratch=input_scratch,
        in_place=widths - 1,
    )(
        jnp.stack([core, half, lax.axis_index("tensor")]),
        *other_list,
        line_kv,
        diagonal_kv,
        first_product,
        hadamard_signs(HB),
        aux,
    )
    spread = spread.reshape(replicas * lines, HB // replicas, 2 * HD)
    shares = lax.all_to_all(spread, (*sequences, "y"), split_axis=0, concat_axis=0, tiled=True)
    shares = shares.reshape(replicas // 2, 2, lines, HB // replicas, 2 * HD)
    return jnp.sum(shares.astype(jnp.float32), axis=(0, 2))


def solution(mesh):
    replicas, groups, widths = mesh.devices.shape
    split = Mesh(
        mesh.devices.reshape(replicas // 2, 2, groups // CORES, CORES, widths),
        ("zh", "zl", "y", "core", "tensor"),
    )
    context = ("y", "core")
    sequences = ("zh", "zl")
    return jax.shard_map(
        per_device,
        mesh=split,
        in_specs=(
            P(sequences, context, "tensor"),
            P(sequences, "tensor", context, None),
            P(sequences, "tensor", context, None),
            P(sequences, "tensor", context, None),
            P(sequences, "tensor", context, None),
            P(sequences, "tensor", context),
            P(sequences, "tensor", context),
            P(sequences, None),
            P(sequences, None),
            P(context, None),
            P(sequences, context),
        ),
        out_specs=P(context, sequences, "tensor"),
        check_vma=False,
    )
```

```python
import functools

import jax
import jax.numpy as jnp
from jax import lax
from jax.experimental import pallas as pl
from jax.experimental.pallas import tpu as pltpu
from jax.sharding import Mesh
from jax.sharding import PartitionSpec as P

HD = 128
GROUP = 4
BLK = 32
PAD = 128
HB = 128
CORES = 2
SPAN = 3
SENT = (0, 2)
LOG2E = 1.4426950408889634

QROWS = GROUP * BLK
KV_AT = 2 * QROWS
AUX_AT = KV_AT + len(SENT) * 2 * BLK
AUX_ROWS = 8
ROWS = AUX_AT + AUX_ROWS
UNIT_BLKS = PAD // BLK
HOPS = (0, 1, 3, 2)


def hadamard_signs(table_size):
    index_row = jnp.arange(table_size, dtype=jnp.int32)
    common = jnp.bitwise_and(index_row[:, None], index_row[None, :])
    parity = jnp.zeros((table_size, table_size), jnp.int32)
    for bit_pos in range(table_size.bit_length() - 1):
        parity = parity + jnp.bitwise_and(jnp.right_shift(common, bit_pos), 1)
    return (1 - 2 * jnp.bitwise_and(parity, 1)).astype(jnp.bfloat16)


def pack_kernel(where_ref, *refs):
    (query_ref, grad_ref, key_ref, value_ref, lse_ref, dots_ref, sign_ref), refs = refs[:7], refs[7:]
    order_ref, exponent_ref, out_ref = refs[:3]
    query_scr, grad_scr, key_scr, value_scr, lse_scr, dots_scr, sign_scr = refs[3:10]
    order_scr, exponent_scr, held_scr, aux_scr, packed_scr, in_sem, out_sem = refs[10:]
    sources = (order_ref, exponent_ref, lse_ref, dots_ref, sign_ref)
    sources += (key_ref, value_ref, query_ref, grad_ref)
    places = (order_scr, exponent_scr, lse_scr, dots_scr, sign_scr)
    places += (key_scr, value_scr, query_scr, grad_scr)
    loads = [
        pltpu.make_async_copy(source, place, in_sem.at[i])
        for i, (source, place) in enumerate(zip(sources, places))
    ]
    for load in loads:
        load.start()
    groups = out_ref.shape[0]
    slots = key_ref.shape[2] // BLK
    for load in loads[:5]:
        load.wait()
    first = where_ref[0] * slots
    for slot in range(slots):
        held_scr[order_scr[0, first + slot] // slots] = slot

    fixed = [sign_scr[...].astype(jnp.float32)]
    for blk in range(sign_ref.shape[0]):
        power = jnp.full((1, HD), jnp.left_shift(jnp.int32(1), exponent_scr[0, blk]), jnp.int32)
        fixed.append(1.0 / power.astype(jnp.float32))
    fixed.append(jnp.zeros((AUX_ROWS - 6, HD), jnp.float32))
    head_of = lax.broadcasted_iota(jnp.int32, (1, HD), 1) // BLK
    stats = (lse_scr[0].astype(jnp.float32), dots_scr[0].astype(jnp.float32))

    def by_head(array, slot):
        part = slot * BLK // HD * HD
        inner = slot % (HD // BLK)
        row = jnp.zeros((1, HD), jnp.float32)
        for head in range(GROUP):
            line = array[head : head + 1, part : part + HD]
            turn = (head - inner) * BLK % HD
            line = pltpu.roll(line, turn, 1) if turn else line
            row = jnp.where(head_of == head, line, row)
        return row

    for slot in range(slots):
        aux = jnp.concatenate([by_head(array, slot) for array in stats] + fixed, axis=0)
        aux_scr[slot] = aux.astype(aux_scr.dtype)
    for load in loads[5:]:
        load.wait()

    stores = []
    for dest in range(groups):
        slot = held_scr[dest]
        rows = pl.ds(pl.multiple_of(slot * BLK, BLK), BLK)
        for head in range(GROUP):
            packed_scr[dest, head * BLK : (head + 1) * BLK, :] = query_scr[0, head, rows, :]
            at = QROWS + head * BLK
            packed_scr[dest, at : at + BLK, :] = grad_scr[0, head, rows, :]
        for place, span in enumerate(SENT):
            at = KV_AT + place * 2 * BLK
            if dest >= span:
                rows = pl.ds(pl.multiple_of(held_scr[dest - span] * BLK, BLK), BLK)
                packed_scr[dest, at : at + BLK, :] = key_scr[0, 0, rows, :]
                packed_scr[dest, at + BLK : at + 2 * BLK, :] = value_scr[0, 0, rows, :]
            else:
                packed_scr[dest, at : at + 2 * BLK, :] = jnp.zeros((2 * BLK, HD), out_ref.dtype)
        packed_scr[dest, AUX_AT:ROWS, :] = aux_scr[slot]
        stores.append(pltpu.make_async_copy(packed_scr.at[dest], out_ref.at[dest], out_sem.at[dest]))
        stores[-1].start()
    for store in stores:
        store.wait()


def block_grads(key_blk, value_blk, query_refs, cols, lse, dots, inside, causal=None):
    query_ref, grad_ref, query_turned, grad_turned = query_refs
    scores = jnp.dot(key_blk, query_turned[:, cols], preferred_element_type=jnp.float32)
    dprobs = jnp.dot(value_blk, grad_turned[:, cols], preferred_element_type=jnp.float32)
    probs = jnp.exp2(scores * (HD ** (-0.5) * LOG2E) - lse)
    if causal is not None:
        before = probs.shape[0] - causal.shape[0]
        diagonal = jnp.where(causal, probs[before:], 0.0)
        probs = jnp.concatenate([probs[:before], diagonal], axis=0) if before else diagonal
    dscores = (probs * (dprobs - dots)).astype(jnp.bfloat16)
    value_part = jnp.dot(
        probs.astype(jnp.bfloat16), grad_ref[cols, :], preferred_element_type=jnp.float32
    )
    key_part = jnp.dot(dscores, query_ref[cols, :], preferred_element_type=jnp.float32)
    return jnp.where(inside, key_part, 0.0), jnp.where(inside, value_part, 0.0)


def unit_stats(stat_ref, unit):
    blocks = range(unit * UNIT_BLKS, (unit + 1) * UNIT_BLKS)
    lse = jnp.concatenate([stat_ref[b, 0:1, :] for b in blocks], axis=1) * LOG2E
    dots = jnp.concatenate([stat_ref[b, 1:2, :] for b in blocks], axis=1)
    return lse, dots


def rows_of(slot_ref, span, src):
    return pl.ds(pl.multiple_of(slot_ref[span, src] * BLK, BLK), BLK)


def store_slab(slot_ref, span, dkey_scr, dvalue_scr, out_ref):
    for src in range(out_ref.shape[0]):
        rows = rows_of(slot_ref, span, src)
        dkey = dkey_scr[rows, :] * HD ** (-0.5)
        out_ref[src, 0:BLK, :] = dkey.astype(out_ref.dtype)
        out_ref[src, BLK : 2 * BLK, :] = dvalue_scr[rows, :].astype(out_ref.dtype)


def own_attend_kernel(
    slot_ref, start_ref, recv_ref,
    query_ref, grad_ref, query_turned, grad_turned, stat_ref, out_ref,
    key_scr, value_scr, dkey_scr, dvalue_scr,
):
    units = key_scr.shape[0] // PAD
    width = UNIT_BLKS * QROWS
    for src in range(recv_ref.shape[0]):
        slot = slot_ref[0, src]
        at = pl.multiple_of(slot * QROWS, QROWS)
        query_blk = recv_ref[src, 0:QROWS, :]
        grad_blk = recv_ref[src, QROWS : 2 * QROWS, :]
        query_ref[pl.ds(at, QROWS), :] = query_blk
        grad_ref[pl.ds(at, QROWS), :] = grad_blk
        query_turned[:, pl.ds(at, QROWS)] = query_blk.T
        grad_turned[:, pl.ds(at, QROWS)] = grad_blk.T
        stat_ref[slot] = recv_ref[src, AUX_AT:ROWS, :].astype(jnp.float32)
        rows = rows_of(slot_ref, 0, src)
        key_scr[rows, :] = recv_ref[src, KV_AT : KV_AT + BLK, :]
        value_scr[rows, :] = recv_ref[src, KV_AT + BLK : KV_AT + 2 * BLK, :]

    queries = (query_ref, grad_ref, query_turned, grad_turned)
    dkey_scr[...] = jnp.zeros_like(dkey_scr)
    dvalue_scr[...] = jnp.zeros_like(dvalue_scr)
    key_at = lax.broadcasted_iota(jnp.int32, (PAD, width), 0)
    column = lax.broadcasted_iota(jnp.int32, (PAD, width), 1)
    causal = key_at <= (column // QROWS) * BLK + column % BLK
    for unit in range(units):
        rows = slice(0, (unit + 1) * PAD)
        cols = slice(unit * width, (unit + 1) * width)
        lse, dots = unit_stats(stat_ref, unit)
        first = (start_ref[unit] - (SPAN - 1) * units) * PAD
        inside = lax.broadcasted_iota(jnp.int32, (rows.stop, HD), 0) >= first
        key_part, value_part = block_grads(
            key_scr[rows, :], value_scr[rows, :], queries, cols, lse, dots, inside, causal
        )
        dkey_scr[rows, :] += key_part
        dvalue_scr[rows, :] += value_part
    store_slab(slot_ref, 0, dkey_scr, dvalue_scr, out_ref)


def earlier_attend_kernel(span, slot_ref, start_ref, kv_ref, *refs):
    queries, refs = refs[:4], refs[4:]
    stat_ref, out_ref, key_scr, value_scr, dkey_scr, dvalue_scr = refs
    units = key_scr.shape[0] // PAD
    width = UNIT_BLKS * QROWS
    pair = 2 * PAD
    for src in range(kv_ref.shape[0]):
        rows = rows_of(slot_ref, span, src)
        key_scr[rows, :] = kv_ref[src, 0:BLK, :]
        value_scr[rows, :] = kv_ref[src, BLK : 2 * BLK, :]
    dkey_scr[...] = jnp.zeros_like(dkey_scr)
    dvalue_scr[...] = jnp.zeros_like(dvalue_scr)
    key_at = lax.broadcasted_iota(jnp.int32, (pair, HD), 0)
    for unit in range(units):
        cols = slice(unit * width, (unit + 1) * width)
        lse, dots = unit_stats(stat_ref, unit)
        first = jnp.clip(start_ref[unit] - (SPAN - 1 - span) * units, 0, units)

        @pl.loop(0, (units - first + 1) // 2)
        def _(step):
            base = units - 2 - 2 * step
            rows = pl.ds(pl.multiple_of(base * PAD, pair), pair)
            key_part, value_part = block_grads(
                key_scr[rows, :],
                value_scr[rows, :],
                queries,
                cols,
                lse,
                dots,
                key_at >= (first - base) * PAD,
            )
            dkey_scr[rows, :] += key_part
            dvalue_scr[rows, :] += value_part

    store_slab(slot_ref, span, dkey_scr, dvalue_scr, out_ref)


def merge_kernel(core_ref, own_ref, far_ref, shared_ref, out_ref):
    core = core_ref[0]
    for src in range(out_ref.shape[0]):
        shared = shared_ref[src].astype(jnp.float32)
        own = own_ref[src] + jnp.where(core == 0, shared, 0.0)
        far = far_ref[src] + jnp.where(core == 0, 0.0, shared)
        out_ref[src, 0] = own.astype(out_ref.dtype)
        out_ref[src, 1] = far.astype(out_ref.dtype)


def collect_kernel(target_ref, recv_ref, out_ref):
    groups = recv_ref.shape[0]
    for slot in range(out_ref.shape[0] // BLK):
        owner = target_ref[slot]
        total = recv_ref[owner, 0].astype(jnp.float32)
        later = owner + SENT[1]
        extra = recv_ref[jnp.minimum(later, groups - 1), 1].astype(jnp.float32)
        total = total + jnp.where(later < groups, extra, 0.0)
        rows = slice(slot * BLK, (slot + 1) * BLK)
        total = total.astype(out_ref.dtype)
        out_ref[rows, 0:HD] = total[0:BLK]
        out_ref[rows, HD : 2 * HD] = total[BLK : 2 * BLK]


def turn_kernel(core_ref, input_ref, own_ref, other_ref):
    span = 2 * HB
    core = core_ref[0]
    for part in range(own_ref.shape[0] // span):
        rows = slice(part * span, (part + 1) * span)
        at = pl.multiple_of((CORES * part + core) * span, span)
        own_ref[rows, :] = input_ref[:, pl.ds(at, span)].T
        at = pl.multiple_of((CORES * part + 1 - core) * span, span)
        other_ref[rows, :] = input_ref[:, pl.ds(at, span)].T


def load_all(sources, places, sems):
    loads = [
        pltpu.make_async_copy(source, places.at[i], sems.at[i]) for i, source in enumerate(sources)
    ]
    for load in loads:
        load.start()
    return loads


def first_product_kernel(*refs):
    far_ref, kv_ref, out_ref, input_scr, sems = refs[-5:]
    loads = load_all(refs[:-5], input_scr, sems)
    last = len(loads)
    out_ref[last] = jnp.dot(far_ref[...], kv_ref[...], preferred_element_type=jnp.float32)
    for step, load in enumerate(loads):
        load.wait()
        out_ref[step] = jnp.dot(input_scr[step], kv_ref[...], preferred_element_type=jnp.float32)


def product_kernel(where_ref, *refs):
    far_ref, first_ref, kv_ref, had_ref, aux_ref, out_ref, input_scr, sems = refs[-8:]
    loads = load_all(refs[:-8], input_scr, sems)
    core, width = where_ref[0], where_ref[1]
    replicas = out_ref.shape[0]
    span = 2 * HB
    parts = far_ref.shape[0] // span
    had = jnp.concatenate([had_ref[...].astype(jnp.float32)] * 2, axis=1)
    widths = len(HOPS)
    for step in (widths - 1, *range(widths - 1)):
        source = (width + widths - HOPS[step]) % widths
        if step < len(loads):
            loads[step].wait()
            inputs = input_scr[step]
        else:
            inputs = far_ref[...]
        grad = jnp.dot(inputs, kv_ref[...], preferred_element_type=jnp.float32)
        grad = grad + first_ref[step]
        for part in range(parts):
            line = source * parts + part
            aux = aux_ref[CORES * line + core].astype(jnp.float32)
            for blk in range(2):
                at = part * span + blk * HB
                rows = grad[at : at + HB]
                sign = aux[2 + blk : 3 + blk, :]
                table = (had * jnp.concatenate([sign, sign], axis=1)).astype(jnp.bfloat16)
                high = rows.astype(jnp.bfloat16)
                low = (rows - high.astype(jnp.float32)).astype(jnp.bfloat16)
                both = jnp.concatenate([high, low], axis=0)
                rotated = jnp.dot(table, both, preferred_element_type=jnp.float32)
                factor = aux[4 + blk : 5 + blk, :] * (HB ** (-0.5))
                rotated *= jnp.concatenate([factor] * (rows.shape[1] // HB), axis=1)
                out_ref[:, line, blk] = rotated.astype(out_ref.dtype).reshape(
                    replicas, HB // replicas, rows.shape[1]
                )


def prefetched(kernel, scalars, out_shape, scratch=(), in_place=0, out_space=pltpu.VMEM):
    vmem = pl.BlockSpec(memory_space=pltpu.VMEM)
    hbm = pl.BlockSpec(memory_space=pltpu.HBM)
    out_spec = pl.BlockSpec(memory_space=out_space)

    def call(*operands):
        held = scalars + in_place
        kept = [
            pltpu.with_memory_space_constraint(array, pltpu.HBM)
            for array in operands[scalars:held]
        ]
        return pl.pallas_call(
            kernel,
            out_shape=out_shape,
            grid_spec=pltpu.PrefetchScalarGridSpec(
                num_scalar_prefetch=scalars,
                in_specs=[hbm] * in_place + [vmem] * (len(operands) - held),
                out_specs=jax.tree.map(lambda _: out_spec, out_shape),
                scratch_shapes=list(scratch),
            ),
            compiler_params=pltpu.CompilerParams(vmem_limit_bytes=16 << 20),
        )(*operands[:scalars], *kept, *operands[held:])

    return call


def around(count, step):
    return [(i, (i + step) % count) for i in range(count)]


def per_device(
    layer_input,
    queries,
    key_states,
    value_states,
    out_grad,
    log_sums,
    grad_dots,
    doc_stretches,
    stretch_order,
    sign_vector,
    exponents,
):
    context = ("y", "core")
    low = jnp.bfloat16
    tokens = queries.shape[2]
    slots = tokens // BLK
    groups = lax.axis_size(context)
    lines = lax.axis_size("y")
    replicas = lax.axis_size("dp")
    order_row = stretch_order[0]
    where = lax.axis_index(context)
    core = lax.axis_index("core")

    raw = (queries, out_grad, key_states, value_states, log_sums, grad_dots, sign_vector)
    packed = prefetched(
        pack_kernel,
        1,
        pltpu.HBM((groups, ROWS, HD), low),
        scratch=(
            *(pltpu.VMEM(array.shape, array.dtype) for array in raw),
            pltpu.SMEM(stretch_order.shape, jnp.int32),
            pltpu.SMEM(exponents.shape, jnp.int32),
            pltpu.SMEM((groups,), jnp.int32),
            pltpu.VMEM((slots, AUX_ROWS, HD), low),
            pltpu.VMEM((groups, ROWS, HD), low),
            pltpu.SemaphoreType.DMA((9,)),
            pltpu.SemaphoreType.DMA((groups,)),
        ),
        in_place=len(raw) + 2,
        out_space=pltpu.HBM,
    )(where.reshape(1), *raw, stretch_order, exponents)
    packed, layer_input = lax.optimization_barrier((packed, layer_input))
    recv = lax.all_to_all(packed, context, split_axis=0, concat_axis=0, tiled=True)

    half = layer_input.shape[2] // CORES
    turned = jax.ShapeDtypeStruct((half, tokens), low)
    own_input, other_input = prefetched(turn_kernel, 1, (turned, turned))(
        core.reshape(1), layer_input[0]
    )
    swap = [(0, 1), (1, 0)]
    other_input = lax.ppermute(other_input, "core", swap)
    widths = lax.axis_size("tensor")
    up, down = around(widths, 1), around(widths, -1)
    near = [
        lax.ppermute(array, "tensor", way)
        for array in (own_input, other_input)
        for way in (up, down)
    ]
    recv, near = lax.optimization_barrier((recv, near))

    order_grid = order_row.reshape(groups, slots)
    chunk_ids = (where - jnp.arange(SPAN, dtype=jnp.int32))[:, None, None]
    slot_map = jnp.sum(
        jnp.where(order_grid[None] // slots == chunk_ids, order_grid[None] % slots, 0), axis=2
    )
    ends = jnp.cumsum(doc_stretches[0])
    chunk_units = tokens // PAD
    unit_ids = where * chunk_units + jnp.arange(chunk_units, dtype=jnp.int32)
    doc_start = jnp.max(jnp.where(ends[None, :] <= unit_ids[:, None], ends[None, :], 0), axis=1)
    starts = doc_start - (where - (SPAN - 1)) * chunk_units

    at = KV_AT + lax.axis_index("core") * 2 * BLK
    shared_kv = lax.ppermute(lax.dynamic_slice_in_dim(recv, at, 2 * BLK, 1), "core", swap)
    sorted_rows = jax.ShapeDtypeStruct((slots * QROWS, HD), low)
    turned_rows = jax.ShapeDtypeStruct((HD, slots * QROWS), low)
    slab = (groups, 2 * BLK, HD)
    chunk_scratch = tuple(
        pltpu.VMEM((tokens, HD), dtype) for dtype in (low, low, jnp.float32, jnp.float32)
    )
    *shared_work, own_slab = prefetched(
        own_attend_kernel,
        2,
        (
            sorted_rows,
            sorted_rows,
            turned_rows,
            turned_rows,
            jax.ShapeDtypeStruct((slots, AUX_ROWS, HD), jnp.float32),
            jax.ShapeDtypeStruct(slab, jnp.float32),
        ),
        scratch=chunk_scratch,
    )(slot_map, starts, recv)
    before_slab = prefetched(
        functools.partial(earlier_attend_kernel, 1),
        2,
        jax.ShapeDtypeStruct(slab, low),
        scratch=chunk_scratch,
    )(slot_map, starts, shared_kv, *shared_work)
    shared_slab = lax.ppermute(before_slab, "core", swap)
    far_slab = prefetched(
        functools.partial(earlier_attend_kernel, 2),
        2,
        jax.ShapeDtypeStruct(slab, jnp.float32),
        scratch=chunk_scratch,
    )(slot_map, starts, recv[:, KV_AT + 2 * BLK : AUX_AT], *shared_work)
    partial_grads = prefetched(
        merge_kernel, 1, jax.ShapeDtypeStruct((groups, len(SENT), 2 * BLK, HD), low)
    )(core.reshape(1), own_slab, far_slab, shared_slab)
    partial_grads, near = lax.optimization_barrier((partial_grads, near))
    own_up, own_down, other_up, other_down = near
    own_list = [own_input, own_up, own_down, lax.ppermute(own_up, "tensor", up)]
    other_list = [other_input, other_up, other_down, lax.ppermute(other_down, "tensor", down)]
    returned = lax.all_to_all(partial_grads, context, split_axis=0, concat_axis=0, tiled=True)
    targets = lax.dynamic_slice_in_dim(order_row, where * slots, slots, 0) // slots
    own_kv = prefetched(collect_kernel, 1, jax.ShapeDtypeStruct((tokens, 2 * HD), low))(
        targets, returned
    )
    other_kv = lax.ppermute(own_kv, "core", swap)

    input_scratch = (
        pltpu.VMEM((widths - 1, half, tokens), low),
        pltpu.SemaphoreType.DMA((widths - 1,)),
    )
    first_product = prefetched(
        first_product_kernel,
        0,
        jax.ShapeDtypeStruct((len(own_list), half, 2 * HD), jnp.float32),
        scratch=input_scratch,
        in_place=widths - 1,
    )(*own_list, own_kv)
    spread = prefetched(
        product_kernel,
        1,
        jax.ShapeDtypeStruct((replicas, lines, 2, HB // replicas, 2 * HD), low),
        scratch=input_scratch,
        in_place=widths - 1,
    )(
        jnp.stack([core, lax.axis_index("tensor")]),
        *other_list,
        first_product,
        other_kv,
        hadamard_signs(HB),
        recv[:, AUX_AT:ROWS],
    )
    spread = spread.reshape(replicas * lines, 2, HB // replicas, 2 * HD)
    shares = lax.all_to_all(spread, ("dp", "y"), split_axis=0, concat_axis=0, tiled=True)
    return jnp.sum(shares.astype(jnp.float32), axis=0)


def solution(mesh):
    replicas, groups, widths = mesh.devices.shape
    split = Mesh(
        mesh.devices.reshape(replicas, groups // CORES, CORES, widths),
        ("dp", "y", "core", "tensor"),
    )
    context = ("y", "core")
    return jax.shard_map(
        per_device,
        mesh=split,
        in_specs=(
            P("dp", context, "tensor"),
            P("dp", "tensor", context, None),
            P("dp", "tensor", context, None),
            P("dp", "tensor", context, None),
            P("dp", "tensor", context, None),
            P("dp", "tensor", context),
            P("dp", "tensor", context),
            P("dp", None),
            P("dp", None),
            P(context, None),
            P("dp", context),
        ),
        out_specs=P(context, "dp", "tensor"),
        check_vma=False,
    )
```

```python
import functools

import jax
import jax.numpy as jnp
from jax import lax
from jax.experimental import pallas as pl
from jax.experimental.pallas import tpu as pltpu
from jax.sharding import Mesh
from jax.sharding import PartitionSpec as P

HD = 128
GROUP = 4
BLK = 32
PAD = 128
HB = 128
CORES = 2
SPAN = 3
SENT = (0, 2)
LOG2E = 1.4426950408889634

QROWS = GROUP * BLK
KV_AT = 2 * QROWS
AUX_AT = KV_AT + len(SENT) * 2 * BLK
AUX_ROWS = 8
ROWS = AUX_AT + AUX_ROWS
UNIT_BLKS = PAD // BLK
HOPS = (0, 1, 3, 2)


def hadamard_signs(table_size):
    index_row = jnp.arange(table_size, dtype=jnp.int32)
    common = jnp.bitwise_and(index_row[:, None], index_row[None, :])
    parity = jnp.zeros((table_size, table_size), jnp.int32)
    for bit_pos in range(table_size.bit_length() - 1):
        parity = parity + jnp.bitwise_and(jnp.right_shift(common, bit_pos), 1)
    return (1 - 2 * jnp.bitwise_and(parity, 1)).astype(jnp.bfloat16)


def pack_kernel(where_ref, *refs):
    (query_ref, grad_ref, key_ref, value_ref, lse_ref, dots_ref, sign_ref), refs = refs[:7], refs[7:]
    order_ref, exponent_ref, out_ref = refs[:3]
    query_scr, grad_scr, key_scr, value_scr, lse_scr, dots_scr, sign_scr = refs[3:10]
    order_scr, exponent_scr, held_scr, aux_scr, packed_scr, in_sem, out_sem = refs[10:]
    sources = (order_ref, exponent_ref, lse_ref, dots_ref, sign_ref)
    sources += (key_ref, value_ref, query_ref, grad_ref)
    places = (order_scr, exponent_scr, lse_scr, dots_scr, sign_scr)
    places += (key_scr, value_scr, query_scr, grad_scr)
    loads = [
        pltpu.make_async_copy(source, place, in_sem.at[i])
        for i, (source, place) in enumerate(zip(sources, places))
    ]
    for load in loads:
        load.start()
    groups = out_ref.shape[0]
    slots = key_ref.shape[2] // BLK
    for load in loads[:5]:
        load.wait()
    first = where_ref[0] * slots
    for slot in range(slots):
        held_scr[order_scr[0, first + slot] // slots] = slot

    fixed = [sign_scr[...].astype(jnp.float32)]
    for blk in range(sign_ref.shape[0]):
        power = jnp.full((1, HD), jnp.left_shift(jnp.int32(1), exponent_scr[0, blk]), jnp.int32)
        fixed.append(1.0 / power.astype(jnp.float32))
    fixed.append(jnp.zeros((AUX_ROWS - 6, HD), jnp.float32))
    head_of = lax.broadcasted_iota(jnp.int32, (1, HD), 1) // BLK
    stats = (lse_scr[0].astype(jnp.float32), dots_scr[0].astype(jnp.float32))

    def by_head(array, slot):
        part = slot * BLK // HD * HD
        inner = slot % (HD // BLK)
        row = jnp.zeros((1, HD), jnp.float32)
        for head in range(GROUP):
            line = array[head : head + 1, part : part + HD]
            turn = (head - inner) * BLK % HD
            line = pltpu.roll(line, turn, 1) if turn else line
            row = jnp.where(head_of == head, line, row)
        return row

    for slot in range(slots):
        aux = jnp.concatenate([by_head(array, slot) for array in stats] + fixed, axis=0)
        aux_scr[slot] = aux.astype(aux_scr.dtype)
    for load in loads[5:]:
        load.wait()

    stores = []
    for dest in range(groups):
        slot = held_scr[dest]
        rows = pl.ds(pl.multiple_of(slot * BLK, BLK), BLK)
        for head in range(GROUP):
            packed_scr[dest, head * BLK : (head + 1) * BLK, :] = query_scr[0, head, rows, :]
            at = QROWS + head * BLK
            packed_scr[dest, at : at + BLK, :] = grad_scr[0, head, rows, :]
        for place, span in enumerate(SENT):
            at = KV_AT + place * 2 * BLK
            if dest >= span:
                rows = pl.ds(pl.multiple_of(held_scr[dest - span] * BLK, BLK), BLK)
                packed_scr[dest, at : at + BLK, :] = key_scr[0, 0, rows, :]
                packed_scr[dest, at + BLK : at + 2 * BLK, :] = value_scr[0, 0, rows, :]
            else:
                packed_scr[dest, at : at + 2 * BLK, :] = jnp.zeros((2 * BLK, HD), out_ref.dtype)
        packed_scr[dest, AUX_AT:ROWS, :] = aux_scr[slot]
        stores.append(pltpu.make_async_copy(packed_scr.at[dest], out_ref.at[dest], out_sem.at[dest]))
        stores[-1].start()
    for store in stores:
        store.wait()


def block_grads(key_blk, value_blk, query_refs, cols, lse, dots, inside, causal=None):
    query_ref, grad_ref, query_turned, grad_turned = query_refs
    scores = jnp.dot(key_blk, query_turned[:, cols], preferred_element_type=jnp.float32)
    dprobs = jnp.dot(value_blk, grad_turned[:, cols], preferred_element_type=jnp.float32)
    probs = jnp.exp2(scores * (HD ** (-0.5) * LOG2E) - lse)
    if causal is not None:
        before = probs.shape[0] - causal.shape[0]
        diagonal = jnp.where(causal, probs[before:], 0.0)
        probs = jnp.concatenate([probs[:before], diagonal], axis=0) if before else diagonal
    dscores = (probs * (dprobs - dots)).astype(jnp.bfloat16)
    value_part = jnp.dot(
        probs.astype(jnp.bfloat16), grad_ref[cols, :], preferred_element_type=jnp.float32
    )
    key_part = jnp.dot(dscores, query_ref[cols, :], preferred_element_type=jnp.float32)
    return jnp.where(inside, key_part, 0.0), jnp.where(inside, value_part, 0.0)


def unit_stats(stat_ref, unit):
    blocks = range(unit * UNIT_BLKS, (unit + 1) * UNIT_BLKS)
    lse = jnp.concatenate([stat_ref[b, 0:1, :] for b in blocks], axis=1) * LOG2E
    dots = jnp.concatenate([stat_ref[b, 1:2, :] for b in blocks], axis=1)
    return lse, dots


def rows_of(slot_ref, span, src):
    return pl.ds(pl.multiple_of(slot_ref[span, src] * BLK, BLK), BLK)


def store_slab(slot_ref, span, dkey_scr, dvalue_scr, out_ref):
    for src in range(out_ref.shape[0]):
        rows = rows_of(slot_ref, span, src)
        dkey = dkey_scr[rows, :] * HD ** (-0.5)
        out_ref[src, 0:BLK, :] = dkey.astype(out_ref.dtype)
        out_ref[src, BLK : 2 * BLK, :] = dvalue_scr[rows, :].astype(out_ref.dtype)


def own_attend_kernel(
    slot_ref, start_ref, recv_ref,
    query_ref, grad_ref, query_turned, grad_turned, stat_ref, out_ref,
    key_scr, value_scr, dkey_scr, dvalue_scr,
):
    units = key_scr.shape[0] // PAD
    width = UNIT_BLKS * QROWS
    for src in range(recv_ref.shape[0]):
        slot = slot_ref[0, src]
        at = pl.multiple_of(slot * QROWS, QROWS)
        query_blk = recv_ref[src, 0:QROWS, :]
        grad_blk = recv_ref[src, QROWS : 2 * QROWS, :]
        query_ref[pl.ds(at, QROWS), :] = query_blk
        grad_ref[pl.ds(at, QROWS), :] = grad_blk
        query_turned[:, pl.ds(at, QROWS)] = query_blk.T
        grad_turned[:, pl.ds(at, QROWS)] = grad_blk.T
        stat_ref[slot] = recv_ref[src, AUX_AT:ROWS, :].astype(jnp.float32)
        rows = rows_of(slot_ref, 0, src)
        key_scr[rows, :] = recv_ref[src, KV_AT : KV_AT + BLK, :]
        value_scr[rows, :] = recv_ref[src, KV_AT + BLK : KV_AT + 2 * BLK, :]

    queries = (query_ref, grad_ref, query_turned, grad_turned)
    key_at = lax.broadcasted_iota(jnp.int32, (PAD, width), 0)
    column = lax.broadcasted_iota(jnp.int32, (PAD, width), 1)
    causal = key_at <= (column // QROWS) * BLK + column % BLK
    for unit in reversed(range(units)):
        rows = slice(0, (unit + 1) * PAD)
        cols = slice(unit * width, (unit + 1) * width)
        lse, dots = unit_stats(stat_ref, unit)
        first = (start_ref[unit] - (SPAN - 1) * units) * PAD
        inside = lax.broadcasted_iota(jnp.int32, (rows.stop, HD), 0) >= first
        key_part, value_part = block_grads(
            key_scr[rows, :], value_scr[rows, :], queries, cols, lse, dots, inside, causal
        )
        if unit == units - 1:
            dkey_scr[...] = key_part
            dvalue_scr[...] = value_part
        else:
            dkey_scr[rows, :] += key_part
            dvalue_scr[rows, :] += value_part
    store_slab(slot_ref, 0, dkey_scr, dvalue_scr, out_ref)


def earlier_attend_kernel(span, slot_ref, start_ref, kv_ref, *refs):
    queries, refs = refs[:4], refs[4:]
    stat_ref, out_ref, key_scr, value_scr, dkey_scr, dvalue_scr = refs
    units = key_scr.shape[0] // PAD
    width = UNIT_BLKS * QROWS
    pair = 2 * PAD
    for src in range(kv_ref.shape[0]):
        rows = rows_of(slot_ref, span, src)
        key_scr[rows, :] = kv_ref[src, 0:BLK, :]
        value_scr[rows, :] = kv_ref[src, BLK : 2 * BLK, :]
    dkey_scr[...] = jnp.zeros_like(dkey_scr)
    dvalue_scr[...] = jnp.zeros_like(dvalue_scr)
    key_at = lax.broadcasted_iota(jnp.int32, (pair, HD), 0)
    for unit in range(units):
        cols = slice(unit * width, (unit + 1) * width)
        lse, dots = unit_stats(stat_ref, unit)
        first = jnp.clip(start_ref[unit] - (SPAN - 1 - span) * units, 0, units)

        @pl.loop(0, (units - first + 1) // 2)
        def _(step):
            base = units - 2 - 2 * step
            rows = pl.ds(pl.multiple_of(base * PAD, pair), pair)
            key_part, value_part = block_grads(
                key_scr[rows, :],
                value_scr[rows, :],
                queries,
                cols,
                lse,
                dots,
                key_at >= (first - base) * PAD,
            )
            dkey_scr[rows, :] += key_part
            dvalue_scr[rows, :] += value_part

    store_slab(slot_ref, span, dkey_scr, dvalue_scr, out_ref)


def merge_kernel(core_ref, own_ref, far_ref, shared_ref, out_ref):
    core = core_ref[0]
    for src in range(out_ref.shape[0]):
        shared = shared_ref[src].astype(jnp.float32)
        own = own_ref[src] + jnp.where(core == 0, shared, 0.0)
        far = far_ref[src] + jnp.where(core == 0, 0.0, shared)
        out_ref[src, 0] = own.astype(out_ref.dtype)
        out_ref[src, 1] = far.astype(out_ref.dtype)


def collect_kernel(target_ref, recv_ref, out_ref):
    groups = recv_ref.shape[0]
    for slot in range(out_ref.shape[0] // BLK):
        owner = target_ref[slot]
        total = recv_ref[owner, 0].astype(jnp.float32)
        later = owner + SENT[1]
        extra = recv_ref[jnp.minimum(later, groups - 1), 1].astype(jnp.float32)
        total = total + jnp.where(later < groups, extra, 0.0)
        rows = slice(slot * BLK, (slot + 1) * BLK)
        total = total.astype(out_ref.dtype)
        out_ref[rows, 0:HD] = total[0:BLK]
        out_ref[rows, HD : 2 * HD] = total[BLK : 2 * BLK]


def turn_kernel(core_ref, input_ref, own_ref, other_ref):
    span = 2 * HB
    core = core_ref[0]
    for part in range(own_ref.shape[0] // span):
        rows = slice(part * span, (part + 1) * span)
        at = pl.multiple_of((CORES * part + core) * span, span)
        own_ref[rows, :] = input_ref[:, pl.ds(at, span)].T
        at = pl.multiple_of((CORES * part + 1 - core) * span, span)
        other_ref[rows, :] = input_ref[:, pl.ds(at, span)].T


def load_all(sources, places, sems):
    loads = [
        pltpu.make_async_copy(source, places.at[i], sems.at[i]) for i, source in enumerate(sources)
    ]
    for load in loads:
        load.start()
    return loads


def first_product_kernel(*refs):
    far_ref, kv_ref, out_ref, input_scr, sems = refs[-5:]
    loads = load_all(refs[:-5], input_scr, sems)
    last = len(loads)
    out_ref[last] = jnp.dot(far_ref[...], kv_ref[...], preferred_element_type=jnp.float32)
    for step, load in enumerate(loads):
        load.wait()
        out_ref[step] = jnp.dot(input_scr[step], kv_ref[...], preferred_element_type=jnp.float32)


def product_kernel(where_ref, *refs):
    far_ref, first_ref, kv_ref, had_ref, aux_ref, out_ref, input_scr, sems = refs[-8:]
    loads = load_all(refs[:-8], input_scr, sems)
    core, width = where_ref[0], where_ref[1]
    replicas = out_ref.shape[0]
    span = 2 * HB
    parts = far_ref.shape[0] // span
    had = jnp.concatenate([had_ref[...].astype(jnp.float32)] * 2, axis=1)
    widths = len(HOPS)
    for step in (widths - 1, *range(widths - 1)):
        source = (width + widths - HOPS[step]) % widths
        if step < len(loads):
            loads[step].wait()
            inputs = input_scr[step]
        else:
            inputs = far_ref[...]
        grad = jnp.dot(inputs, kv_ref[...], preferred_element_type=jnp.float32)
        grad = grad + first_ref[step]
        for part in range(parts):
            line = source * parts + part
            aux = aux_ref[CORES * line + core].astype(jnp.float32)
            for blk in range(2):
                at = part * span + blk * HB
                rows = grad[at : at + HB]
                sign = aux[2 + blk : 3 + blk, :]
                table = (had * jnp.concatenate([sign, sign], axis=1)).astype(jnp.bfloat16)
                high = rows.astype(jnp.bfloat16)
                low = (rows - high.astype(jnp.float32)).astype(jnp.bfloat16)
                both = jnp.concatenate([high, low], axis=0)
                rotated = jnp.dot(table, both, preferred_element_type=jnp.float32)
                factor = aux[4 + blk : 5 + blk, :] * (HB ** (-0.5))
                rotated *= jnp.concatenate([factor] * (rows.shape[1] // HB), axis=1)
                out_ref[:, line, blk] = rotated.astype(out_ref.dtype).reshape(
                    replicas, HB // replicas, rows.shape[1]
                )


def prefetched(kernel, scalars, out_shape, scratch=(), in_place=0, out_space=pltpu.VMEM):
    vmem = pl.BlockSpec(memory_space=pltpu.VMEM)
    hbm = pl.BlockSpec(memory_space=pltpu.HBM)
    out_spec = pl.BlockSpec(memory_space=out_space)

    def call(*operands):
        held = scalars + in_place
        kept = [
            pltpu.with_memory_space_constraint(array, pltpu.HBM)
            for array in operands[scalars:held]
        ]
        return pl.pallas_call(
            kernel,
            out_shape=out_shape,
            grid_spec=pltpu.PrefetchScalarGridSpec(
                num_scalar_prefetch=scalars,
                in_specs=[hbm] * in_place + [vmem] * (len(operands) - held),
                out_specs=jax.tree.map(lambda _: out_spec, out_shape),
                scratch_shapes=list(scratch),
            ),
            compiler_params=pltpu.CompilerParams(vmem_limit_bytes=16 << 20),
        )(*operands[:scalars], *kept, *operands[held:])

    return call


def around(count, step):
    return [(i, (i + step) % count) for i in range(count)]


def per_device(
    layer_input,
    queries,
    key_states,
    value_states,
    out_grad,
    log_sums,
    grad_dots,
    doc_stretches,
    stretch_order,
    sign_vector,
    exponents,
):
    context = ("y", "core")
    low = jnp.bfloat16
    tokens = queries.shape[2]
    slots = tokens // BLK
    groups = lax.axis_size(context)
    lines = lax.axis_size("y")
    replicas = lax.axis_size("dp")
    order_row = stretch_order[0]
    where = lax.axis_index(context)
    core = lax.axis_index("core")

    raw = (queries, out_grad, key_states, value_states, log_sums, grad_dots, sign_vector)
    packed = prefetched(
        pack_kernel,
        1,
        pltpu.HBM((groups, ROWS, HD), low),
        scratch=(
            *(pltpu.VMEM(array.shape, array.dtype) for array in raw),
            pltpu.SMEM(stretch_order.shape, jnp.int32),
            pltpu.SMEM(exponents.shape, jnp.int32),
            pltpu.SMEM((groups,), jnp.int32),
            pltpu.VMEM((slots, AUX_ROWS, HD), low),
            pltpu.VMEM((groups, ROWS, HD), low),
            pltpu.SemaphoreType.DMA((9,)),
            pltpu.SemaphoreType.DMA((groups,)),
        ),
        in_place=len(raw) + 2,
        out_space=pltpu.HBM,
    )(where.reshape(1), *raw, stretch_order, exponents)
    packed, layer_input = lax.optimization_barrier((packed, layer_input))
    recv = lax.all_to_all(packed, context, split_axis=0, concat_axis=0, tiled=True)

    half = layer_input.shape[2] // CORES
    turned = jax.ShapeDtypeStruct((half, tokens), low)
    own_input, other_input = prefetched(turn_kernel, 1, (turned, turned))(
        core.reshape(1), layer_input[0]
    )
    swap = [(0, 1), (1, 0)]
    other_input = lax.ppermute(other_input, "core", swap)
    widths = lax.axis_size("tensor")
    up, down = around(widths, 1), around(widths, -1)
    near = [
        lax.ppermute(array, "tensor", way)
        for array in (own_input, other_input)
        for way in (up, down)
    ]
    recv, near = lax.optimization_barrier((recv, near))

    order_grid = order_row.reshape(groups, slots)
    chunk_ids = (where - jnp.arange(SPAN, dtype=jnp.int32))[:, None, None]
    slot_map = jnp.sum(
        jnp.where(order_grid[None] // slots == chunk_ids, order_grid[None] % slots, 0), axis=2
    )
    ends = jnp.cumsum(doc_stretches[0])
    chunk_units = tokens // PAD
    unit_ids = where * chunk_units + jnp.arange(chunk_units, dtype=jnp.int32)
    doc_start = jnp.max(jnp.where(ends[None, :] <= unit_ids[:, None], ends[None, :], 0), axis=1)
    starts = doc_start - (where - (SPAN - 1)) * chunk_units

    at = KV_AT + lax.axis_index("core") * 2 * BLK
    shared_kv = lax.ppermute(lax.dynamic_slice_in_dim(recv, at, 2 * BLK, 1), "core", swap)
    sorted_rows = jax.ShapeDtypeStruct((slots * QROWS, HD), low)
    turned_rows = jax.ShapeDtypeStruct((HD, slots * QROWS), low)
    slab = (groups, 2 * BLK, HD)
    chunk_scratch = tuple(
        pltpu.VMEM((tokens, HD), dtype) for dtype in (low, low, jnp.float32, jnp.float32)
    )
    *shared_work, own_slab = prefetched(
        own_attend_kernel,
        2,
        (
            sorted_rows,
            sorted_rows,
            turned_rows,
            turned_rows,
            jax.ShapeDtypeStruct((slots, AUX_ROWS, HD), jnp.float32),
            jax.ShapeDtypeStruct(slab, jnp.float32),
        ),
        scratch=chunk_scratch,
    )(slot_map, starts, recv)
    before_slab = prefetched(
        functools.partial(earlier_attend_kernel, 1),
        2,
        jax.ShapeDtypeStruct(slab, low),
        scratch=chunk_scratch,
    )(slot_map, starts, shared_kv, *shared_work)
    shared_slab = lax.ppermute(before_slab, "core", swap)
    far_slab = prefetched(
        functools.partial(earlier_attend_kernel, 2),
        2,
        jax.ShapeDtypeStruct(slab, jnp.float32),
        scratch=chunk_scratch,
    )(slot_map, starts, recv[:, KV_AT + 2 * BLK : AUX_AT], *shared_work)
    partial_grads = prefetched(
        merge_kernel, 1, jax.ShapeDtypeStruct((groups, len(SENT), 2 * BLK, HD), low)
    )(core.reshape(1), own_slab, far_slab, shared_slab)
    partial_grads, near = lax.optimization_barrier((partial_grads, near))
    own_up, own_down, other_up, other_down = near
    own_list = [own_input, own_up, own_down, lax.ppermute(own_up, "tensor", up)]
    other_list = [other_input, other_up, other_down, lax.ppermute(other_down, "tensor", down)]
    returned = lax.all_to_all(partial_grads, context, split_axis=0, concat_axis=0, tiled=True)
    targets = lax.dynamic_slice_in_dim(order_row, where * slots, slots, 0) // slots
    own_kv = prefetched(collect_kernel, 1, jax.ShapeDtypeStruct((tokens, 2 * HD), low))(
        targets, returned
    )
    other_kv = lax.ppermute(own_kv, "core", swap)

    input_scratch = (
        pltpu.VMEM((widths - 1, half, tokens), low),
        pltpu.SemaphoreType.DMA((widths - 1,)),
    )
    first_product = prefetched(
        first_product_kernel,
        0,
        jax.ShapeDtypeStruct((len(own_list), half, 2 * HD), jnp.float32),
        scratch=input_scratch,
        in_place=widths - 1,
    )(*own_list, own_kv)
    spread = prefetched(
        product_kernel,
        1,
        jax.ShapeDtypeStruct((replicas, lines, 2, HB // replicas, 2 * HD), low),
        scratch=input_scratch,
        in_place=widths - 1,
    )(
        jnp.stack([core, lax.axis_index("tensor")]),
        *other_list,
        first_product,
        other_kv,
        hadamard_signs(HB),
        recv[:, AUX_AT:ROWS],
    )
    spread = spread.reshape(replicas * lines, 2, HB // replicas, 2 * HD)
    shares = lax.all_to_all(spread, ("dp", "y"), split_axis=0, concat_axis=0, tiled=True)
    return jnp.sum(shares.astype(jnp.float32), axis=0)


def solution(mesh):
    replicas, groups, widths = mesh.devices.shape
    split = Mesh(
        mesh.devices.reshape(replicas, groups // CORES, CORES, widths),
        ("dp", "y", "core", "tensor"),
    )
    context = ("y", "core")
    return jax.shard_map(
        per_device,
        mesh=split,
        in_specs=(
            P("dp", context, "tensor"),
            P("dp", "tensor", context, None),
            P("dp", "tensor", context, None),
            P("dp", "tensor", context, None),
            P("dp", "tensor", context, None),
            P("dp", "tensor", context),
            P("dp", "tensor", context),
            P("dp", None),
            P("dp", None),
            P(context, None),
            P("dp", context),
        ),
        out_specs=P(context, "dp", "tensor"),
        check_vma=False,
    )
```
